128 devices in a mesh: lat: 8 (over x_hi, z), lon: 16 (over y, x_lo, core).
Axes of the slice: x: 4 (x_hi: 2, x_lo: 2; x = x_hi * 2 + x_lo), y: 4, z: 4, core: 2. Of those that a mesh axis runs over, the one named last changes fastest.
Arguments:
- obs_rows: bfloat16 [131072, 512], P(('lat', 'lon')), may hold values from -6 to 6
- obs_dest: int32 [131072, 1], P(('lat', 'lon')), may hold values from 0 to 127; in each aligned block of 1024 rows (0 to 1023, 1024 to 2047, ...) at most 16 rows name the same one
- obs_token: int32 [131072], P(('lat', 'lon')), may hold values from 0 to 511
- obs_count: int32 [128], P(('lat', 'lon')), may hold values from 640 to 1024, as said below
- background: bfloat16 [128, 512, 512], P('lat', 'lon'), may hold values from -6 to 6
- w_obs_in: bfloat16 [512, 2048], replicated, may hold values from -0.25 to 0.25
- w_obs_out: bfloat16 [2048, 512], replicated, may hold values from -0.125 to 0.125
- w_qkv: bfloat16 [2, 512, 1536], replicated, may hold values from -2 to 2
- w_proj: bfloat16 [2, 512, 512], replicated, may hold values from -0.25 to 0.25
- w_up: bfloat16 [2, 512, 2048], replicated, may hold values from -0.25 to 0.25
- w_down: bfloat16 [2, 2048, 512], replicated, may hold values from -0.125 to 0.125
- norm_gain: float32 [2, 2, 512], replicated, may hold values from 0.1 to 1.9
Outputs:
- tokens_out: bfloat16 [128, 512, 512], P('lat', 'lon')
The draws below stay inside these ranges and needn't reach their ends.
Inputs may be any that keep to these rules, and one draw needn't show every extreme that they name: `obs_dest`: of the 1024 rows of one swath owner, live or not, at most 16 name one tile owner, and some swath owner has exactly 16 rows naming one tile owner. The live rows of a swath owner are its first obs_count rows; some swath owner has all 1024 rows live and another has exactly the least count.
All inputs are finite; a program needn't handle non-finite values.
Results may differ from the reference program's by a relative error of at most 0.018.
Values may be sent and summed in bfloat16 or wider, within the bound.
No kernel may reach another device: no remote copies, remote signals or barrier semaphores. Data moves between devices by JAX's collectives and lax.ppermute only.
A program may use at most 64 MiB of HBM per device.

```python
import math
import jax
import jax.numpy as jnp
import numpy as np
from jax import lax

D = 512
FF = 2048
HEADS = 8
HEAD_DIM = 64
WIN = 16
CLAT = 16
CLON = 32
OBS_DEV = 1024
OWNERS = 128
CAP = 16
NLAT = 128
NLON = 512
N_LON = 16


def draw_obs_count(key, part):
    first_key, second_key, third_key = jax.random.split(key, 3)
    counts = jax.random.randint(first_key, (OWNERS,), 5 * OBS_DEV // 8, OBS_DEV + 1, dtype=jnp.int32)
    full_owner = jax.random.randint(second_key, (), 0, OWNERS, dtype=jnp.int32)
    offset = jax.random.randint(third_key, (), 1, OWNERS, dtype=jnp.int32)
    least_owner = (full_owner + offset) % OWNERS
    owner_ids = jnp.arange(OWNERS, dtype=jnp.int32)
    counts = jnp.where(owner_ids == least_owner, 5 * OBS_DEV // 8, counts)
    return jnp.where(owner_ids == full_owner, OBS_DEV, counts).astype(jnp.int32)


def draw_w_qkv(key, part):
    first_key = jax.random.fold_in(key, 0)
    base = jax.random.normal(first_key, (2, D, 3 * D), jnp.float32) * (1.0 / math.sqrt(D))
    return jnp.clip(base, -2.0, 2.0).astype(jnp.bfloat16)


def touch_ends(entries, rng, low, largest):
    shape = entries.shape
    index_at = [jax.random.randint(jax.random.fold_in(rng, axis), (), 0, shape[axis]) for axis in range(len(shape))]
    entries = entries.at[tuple(index_at)].set(low)
    longest = shape.index(max(shape))
    index_at[longest] = (index_at[longest] + 1) % shape[longest]
    return entries.at[tuple(index_at)].set(largest)


def block_scale(own_key, extent, pieces, smallest, top_value):
    def one(position, blocks):
        draws = jax.random.uniform(jax.random.fold_in(jax.random.fold_in(own_key, 6), position), (blocks,), jnp.float32, smallest / len(pieces), top_value / len(pieces))
        return jnp.repeat(jnp.exp(draws), extent[position] // blocks).reshape((-1,) + (1,) * (len(extent) - position - 1))

    level = one(*pieces[0])
    for cut in pieces[1:]:
        level = level * one(*cut)
    return level


def deal_out(stream_key, own, number, rows, count, top, bound, lean):
    order = jax.random.permutation(stream_key, count)
    crowded, usual = shares(count, rows * top, bound, lean, True), shares(count, rows * top, bound, lean, False)
    places = jnp.arange(count)

    def named(lengths, turn):
        used = int((lengths > 0).sum())
        fixed = max(1, used // 4)
        shifted = fixed + (places - fixed + turn * (used - fixed)) % max(1, count - fixed)
        return jnp.zeros((count,), jnp.int32).at[order[jnp.where(places < fixed, places, shifted)]].set(jnp.asarray(lengths, jnp.int32))

    lengths = jnp.where(number % 4 == 0, named(crowded, number // 4), named(usual, number - number // 4 - 1))
    mixed = jax.random.permutation(jax.random.fold_in(own, 3), count)
    giver, taker = mixed[0:count // 2 * 2:2], mixed[1:count // 2 * 2:2]
    slack = jnp.minimum(lengths[giver] - 1, bound - lengths[taker]) // 2
    slack = jnp.where((giver == order[0]) | (taker == order[0]) | (lengths[taker] == 0), 0, jnp.maximum(slack, 0))
    shifted = jax.random.randint(jax.random.fold_in(own, 4), (count // 2,), 0, 1 << 20) % (slack + 1)
    lengths = lengths.at[giver].add(-shifted).at[taker].add(shifted)
    items = jnp.searchsorted(jnp.cumsum(lengths), jnp.arange(rows * top), side="right").astype(jnp.int32)
    grid = items.reshape(top, rows).T
    grid = grid[jax.random.permutation(jax.random.fold_in(own, 1), rows)]
    turn = jax.random.randint(jax.random.fold_in(own, 2), (rows, 1), 0, top)
    return jnp.take_along_axis(grid, (jnp.arange(top)[None, :] + turn) % top, axis=1)


def shares(count, total, reach, skew, full):
    portions = [(1 << 20) // math.isqrt(standing ** skew) + 1 for standing in range(1, count + 1)]
    largest = reach if full else min(reach, max(-(-total // count), total * portions[0] // sum(portions)))
    least = 1 if total - largest >= count - 1 else 0
    given, surplus = [largest] + [least] * (count - 1), total - largest - least * (count - 1)
    while surplus > 0:
        candidates = [i for i in range(1, count) if given[i] < largest] or [i for i in range(1, count) if given[i] < reach]
        pool, remaining = sum([portions[i] for i in candidates]), surplus
        for i in candidates:
            addition = min(reach - given[i], max(1, remaining * portions[i] // pool), surplus)
            given[i] = given[i] + addition
            surplus = surplus - addition
    return np.array(given)


def bell_draw(rng, shape, scale, reach, cuts=(), held_as=jnp.bfloat16):
    array = jax.random.normal(rng, shape, jnp.float32) * scale
    if len(cuts) > 0:
        array = block_scale(rng, shape, cuts, -0.22, 0.18) * array
    return jnp.clip(array, min=-reach, max=reach).astype(held_as)


def setup_inputs(seed: int = 0) -> dict:
    seeds = jax.random.split(jax.random.key(seed), 13)
    obs_rows = bell_draw(seeds[0], (OWNERS * OBS_DEV, D), 1.0, 6.0, ((0, 128),))
    obs_dest_keys = jax.random.split(jax.random.fold_in(seeds[1], 1), (OWNERS * OBS_DEV) // OBS_DEV)
    obs_dest_turns = jax.random.permutation(jax.random.fold_in(seeds[1], 3), (OWNERS * OBS_DEV) // OBS_DEV)
    obs_dest = jax.vmap(lambda own, number: deal_out(jax.random.fold_in(seeds[1], 2), own, number, OBS_DEV, OWNERS, 1, CAP, 2))(obs_dest_keys, obs_dest_turns).reshape((OWNERS * OBS_DEV, 1))
    obs_token = touch_ends(jax.random.randint(seeds[2], (OWNERS * OBS_DEV,), 0, CLAT * CLON), jax.random.fold_in(seeds[2], 1), 0, (CLAT * CLON) - 1).astype(jnp.int32)
    obs_count = draw_obs_count(jax.random.fold_in(seeds[12], 71), 0)
    background = bell_draw(seeds[4], (NLAT, NLON, D), 1.0, 6.0, ((0, 8), (1, 16)))
    w_obs_in = bell_draw(seeds[5], (D, FF), D ** -0.5, 0.25)
    w_obs_out = bell_draw(seeds[6], (FF, D), FF ** -0.5, 0.125)
    w_qkv = draw_w_qkv(jax.random.fold_in(seeds[12], 71), 0)
    w_proj = bell_draw(seeds[8], (2, D, D), D ** -0.5, 0.25)
    w_up = bell_draw(seeds[9], (2, D, FF), D ** -0.5, 0.25)
    w_down = bell_draw(seeds[10], (2, FF, D), FF ** -0.5, 0.125)
    norm_gain = jnp.clip(1.0 + 0.18 * jax.random.normal(seeds[11], (2, 2, D), jnp.float32), 0.1, 1.9)
    return {"obs_rows": obs_rows, "obs_dest": obs_dest, "obs_token": obs_token, "obs_count": obs_count, "background": background, "w_obs_in": w_obs_in, "w_obs_out": w_obs_out, "w_qkv": w_qkv, "w_proj": w_proj, "w_up": w_up, "w_down": w_down, "norm_gain": norm_gain}


epsilon = 1e-05

def norm_rows(inputs, gain_row):
    inputs = inputs.astype(jnp.float32)
    row_mean = lax.optimization_barrier(jnp.mean(inputs, -1, keepdims=True))
    centred = inputs - row_mean
    row_var = lax.optimization_barrier(jnp.mean(centred * centred, -1, keepdims=True))
    return centred * lax.rsqrt(row_var + epsilon) * gain_row

def partition(grid_cells):
    row_count, col_count, width = grid_cells.shape
    blocks = grid_cells.reshape(row_count // WIN, WIN, col_count // WIN, WIN, width).transpose(0, 2, 1, 3, 4)
    return blocks.reshape(-1, WIN * WIN, width)

def unpartition(windows, row_count, col_count):
    width = windows.shape[-1]
    blocks = windows.reshape(row_count // WIN, col_count // WIN, WIN, WIN, width).transpose(0, 2, 1, 3, 4)
    return blocks.reshape(row_count, col_count, width)

def attend_windows(windows, regions, qkv_weight, proj_weight, gain_row):
    window_count = windows.shape[0]
    normed = norm_rows(windows, gain_row).astype(jnp.bfloat16)
    projected = jnp.dot(normed.reshape(-1, D), qkv_weight, preferred_element_type=jnp.float32)
    projected = projected.astype(jnp.bfloat16).reshape(window_count, WIN * WIN, 3, HEADS, HEAD_DIM)
    queries = projected[:, :, 0].astype(jnp.float32)
    key_rows = projected[:, :, 1].astype(jnp.float32)
    value_rows = projected[:, :, 2].astype(jnp.float32)
    scores = jnp.einsum('wqhd,wkhd->whqk', queries, key_rows) * (1.0 / math.sqrt(HEAD_DIM))
    same_region = regions[:, None, :, None] == regions[:, None, None, :]
    scores = jnp.where(same_region, scores, -1e+30)
    weights = jax.nn.softmax(scores, -1).astype(jnp.bfloat16)
    mixed_heads = jnp.einsum('whqk,wkhd->wqhd', weights.astype(jnp.float32), value_rows)
    mixed_heads = mixed_heads.astype(jnp.bfloat16).reshape(-1, D)
    attended = windows.astype(jnp.float32).reshape(-1, D) + jnp.dot(mixed_heads, proj_weight, preferred_element_type=jnp.float32)
    return attended.reshape(windows.shape)

def feed(attended, gain_row, up_weight, down_weight):
    flat_rows = attended.reshape(-1, D)
    normed = norm_rows(flat_rows, gain_row).astype(jnp.bfloat16)
    hidden = jax.nn.gelu(jnp.dot(normed, up_weight, preferred_element_type=jnp.float32), approximate=True).astype(jnp.bfloat16)
    result = flat_rows + jnp.dot(hidden, down_weight, preferred_element_type=jnp.float32)
    return result.astype(jnp.bfloat16).reshape(attended.shape)

def block_grid(grid_cells, region_grid, layer, w_qkv, w_proj, w_up, w_down, norm_gain):
    row_count, col_count = (grid_cells.shape[0], grid_cells.shape[1])
    windows = partition(grid_cells)
    regions = partition(region_grid[:, :, None])[:, :, 0]
    window_count = windows.shape[0]
    group_size = 8

    def apply_block(window_pair):
        group_windows, group_regions = window_pair
        attended = attend_windows(group_windows, group_regions, w_qkv[layer], w_proj[layer], norm_gain[layer, 0])
        return feed(attended, norm_gain[layer, 1], w_up[layer], w_down[layer])
    result = lax.map(apply_block, (windows.reshape(window_count // group_size, group_size, WIN * WIN, D), regions.reshape(window_count // group_size, group_size, WIN * WIN)))
    return unpartition(result.reshape(window_count, WIN * WIN, D), row_count, col_count)

def reference(obs_rows, obs_dest, obs_token, obs_count, background, w_obs_in, w_obs_out, w_qkv, w_proj, w_up, w_down, norm_gain):
    per_owner = obs_rows.reshape(OWNERS, OBS_DEV, D)

    def encode(row_block):
        hidden = jax.nn.gelu(jnp.dot(row_block, w_obs_in, preferred_element_type=jnp.float32), approximate=True).astype(jnp.bfloat16)
        return jnp.dot(hidden, w_obs_out, preferred_element_type=jnp.float32).astype(jnp.bfloat16)
    encoded = lax.map(encode, per_owner).reshape(-1, D)
    row_ids = jnp.arange(OWNERS * OBS_DEV, dtype=jnp.int32)
    live_rows = row_ids % OBS_DEV < obs_count[(row_ids // OBS_DEV).astype(jnp.int32)]
    destination = obs_dest[:, 0]
    cells_total = NLAT * NLON
    flat_cell = (destination // N_LON * CLAT + obs_token // CLON) * NLON + destination % N_LON * CLON + obs_token % CLON
    flat_cell = jnp.where(live_rows, flat_cell, cells_total).astype(jnp.int32)
    cell_sums = jax.ops.segment_sum(encoded.astype(jnp.float32), flat_cell, num_segments=cells_total + 1)[:cells_total]
    cell_tally = jax.ops.segment_sum(jnp.ones((OWNERS * OBS_DEV,), jnp.float32), flat_cell, num_segments=cells_total + 1)[:cells_total]
    grid_state = background.reshape(cells_total, D).astype(jnp.float32) + cell_sums / jnp.maximum(cell_tally, 1.0)[:, None]
    grid_state = grid_state.astype(jnp.bfloat16).reshape(NLAT, NLON, D)
    zero_region = jnp.zeros((NLAT, NLON), jnp.int32)
    grid_state = block_grid(grid_state, zero_region, 0, w_qkv, w_proj, w_up, w_down, norm_gain)
    shift_cells = WIN // 2
    rolled = jnp.roll(grid_state, (-shift_cells, -shift_cells), (0, 1))
    initial = (jnp.arange(NLAT, dtype=jnp.int32) + shift_cells) % NLAT
    region_grid = jnp.broadcast_to((initial < shift_cells).astype(jnp.int32)[:, None], (NLAT, NLON))
    rolled = block_grid(rolled, region_grid, 1, w_qkv, w_proj, w_up, w_down, norm_gain)
    return jnp.roll(rolled, (shift_cells, shift_cells), (0, 1))
```

```python
import functools

import jax
import jax.numpy as jnp
from jax import lax
from jax.experimental import pallas as pl
from jax.experimental.pallas import tpu as pltpu
from jax.sharding import PartitionSpec as P

D = 512
FF = 2048
HEADS = 8
WIN = 16
HALF = 8
CLAT = 16
CLON = 32
CELLS = CLAT * CLON
OBS_DEV = 1024
OWNERS = 128
CAP = 16
LANES = 128
SLAB = 4 * CAP + 8
BLK = 256
EPS = 1e-5
BF = jnp.bfloat16
F32 = jnp.float32
VMEM = pl.BlockSpec(memory_space=pltpu.VMEM)
SMEM = pl.BlockSpec(memory_space=pltpu.SMEM)


def gelu(v):
    c = 0.7978845608028654
    inner = v * (c + (c * 0.044715) * (v * v))
    half = 0.5 * v
    return half + half * jnp.tanh(inner)


def dot(a, b):
    return jnp.dot(a, b, preferred_element_type=F32)


def dot_nt(a, b):
    return lax.dot_general(a, b, (((1,), (1,)), ((), ())), preferred_element_type=F32)


def normed(x, gain):
    mean = jnp.mean(x, -1, keepdims=True)
    centred = x - mean
    var = jnp.mean(centred * centred, -1, keepdims=True)
    return (centred * lax.rsqrt(var + EPS) * gain).astype(BF)


def iota(shape, axis):
    return lax.broadcasted_iota(jnp.int32, shape, axis)


def encode_kernel(place, count, dest, token, rows, w_in, w_out, slab, encoded, slots):
    live_count = count[0]
    lane_base = (place[0] % 8) * CAP
    before = iota((BLK, BLK), 0) < iota((BLK, BLK), 1)
    upper = jnp.where(before, 1.0, 0.0).astype(BF)
    owner_col = iota((OWNERS, BLK), 0)
    lane_col = iota((LANES, BLK), 0)
    carry = jnp.zeros((OWNERS, 1), F32)
    high = jnp.zeros((OWNERS, LANES), F32)
    low = jnp.zeros((OWNERS, LANES), F32)
    for b in range(OBS_DEV // BLK):
        cols = slice(b * BLK, (b + 1) * BLK)
        target = dest[:, cols]
        live = (iota((1, BLK), 1) + b * BLK) < live_count
        hits = jnp.where((owner_col == target) & live, 1.0, 0.0)
        hits_bf = hits.astype(BF)
        earlier = dot(hits_bf, upper) + carry
        carry = carry + jnp.sum(hits, 1, keepdims=True)
        rank = jnp.sum(earlier * hits, 0, keepdims=True).astype(jnp.int32)
        slots[:, cols] = jnp.where(live, target * CAP + rank, -1)
        cell = token[:, cols]
        spread = lane_col == (rank + lane_base)
        row_part = jnp.where(spread, (cell // CLON).astype(F32), 0.0).astype(BF)
        col_part = jnp.where(spread, (cell % CLON + 1).astype(F32), 0.0).astype(BF)
        high = high + dot_nt(hits_bf, row_part)
        low = low + dot_nt(hits_bf, col_part)
    sub = iota((OWNERS, 8, LANES), 1)
    marks = jnp.where(sub == 0, high[:, None, :], jnp.where(sub == 1, low[:, None, :], 0.0))
    slab[:, 4 * CAP : SLAB, :] = marks.astype(BF)

    def encode_block(b, _):
        r = pl.ds(pl.multiple_of(b * BLK, BLK), BLK)
        x = rows[r, :]
        total = jnp.zeros((BLK, D), F32)
        for t in range(FF // 512):
            f = slice(t * 512, (t + 1) * 512)
            hidden = gelu(dot(x, w_in[:, f])).astype(BF)
            total = total + dot(hidden, w_out[f, :])
        encoded[r, :] = total.astype(BF)
        return 0

    lax.fori_loop(0, OBS_DEV // BLK, encode_block, 0)

    def place_block(b, _):
        wanted = iota((BLK, OBS_DEV), 0) + b * BLK
        pick = jnp.where(slots[...] == wanted, 1.0, 0.0).astype(BF)
        moved = dot(pick, encoded[...]).astype(BF).reshape(BLK // CAP, CAP, D)
        d = pl.ds(b * (BLK // CAP), BLK // CAP)
        for k in range(4):
            slab[d, k * CAP : (k + 1) * CAP, :] = moved[:, :, k * LANES : (k + 1) * LANES]
        return 0

    lax.fori_loop(0, OWNERS * CAP // BLK, place_block, 0)


def encode(place, count, dest, token, rows, w_in, w_out):
    return pl.pallas_call(
        encode_kernel,
        out_shape=jax.ShapeDtypeStruct((OWNERS, SLAB, LANES), BF),
        in_specs=[SMEM, SMEM] + [VMEM] * 5,
        out_specs=VMEM,
        scratch_shapes=[pltpu.VMEM((OBS_DEV, D), BF), pltpu.VMEM((1, OBS_DEV), jnp.int32)],
        compiler_params=pltpu.CompilerParams(vmem_limit_bytes=24 << 20),
        cost_estimate=pl.CostEstimate(
            flops=7 << 30, transcendentals=OBS_DEV * FF, bytes_accessed=8 << 20
        ),
        name="encode",
    )(place, count, dest, token, rows, w_in, w_out)


def block_body(x, bias, gain_a, gain_b, w_qkv, w_proj, w_up, w_down, qkv, mixed):
    count = x.shape[0]
    area = WIN * WIN
    qkv[...] = dot(normed(x, gain_a), w_qkv[...]).astype(BF)
    first = iota((area, LANES), 1) < 64
    ones = jnp.ones((area, LANES), BF)
    for w in range(count // area):
        r = slice(w * area, (w + 1) * area)
        for pair in range(HEADS // 2):
            c = pair * LANES
            q = qkv[r, c : c + LANES] * BF(0.125)
            k = qkv[r, D + c : D + c + LANES]
            v = jnp.concatenate([qkv[r, 2 * D + c : 2 * D + c + LANES], ones], 1)
            out = []
            for head in range(2):
                mine = first if head == 0 else jnp.logical_not(first)
                scores = dot_nt(jnp.where(mine, q, BF(0)), k)
                if bias is not None:
                    scores = scores + bias
                probs = jnp.exp(scores - jnp.max(scores, -1, keepdims=True)).astype(BF)
                both = dot(probs, v)
                out.append(both[:, :LANES] / both[:, LANES:])
            mixed[r, c : c + LANES] = jnp.where(first, out[0], out[1]).astype(BF)
    attended = x + dot(mixed[...], w_proj[...])
    h = normed(attended, gain_b)
    total = attended
    for t in range(FF // 512):
        f = slice(t * 512, (t + 1) * 512)
        total = total + dot(gelu(dot(h, w_up[:, f])).astype(BF), w_down[f, :])
    return total.astype(BF)


def bin_kernel(arrived, background, gains, w_qkv, w_proj, w_up, w_down, out, lined, pick, qkv, mixed, state):
    for k in range(4):
        lined[:, k * LANES : (k + 1) * LANES] = arrived[:, k * CAP : (k + 1) * CAP, :].reshape(
            OWNERS * CAP, LANES
        )
    sub = iota((OWNERS, 8, LANES), 1)
    weight = jnp.where(sub == 0, float(CLON), 1.0)
    marks = arrived[:, 4 * CAP : SLAB, :].astype(F32) * weight
    marks = jnp.sum(marks.reshape(OWNERS // 8, 64, LANES), 1).astype(jnp.int32)
    row = iota((CELLS, LANES), 0)
    inner = row % BLK
    cell = (inner // WIN) * CLON + (row // BLK) * WIN + inner % WIN + 1
    tally = jnp.zeros((CELLS, LANES), F32)
    for g in range(OWNERS // 8):
        hit = jnp.where(cell == marks[g : g + 1, :], 1.0, 0.0)
        tally = tally + hit
        pick[:, g * LANES : (g + 1) * LANES] = hit.astype(BF)
    tally = jnp.sum(tally, 1, keepdims=True)
    sums = dot(pick[...], lined[...]) / jnp.maximum(tally, 1.0)
    for w in range(2):
        r = slice(w * BLK, (w + 1) * BLK)
        back = background[:, w * WIN : (w + 1) * WIN, :].astype(F32).reshape(BLK, D)
        state[r, :] = (back + sums[r, :]).astype(BF).astype(F32)
    done = block_body(
        state[...], None, gains[0:1, :], gains[1:2, :], w_qkv, w_proj, w_up, w_down, qkv, mixed
    )
    for w in range(2):
        out[:, w * WIN : (w + 1) * WIN, :] = done[w * BLK : (w + 1) * BLK].reshape(WIN, WIN, D)


BLOCK_SCRATCH = [
    pltpu.VMEM((CELLS, 3 * D), BF),
    pltpu.VMEM((CELLS, D), BF),
    pltpu.VMEM((CELLS, D), F32),
]
BLOCK_COST = pl.CostEstimate(flops=4 << 30, transcendentals=2 << 20, bytes_accessed=8 << 20)


def bin_block(arrived, background, gains, w_qkv, w_proj, w_up, w_down):
    return pl.pallas_call(
        bin_kernel,
        out_shape=jax.ShapeDtypeStruct((CLAT, CLON, D), BF),
        in_specs=[VMEM] * 7,
        out_specs=VMEM,
        scratch_shapes=[
            pltpu.VMEM((OWNERS * CAP, D), BF),
            pltpu.VMEM((CELLS, OWNERS * CAP), BF),
        ]
        + BLOCK_SCRATCH,
        compiler_params=pltpu.CompilerParams(vmem_limit_bytes=28 << 20),
        cost_estimate=BLOCK_COST,
        name="bin_block",
    )(arrived, background, gains, w_qkv, w_proj, w_up, w_down)


def shift_kernel(last, grid, below, right, corner, gains, w_qkv, w_proj, w_up, w_down, out, qkv, mixed, state, bias):
    area = WIN * WIN
    split = (iota((area, area), 0) < area // 2) != (iota((area, area), 1) < area // 2)
    bias[...] = jnp.where(split & (last[0] == 1), -1e30, 0.0)
    top = grid[HALF:, HALF:, :].astype(F32)
    bottom = below[...].astype(F32)
    h = area // 2
    state[0:h, :] = top[:, :WIN, :].reshape(h, D)
    state[h : 2 * h, :] = bottom[:, :WIN, :].reshape(h, D)
    top = jnp.concatenate([top[:, WIN:, :], right[...].astype(F32)], 1)
    bottom = jnp.concatenate([bottom[:, WIN:, :], corner[...].astype(F32)], 1)
    state[2 * h : 3 * h, :] = top.reshape(h, D)
    state[3 * h : 4 * h, :] = bottom.reshape(h, D)
    done = block_body(
        state[...], bias[...], gains[0:1, :], gains[1:2, :], w_qkv, w_proj, w_up, w_down, qkv, mixed
    )
    for w in range(2):
        out[:, w * WIN : (w + 1) * WIN, :] = done[w * BLK : (w + 1) * BLK].reshape(WIN, WIN, D)


def shift_block(last, grid, below, right, corner, gains, w_qkv, w_proj, w_up, w_down):
    return pl.pallas_call(
        shift_kernel,
        out_shape=jax.ShapeDtypeStruct((CLAT, CLON, D), BF),
        in_specs=[SMEM] + [VMEM] * 9,
        out_specs=VMEM,
        scratch_shapes=BLOCK_SCRATCH + [pltpu.VMEM((WIN * WIN, WIN * WIN), F32)],
        compiler_params=pltpu.CompilerParams(vmem_limit_bytes=28 << 20),
        cost_estimate=BLOCK_COST,
        name="shift_block",
    )(last, grid, below, right, corner, gains, w_qkv, w_proj, w_up, w_down)


def moved(block, lat_step, lon_step):
    lat_count = lax.axis_size("lat")
    lon_count = lax.axis_size("lon")
    route = [
        (
            i * lon_count + j,
            (i + lat_step) % lat_count * lon_count + (j + lon_step) % lon_count,
        )
        for i in range(lat_count)
        for j in range(lon_count)
    ]
    return lax.ppermute(block, ("lat", "lon"), route)


def on_device(
    obs_rows,
    obs_dest,
    obs_token,
    obs_count,
    background,
    w_obs_in,
    w_obs_out,
    w_qkv,
    w_proj,
    w_up,
    w_down,
    norm_gain,
):
    lat = lax.axis_index("lat")
    place = (lat * lax.axis_size("lon") + lax.axis_index("lon")).astype(jnp.int32).reshape(1)
    slab = encode(
        place,
        obs_count,
        obs_dest.reshape(1, OBS_DEV),
        obs_token.reshape(1, OBS_DEV),
        obs_rows,
        w_obs_in,
        w_obs_out,
    )
    arrived = lax.all_to_all(slab, ("lat", "lon"), split_axis=0, concat_axis=0, tiled=True)
    grid = bin_block(arrived, background, norm_gain[0], w_qkv[0], w_proj[0], w_up[0], w_down[0])
    below = moved(grid[:HALF, HALF:], -1, 0)
    right = moved(grid[HALF:, :HALF], 0, -1)
    corner = moved(grid[:HALF, :HALF], -1, -1)
    last = (lat == lax.axis_size("lat") - 1).astype(jnp.int32).reshape(1)
    done = shift_block(
        last, grid, below, right, corner, norm_gain[1], w_qkv[1], w_proj[1], w_up[1], w_down[1]
    )
    cut = CLON - HALF
    above = moved(done[HALF:, :cut], 1, 0)
    left = moved(done[:HALF, cut:], 0, 1)
    corner = moved(done[HALF:, cut:], 1, 1)
    top = jnp.concatenate([corner, above], 1)
    bottom = jnp.concatenate([left, done[:HALF, :cut]], 1)
    return jnp.concatenate([top, bottom], 0)


def solution(mesh):
    both = P(("lat", "lon"))
    rows = P(("lat", "lon"), None)
    grid = P("lat", "lon", None)
    return jax.shard_map(
        on_device,
        mesh=mesh,
        in_specs=(rows, rows, both, both, grid) + (P(),) * 7,
        out_specs=grid,
        check_vma=False,
    )
```

```python
import jax
import jax.numpy as jnp
from jax import lax
from jax.experimental import pallas as pl
from jax.experimental.pallas import tpu as pltpu
from jax.sharding import PartitionSpec as P

D = 512
FF = 2048
HEADS = 8
WIN = 16
HALF = 8
CLAT = 16
CLON = 32
CELLS = CLAT * CLON
OBS_DEV = 1024
OWNERS = 128
CAP = 16
LANES = 128
SLAB = 4 * CAP + 8
BLK = 256
TILE = 512
EPS = 1e-5
ENCODE_VMEM = 67043328 - (100 << 10)
BIN_VMEM = 67043328 - (3000 << 10)
SHIFT_VMEM = 67043328 - (1100 << 10)
BF = jnp.bfloat16
F32 = jnp.float32
VMEM = pl.BlockSpec(memory_space=pltpu.VMEM)
HBM = pl.BlockSpec(memory_space=pltpu.HBM)
SMEM = pl.BlockSpec(memory_space=pltpu.SMEM)


def gelu(v):
    c = 0.7978845608028654
    inner = v * (c + (c * 0.044715) * (v * v))
    half = 0.5 * v
    return half + half * jnp.tanh(inner)


def dot(a, b):
    return jnp.dot(a, b, preferred_element_type=F32)


def dot_nt(a, b):
    return lax.dot_general(a, b, (((1,), (1,)), ((), ())), preferred_element_type=F32)


def normed(x, gain):
    mean = jnp.mean(x, -1, keepdims=True)
    centred = x - mean
    var = jnp.mean(centred * centred, -1, keepdims=True)
    return (centred * lax.rsqrt(var + EPS) * gain).astype(BF)


def iota(shape, axis):
    return lax.broadcasted_iota(jnp.int32, shape, axis)


def encode_kernel(
    place, count, dest, token, rows_hbm, w_in_hbm, w_out_hbm, slab_hbm,
    rows, w_in, w_out, slab, encoded, slots, in_sems, out_sems,
):
    tiles = FF // TILE
    rows_copy = pltpu.make_async_copy(rows_hbm, rows, in_sems.at[2 * tiles])
    w_in_copies = []
    w_out_copies = []
    for t in range(tiles):
        f = slice(t * TILE, (t + 1) * TILE)
        w_in_copies.append(pltpu.make_async_copy(w_in_hbm.at[:, f], w_in.at[:, f], in_sems.at[t]))
        w_out_copies.append(
            pltpu.make_async_copy(w_out_hbm.at[f, :], w_out.at[f, :], in_sems.at[tiles + t])
        )
    rows_copy.start()
    for t in range(tiles):
        w_in_copies[t].start()
        w_out_copies[t].start()

    live_count = count[0]
    lane_base = (place[0] % 8) * CAP
    before = iota((BLK, BLK), 0) < iota((BLK, BLK), 1)
    upper = jnp.where(before, 1.0, 0.0).astype(BF)
    owner_col = iota((OWNERS, BLK), 0)
    lane_col = iota((LANES, BLK), 0)
    carry = jnp.zeros((OWNERS, 1), F32)
    high = jnp.zeros((OWNERS, LANES), F32)
    low = jnp.zeros((OWNERS, LANES), F32)
    for b in range(OBS_DEV // BLK):
        cols = slice(b * BLK, (b + 1) * BLK)
        target = dest[:, cols]
        live = (iota((1, BLK), 1) + b * BLK) < live_count
        hits = jnp.where((owner_col == target) & live, 1.0, 0.0)
        hits_bf = hits.astype(BF)
        earlier = dot(hits_bf, upper) + carry
        carry = carry + jnp.sum(hits, 1, keepdims=True)
        rank = jnp.sum(earlier * hits, 0, keepdims=True).astype(jnp.int32)
        slots[:, cols] = jnp.where(live, target * CAP + rank, -1)
        cell = token[:, cols]
        spread = lane_col == (rank + lane_base)
        row_part = jnp.where(spread, (cell // CLON).astype(F32), 0.0).astype(BF)
        col_part = jnp.where(spread, (cell % CLON + 1).astype(F32), 0.0).astype(BF)
        high = high + dot_nt(hits_bf, row_part)
        low = low + dot_nt(hits_bf, col_part)
    sub = iota((OWNERS, 8, LANES), 1)
    marks = jnp.where(sub == 0, high[:, None, :], jnp.where(sub == 1, low[:, None, :], 0.0))
    slab[:, 4 * CAP : SLAB, :] = marks.astype(BF)
    rows_copy.wait()

    def encode_block(b, _):
        r = pl.ds(pl.multiple_of(b * BLK, BLK), BLK)
        x = rows[r, :]
        total = jnp.zeros((BLK, D), F32)
        for t in range(tiles):

            @pl.when(b == 0)
            def _():
                w_in_copies[t].wait()
                w_out_copies[t].wait()

            f = slice(t * TILE, (t + 1) * TILE)
            hidden = gelu(dot(x, w_in[:, f])).astype(BF)
            total = total + dot(hidden, w_out[f, :])
        encoded[r, :] = total.astype(BF)
        return 0

    lax.fori_loop(0, OBS_DEV // BLK, encode_block, 0)
    step = BLK // CAP

    def slab_copy(b):
        d = pl.ds(b * step, step)
        return pltpu.make_async_copy(slab.at[d], slab_hbm.at[d], out_sems.at[b])

    def place_block(b, _):
        wanted = iota((BLK, OBS_DEV), 0) + b * BLK
        pick = jnp.where(slots[...] == wanted, 1.0, 0.0).astype(BF)
        moved = dot(pick, encoded[...]).astype(BF).reshape(step, CAP, D)
        d = pl.ds(b * step, step)
        for k in range(4):
            slab[d, k * CAP : (k + 1) * CAP, :] = moved[:, :, k * LANES : (k + 1) * LANES]
        slab_copy(b).start()
        return 0

    lax.fori_loop(0, OWNERS // step, place_block, 0)
    for b in range(OWNERS // step):
        slab_copy(b).wait()


def encode(place, count, dest, token, rows, w_in, w_out):
    return pl.pallas_call(
        encode_kernel,
        out_shape=jax.ShapeDtypeStruct((OWNERS, SLAB, LANES), BF),
        in_specs=[SMEM, SMEM, VMEM, VMEM, HBM, HBM, HBM],
        out_specs=HBM,
        scratch_shapes=[
            pltpu.VMEM((OBS_DEV, D), BF),
            pltpu.VMEM((D, FF), BF),
            pltpu.VMEM((FF, D), BF),
            pltpu.VMEM((OWNERS, SLAB, LANES), BF),
            pltpu.VMEM((OBS_DEV, D), BF),
            pltpu.VMEM((1, OBS_DEV), jnp.int32),
            pltpu.SemaphoreType.DMA((2 * FF // TILE + 1,)),
            pltpu.SemaphoreType.DMA((OWNERS * CAP // BLK,)),
        ],
        compiler_params=pltpu.CompilerParams(vmem_limit_bytes=ENCODE_VMEM),
        cost_estimate=pl.CostEstimate(
            flops=7 << 30, transcendentals=OBS_DEV * FF, bytes_accessed=8 << 20
        ),
        name="encode",
    )(place, count, dest, token, rows, w_in, w_out)


def weight_copies(layer, hbm, vmem, sems):
    w_qkv, w_proj, w_up, w_down = hbm
    v_qkv, v_proj, v_up, v_down = vmem
    pairs = [(w_qkv.at[layer], v_qkv), (w_proj.at[layer], v_proj)]
    for t in range(FF // TILE):
        f = slice(t * TILE, (t + 1) * TILE)
        pairs.append((w_up.at[layer, :, f], v_up.at[:, f]))
        pairs.append((w_down.at[layer, f, :], v_down.at[f, :]))
    copies = [pltpu.make_async_copy(a, b, sems.at[i]) for i, (a, b) in enumerate(pairs)]
    for copy in copies:
        copy.start()
    return copies


def block_body(x, bias, gain_a, gain_b, weights, copies, qkv, mixed):
    w_qkv, w_proj, w_up, w_down = weights
    count = x.shape[0]
    area = WIN * WIN
    h = normed(x, gain_a)
    copies[0].wait()
    qkv[...] = dot(h, w_qkv[...]).astype(BF)
    first = iota((area, LANES), 1) < 64
    ones = jnp.ones((area, LANES), BF)
    for w in range(count // area):
        r = slice(w * area, (w + 1) * area)
        for pair in range(HEADS // 2):
            c = pair * LANES
            q = qkv[r, c : c + LANES] * BF(0.125)
            k = qkv[r, D + c : D + c + LANES]
            v = jnp.concatenate([qkv[r, 2 * D + c : 2 * D + c + LANES], ones], 1)
            out = []
            for head in range(2):
                mine = first if head == 0 else jnp.logical_not(first)
                scores = dot_nt(jnp.where(mine, q, BF(0)), k)
                if bias is not None:
                    scores = scores + bias
                probs = jnp.exp(scores - jnp.max(scores, -1, keepdims=True)).astype(BF)
                both = dot(probs, v)
                out.append(both[:, :LANES] / both[:, LANES:])
            mixed[r, c : c + LANES] = jnp.where(first, out[0], out[1]).astype(BF)
    copies[1].wait()
    attended = x + dot(mixed[...], w_proj[...])
    h = normed(attended, gain_b)
    total = attended
    for t in range(FF // TILE):
        copies[2 + 2 * t].wait()
        copies[3 + 2 * t].wait()
        f = slice(t * TILE, (t + 1) * TILE)
        total = total + dot(gelu(dot(h, w_up[:, f])).astype(BF), w_down[f, :])
    return total.astype(BF)


def bin_kernel(
    arrived, background_hbm, gains, wq, wp, wu, wd, keep, below, right, corner,
    lined, pick, background, vq, vp, vu, vd, qkv, mixed, state, sems, back_sem,
):
    back_copy = pltpu.make_async_copy(background_hbm, background, back_sem.at[0])
    back_copy.start()
    copies = weight_copies(0, (wq, wp, wu, wd), (vq, vp, vu, vd), sems)
    for k in range(4):
        lined[:, k * LANES : (k + 1) * LANES] = arrived[:, k * CAP : (k + 1) * CAP, :].reshape(
            OWNERS * CAP, LANES
        )
    sub = iota((OWNERS, 8, LANES), 1)
    weight = jnp.where(sub == 0, float(CLON), 1.0)
    marks = arrived[:, 4 * CAP : SLAB, :].astype(F32) * weight
    marks = jnp.sum(marks.reshape(OWNERS // 8, 64, LANES), 1).astype(jnp.int32)
    row = iota((CELLS, LANES), 0)
    inner = row % BLK
    cell = (inner // WIN) * CLON + (row // BLK) * WIN + inner % WIN + 1
    tally = jnp.zeros((CELLS, LANES), F32)
    for g in range(OWNERS // 8):
        hit = jnp.where(cell == marks[g : g + 1, :], 1.0, 0.0)
        tally = tally + hit
        pick[:, g * LANES : (g + 1) * LANES] = hit.astype(BF)
    tally = jnp.sum(tally, 1, keepdims=True)
    sums = dot(pick[...], lined[...]) / jnp.maximum(tally, 1.0)
    back_copy.wait()
    for w in range(2):
        r = slice(w * BLK, (w + 1) * BLK)
        back = background[:, w * WIN : (w + 1) * WIN, :].astype(F32).reshape(BLK, D)
        state[r, :] = (back + sums[r, :]).astype(BF).astype(F32)
    done = block_body(
        state[...], None, gains[0, 0:1, :], gains[0, 1:2, :], (vq, vp, vu, vd), copies, qkv, mixed
    )
    one = done[:BLK].reshape(WIN, WIN, D)
    two = done[BLK:].reshape(WIN, WIN, D)
    corner[...] = one[:HALF, :HALF]
    right[...] = one[HALF:, :HALF]
    below[:, :HALF, :] = one[:HALF, HALF:]
    below[:, HALF:, :] = two[:HALF]
    keep[:, :HALF, :] = one[HALF:, HALF:]
    keep[:, HALF:, :] = two[HALF:]


WEIGHT_SCRATCH = [
    pltpu.VMEM((D, 3 * D), BF),
    pltpu.VMEM((D, D), BF),
    pltpu.VMEM((D, FF), BF),
    pltpu.VMEM((FF, D), BF),
]
BLOCK_SCRATCH = [
    pltpu.VMEM((CELLS, 3 * D), BF),
    pltpu.VMEM((CELLS, D), BF),
    pltpu.VMEM((CELLS, D), F32),
]
WEIGHT_SEMS = pltpu.SemaphoreType.DMA((2 + 2 * FF // TILE,))
BLOCK_COST = pl.CostEstimate(flops=4 << 30, transcendentals=2 << 20, bytes_accessed=8 << 20)
PIECES = (
    jax.ShapeDtypeStruct((HALF, CLON - HALF, D), BF),
    jax.ShapeDtypeStruct((HALF, CLON - HALF, D), BF),
    jax.ShapeDtypeStruct((HALF, HALF, D), BF),
    jax.ShapeDtypeStruct((HALF, HALF, D), BF),
)


def bin_block(arrived, background, gains, *weights):
    return pl.pallas_call(
        bin_kernel,
        out_shape=PIECES,
        in_specs=[VMEM, HBM, VMEM] + [HBM] * 4,
        out_specs=[VMEM] * 4,
        scratch_shapes=[
            pltpu.VMEM((OWNERS * CAP, D), BF),
            pltpu.VMEM((CELLS, OWNERS * CAP), BF),
            pltpu.VMEM((CLAT, CLON, D), BF),
        ]
        + WEIGHT_SCRATCH
        + BLOCK_SCRATCH
        + [WEIGHT_SEMS, pltpu.SemaphoreType.DMA((1,))],
        compiler_params=pltpu.CompilerParams(vmem_limit_bytes=BIN_VMEM),
        cost_estimate=BLOCK_COST,
        name="bin_block",
    )(arrived, background, gains, *weights)


def shift_kernel(
    last, mine, below, right, corner, gains, wq, wp, wu, wd, keep, above, left, diagonal,
    vq, vp, vu, vd, qkv, mixed, state, bias, sems,
):
    copies = weight_copies(1, (wq, wp, wu, wd), (vq, vp, vu, vd), sems)
    area = WIN * WIN
    split = (iota((area, area), 0) < area // 2) != (iota((area, area), 1) < area // 2)
    bias[...] = jnp.where(split & (last[0] == 1), -1e30, 0.0)
    top = mine[...].astype(F32)
    bottom = below[...].astype(F32)
    h = area // 2
    state[0:h, :] = top[:, :WIN, :].reshape(h, D)
    state[h : 2 * h, :] = bottom[:, :WIN, :].reshape(h, D)
    top = jnp.concatenate([top[:, WIN:, :], right[...].astype(F32)], 1)
    bottom = jnp.concatenate([bottom[:, WIN:, :], corner[...].astype(F32)], 1)
    state[2 * h : 3 * h, :] = top.reshape(h, D)
    state[3 * h : 4 * h, :] = bottom.reshape(h, D)
    done = block_body(
        state[...], bias[...], gains[1, 0:1, :], gains[1, 1:2, :], (vq, vp, vu, vd), copies, qkv, mixed
    )
    one = done[:BLK].reshape(WIN, WIN, D)
    two = done[BLK:].reshape(WIN, WIN, D)
    diagonal[...] = two[HALF:, HALF:]
    left[...] = two[:HALF, HALF:]
    above[:, :WIN, :] = one[HALF:]
    above[:, WIN:, :] = two[HALF:, :HALF]
    keep[:, :WIN, :] = one[:HALF]
    keep[:, WIN:, :] = two[:HALF, :HALF]


def shift_block(last, mine, below, right, corner, gains, *weights):
    return pl.pallas_call(
        shift_kernel,
        out_shape=PIECES,
        in_specs=[SMEM] + [VMEM] * 5 + [HBM] * 4,
        out_specs=[VMEM] * 4,
        scratch_shapes=WEIGHT_SCRATCH
        + BLOCK_SCRATCH
        + [pltpu.VMEM((WIN * WIN, WIN * WIN), F32), WEIGHT_SEMS],
        compiler_params=pltpu.CompilerParams(vmem_limit_bytes=SHIFT_VMEM),
        cost_estimate=BLOCK_COST,
        name="shift_block",
    )(last, mine, below, right, corner, gains, *weights)


def moved(block, lat_step, lon_step):
    lat_count = lax.axis_size("lat")
    lon_count = lax.axis_size("lon")
    route = [
        (
            i * lon_count + j,
            (i + lat_step) % lat_count * lon_count + (j + lon_step) % lon_count,
        )
        for i in range(lat_count)
        for j in range(lon_count)
    ]
    return lax.ppermute(block, ("lat", "lon"), route)


def on_device(
    obs_rows,
    obs_dest,
    obs_token,
    obs_count,
    background,
    w_obs_in,
    w_obs_out,
    w_qkv,
    w_proj,
    w_up,
    w_down,
    norm_gain,
):
    lat = lax.axis_index("lat")
    place = (lat * lax.axis_size("lon") + lax.axis_index("lon")).astype(jnp.int32).reshape(1)
    slab = encode(
        place,
        obs_count,
        obs_dest.reshape(1, OBS_DEV),
        obs_token.reshape(1, OBS_DEV),
        obs_rows,
        w_obs_in,
        w_obs_out,
    )
    arrived = lax.all_to_all(slab, ("lat", "lon"), split_axis=0, concat_axis=0, tiled=True)
    weights = (w_qkv, w_proj, w_up, w_down)
    mine, below, right, corner = bin_block(arrived, background, norm_gain, *weights)
    below = moved(below, -1, 0)
    right = moved(right, 0, -1)
    corner = moved(corner, -1, -1)
    last = (lat == lax.axis_size("lat") - 1).astype(jnp.int32).reshape(1)
    mine, above, left, corner = shift_block(
        last, mine, below, right, corner, norm_gain, *weights
    )
    above = moved(above, 1, 0)
    left = moved(left, 0, 1)
    corner = moved(corner, 1, 1)
    top = jnp.concatenate([corner, above], 1)
    bottom = jnp.concatenate([left, mine], 1)
    return jnp.concatenate([top, bottom], 0)


def solution(mesh):
    both = P(("lat", "lon"))
    rows = P(("lat", "lon"), None)
    grid = P("lat", "lon", None)
    return jax.shard_map(
        on_device,
        mesh=mesh,
        in_specs=(rows, rows, both, both, grid) + (P(),) * 7,
        out_specs=grid,
        check_vma=False,
    )
```

```python
import jax
import jax.numpy as jnp
from jax import lax
from jax.experimental import pallas as pl
from jax.experimental.pallas import tpu as pltpu
from jax.sharding import PartitionSpec as P

D = 512
FF = 2048
HEADS = 8
WIN = 16
HALF = 8
CLAT = 16
CLON = 32
CELLS = CLAT * CLON
OBS_DEV = 1024
OWNERS = 128
CAP = 16
LANES = 128
SLAB = 4 * CAP + 8
BLK = 256
TILE = 512
EPS = 1e-5
ENCODE_VMEM = 67043328 - (100 << 10)
BIN_VMEM = (64 << 20) - (16000 << 10)
SHIFT_VMEM = (64 << 20) - (12000 << 10)
BF = jnp.bfloat16
F32 = jnp.float32
VMEM = pl.BlockSpec(memory_space=pltpu.VMEM)
HBM = pl.BlockSpec(memory_space=pltpu.HBM)
SMEM = pl.BlockSpec(memory_space=pltpu.SMEM)


def gelu(v):
    c = 0.7978845608028654
    inner = v * (c + (c * 0.044715) * (v * v))
    half = 0.5 * v
    return half + half * jnp.tanh(inner)


def dot(a, b):
    return jnp.dot(a, b, preferred_element_type=F32)


def dot_nt(a, b):
    return lax.dot_general(a, b, (((1,), (1,)), ((), ())), preferred_element_type=F32)


def normed(x, gain):
    mean = jnp.mean(x, -1, keepdims=True)
    centred = x - mean
    var = jnp.mean(centred * centred, -1, keepdims=True)
    return (centred * lax.rsqrt(var + EPS) * gain).astype(BF)


def iota(shape, axis):
    return lax.broadcasted_iota(jnp.int32, shape, axis)


def encode_kernel(
    place, count, dest, token, rows_hbm, w_in_hbm, w_out_hbm, slab_hbm,
    rows, w_in, w_out, slab, encoded, total, slots, in_sems, out_sems,
):
    tiles = FF // TILE
    rows_copy = pltpu.make_async_copy(rows_hbm, rows, in_sems.at[2 * tiles])
    w_in_copies = []
    w_out_copies = []
    for t in range(tiles):
        f = slice(t * TILE, (t + 1) * TILE)
        w_in_copies.append(pltpu.make_async_copy(w_in_hbm.at[:, f], w_in.at[:, f], in_sems.at[t]))
        w_out_copies.append(
            pltpu.make_async_copy(w_out_hbm.at[f, :], w_out.at[f, :], in_sems.at[tiles + t])
        )
    rows_copy.start()
    w_in_copies[0].start()
    w_out_copies[0].start()

    live_count = count[0]
    lane_base = (place[0] % 8) * CAP
    before = iota((BLK, BLK), 0) < iota((BLK, BLK), 1)
    upper = jnp.where(before, 1.0, 0.0).astype(BF)
    owner_col = iota((OWNERS, BLK), 0)
    lane_col = iota((LANES, BLK), 0)
    carry = jnp.zeros((OWNERS, 1), F32)
    high = jnp.zeros((OWNERS, LANES), F32)
    low = jnp.zeros((OWNERS, LANES), F32)
    for b in range(OBS_DEV // BLK):
        cols = slice(b * BLK, (b + 1) * BLK)
        target = dest[:, cols]
        live = (iota((1, BLK), 1) + b * BLK) < live_count
        hits = jnp.where((owner_col == target) & live, 1.0, 0.0)
        hits_bf = hits.astype(BF)
        earlier = dot(hits_bf, upper) + carry
        carry = carry + jnp.sum(hits, 1, keepdims=True)
        rank = jnp.sum(earlier * hits, 0, keepdims=True).astype(jnp.int32)
        slots[:, cols] = jnp.where(live, target * CAP + rank, -1)
        cell = token[:, cols]
        spread = lane_col == (rank + lane_base)
        row_part = jnp.where(spread, (cell // CLON).astype(F32), 0.0).astype(BF)
        col_part = jnp.where(spread, (cell % CLON + 1).astype(F32), 0.0).astype(BF)
        high = high + dot_nt(hits_bf, row_part)
        low = low + dot_nt(hits_bf, col_part)
    sub = iota((OWNERS, 8, LANES), 1)
    marks = jnp.where(sub == 0, high[:, None, :], jnp.where(sub == 1, low[:, None, :], 0.0))
    slab[:, 4 * CAP : SLAB, :] = marks.astype(BF)
    rows_copy.wait()
    for t in range(tiles):
        w_in_copies[t].wait()
        w_out_copies[t].wait()
        if t + 1 < tiles:
            w_in_copies[t + 1].start()
            w_out_copies[t + 1].start()
        f = slice(t * TILE, (t + 1) * TILE)

        def encode_block(b, _):
            r = pl.ds(pl.multiple_of(b * BLK, BLK), BLK)
            hidden = gelu(dot(rows[r, :], w_in[:, f])).astype(BF)
            part = dot(hidden, w_out[f, :])
            if t > 0:
                part = total[r, :] + part
            if t + 1 < tiles:
                total[r, :] = part
            else:
                encoded[r, :] = part.astype(BF)
            return 0

        lax.fori_loop(0, OBS_DEV // BLK, encode_block, 0)
    step = BLK // CAP

    def slab_copy(b):
        d = pl.ds(b * step, step)
        return pltpu.make_async_copy(slab.at[d], slab_hbm.at[d], out_sems.at[b])

    def place_block(b, _):
        wanted = iota((BLK, OBS_DEV), 0) + b * BLK
        pick = jnp.where(slots[...] == wanted, 1.0, 0.0).astype(BF)
        moved = dot(pick, encoded[...]).astype(BF).reshape(step, CAP, D)
        d = pl.ds(b * step, step)
        for k in range(4):
            slab[d, k * CAP : (k + 1) * CAP, :] = moved[:, :, k * LANES : (k + 1) * LANES]
        slab_copy(b).start()
        return 0

    lax.fori_loop(0, OWNERS // step, place_block, 0)
    for b in range(OWNERS // step):
        slab_copy(b).wait()


def encode(place, count, dest, token, rows, w_in, w_out):
    return pl.pallas_call(
        encode_kernel,
        out_shape=jax.ShapeDtypeStruct((OWNERS, SLAB, LANES), BF),
        in_specs=[SMEM, SMEM, VMEM, VMEM, HBM, HBM, HBM],
        out_specs=HBM,
        scratch_shapes=[
            pltpu.VMEM((OBS_DEV, D), BF),
            pltpu.VMEM((D, FF), BF),
            pltpu.VMEM((FF, D), BF),
            pltpu.VMEM((OWNERS, SLAB, LANES), BF),
            pltpu.VMEM((OBS_DEV, D), BF),
            pltpu.VMEM((OBS_DEV, D), F32),
            pltpu.VMEM((1, OBS_DEV), jnp.int32),
            pltpu.SemaphoreType.DMA((2 * FF // TILE + 1,)),
            pltpu.SemaphoreType.DMA((OWNERS * CAP // BLK,)),
        ],
        compiler_params=pltpu.CompilerParams(vmem_limit_bytes=ENCODE_VMEM),
        cost_estimate=pl.CostEstimate(
            flops=7 << 30, transcendentals=OBS_DEV * FF, bytes_accessed=8 << 20
        ),
        name="encode",
    )(place, count, dest, token, rows, w_in, w_out)


def weight_copies(layer, hbm, vmem, sems):
    w_qkv, w_proj, w_up, w_down = hbm
    v_qkv, v_proj, v_up, v_down = vmem
    pairs = [(w_qkv.at[layer], v_qkv), (w_proj.at[layer], v_proj)]
    for t in range(FF // TILE):
        f = slice(t * TILE, (t + 1) * TILE)
        pairs.append((w_up.at[layer, :, f], v_up.at[:, f]))
        pairs.append((w_down.at[layer, f, :], v_down.at[f, :]))
    return [pltpu.make_async_copy(a, b, sems.at[i]) for i, (a, b) in enumerate(pairs)]


def block_body(layer, x, bias, gains, weights, copies, qkv, mixed):
    w_qkv, w_proj, w_up, w_down = weights
    count = x.shape[0]
    area = WIN * WIN
    h = normed(x, gains[layer, 0:1, :])
    copies[0].wait()
    for copy in copies[1:]:
        copy.start()
    qkv[...] = dot(h, w_qkv[...]).astype(BF)
    first = iota((area, LANES), 1) < 64
    ones = jnp.ones((area, LANES), BF)
    for w in range(count // area):
        r = slice(w * area, (w + 1) * area)
        for pair in range(HEADS // 2):
            c = pair * LANES
            q = qkv[r, c : c + LANES] * BF(0.125)
            k = qkv[r, D + c : D + c + LANES]
            v = jnp.concatenate([qkv[r, 2 * D + c : 2 * D + c + LANES], ones], 1)
            out = []
            for head in range(2):
                mine = first if head == 0 else jnp.logical_not(first)
                scores = dot_nt(jnp.where(mine, q, BF(0)), k)
                if bias is not None:
                    scores = scores + bias
                probs = jnp.exp(scores - jnp.max(scores, -1, keepdims=True)).astype(BF)
                both = dot(probs, v)
                out.append(both[:, :LANES] / both[:, LANES:])
            mixed[r, c : c + LANES] = jnp.where(first, out[0], out[1]).astype(BF)
    copies[1].wait()
    attended = x + dot(mixed[...], w_proj[...])
    h = normed(attended, gains[layer, 1:2, :])
    total = attended
    for t in range(FF // TILE):
        copies[2 * t + 2].wait()
        copies[2 * t + 3].wait()
        f = slice(t * TILE, (t + 1) * TILE)
        total = total + dot(gelu(dot(h, w_up[:, f])).astype(BF), w_down[f, :])
    return total.astype(BF)


def bin_kernel(
    arrived, background, gains, wq, wp, wu, wd, keep, below, right, corner,
    lined, pick, vq, vp, vu, vd, qkv, mixed, state, sems,
):
    copies = weight_copies(0, (wq, wp, wu, wd), (vq, vp, vu, vd), sems)
    copies[0].start()
    for k in range(4):
        lined[:, k * LANES : (k + 1) * LANES] = arrived[:, k * CAP : (k + 1) * CAP, :].reshape(
            OWNERS * CAP, LANES
        )
    sub = iota((OWNERS, 8, LANES), 1)
    weight = jnp.where(sub == 0, float(CLON), 1.0)
    marks = arrived[:, 4 * CAP : SLAB, :].astype(F32) * weight
    marks = jnp.sum(marks.reshape(OWNERS // 8, 64, LANES), 1).astype(jnp.int32)
    row = iota((CELLS, LANES), 0)
    inner = row % BLK
    cell = (inner // WIN) * CLON + (row // BLK) * WIN + inner % WIN + 1
    tally = jnp.zeros((CELLS, LANES), F32)
    for g in range(OWNERS // 8):
        hit = jnp.where(cell == marks[g : g + 1, :], 1.0, 0.0)
        tally = tally + hit
        pick[:, g * LANES : (g + 1) * LANES] = hit.astype(BF)
    tally = jnp.sum(tally, 1, keepdims=True)
    sums = dot(pick[...], lined[...]) / jnp.maximum(tally, 1.0)
    for w in range(2):
        r = slice(w * BLK, (w + 1) * BLK)
        back = background[:, w * WIN : (w + 1) * WIN, :].astype(F32).reshape(BLK, D)
        state[r, :] = (back + sums[r, :]).astype(BF).astype(F32)
    done = block_body(0, state[...], None, gains, (vq, vp, vu, vd), copies, qkv, mixed)
    one = done[:BLK].reshape(WIN, WIN, D)
    two = done[BLK:].reshape(WIN, WIN, D)
    corner[...] = one[:HALF, :HALF]
    right[...] = one[HALF:, :HALF]
    below[:, :HALF, :] = one[:HALF, HALF:]
    below[:, HALF:, :] = two[:HALF]
    keep[:, :HALF, :] = one[HALF:, HALF:]
    keep[:, HALF:, :] = two[HALF:]


WEIGHT_SCRATCH = [
    pltpu.VMEM((D, 3 * D), BF),
    pltpu.VMEM((D, D), BF),
    pltpu.VMEM((D, FF), BF),
    pltpu.VMEM((FF, D), BF),
]
WEIGHT_SEMS = pltpu.SemaphoreType.DMA((2 + 2 * FF // TILE,))
BLOCK_SCRATCH = [
    pltpu.VMEM((CELLS, 3 * D), BF),
    pltpu.VMEM((CELLS, D), BF),
    pltpu.VMEM((CELLS, D), F32),
]
BLOCK_COST = pl.CostEstimate(flops=4 << 30, transcendentals=2 << 20, bytes_accessed=8 << 20)
PIECES = (
    jax.ShapeDtypeStruct((HALF, CLON - HALF, D), BF),
    jax.ShapeDtypeStruct((HALF, CLON - HALF, D), BF),
    jax.ShapeDtypeStruct((HALF, HALF, D), BF),
    jax.ShapeDtypeStruct((HALF, HALF, D), BF),
)


def bin_block(arrived, background, gains, *weights):
    return pl.pallas_call(
        bin_kernel,
        out_shape=PIECES,
        in_specs=[VMEM] * 3 + [HBM] * 4,
        out_specs=[VMEM] * 4,
        scratch_shapes=[
            pltpu.VMEM((OWNERS * CAP, D), BF),
            pltpu.VMEM((CELLS, OWNERS * CAP), BF),
        ]
        + WEIGHT_SCRATCH
        + BLOCK_SCRATCH
        + [WEIGHT_SEMS],
        compiler_params=pltpu.CompilerParams(vmem_limit_bytes=BIN_VMEM),
        cost_estimate=BLOCK_COST,
        name="bin_block",
    )(arrived, background, gains, *weights)


def shift_kernel(
    last, mine, below, right, corner, gains, wq, wp, wu, wd, keep, above, left, diagonal,
    vq, vp, vu, vd, qkv, mixed, state, bias, sems,
):
    copies = weight_copies(1, (wq, wp, wu, wd), (vq, vp, vu, vd), sems)
    copies[0].start()
    area = WIN * WIN
    split = (iota((area, area), 0) < area // 2) != (iota((area, area), 1) < area // 2)
    bias[...] = jnp.where(split & (last[0] == 1), -1e30, 0.0)
    top = mine[...].astype(F32)
    bottom = below[...].astype(F32)
    h = area // 2
    state[0:h, :] = top[:, :WIN, :].reshape(h, D)
    state[h : 2 * h, :] = bottom[:, :WIN, :].reshape(h, D)
    top = jnp.concatenate([top[:, WIN:, :], right[...].astype(F32)], 1)
    bottom = jnp.concatenate([bottom[:, WIN:, :], corner[...].astype(F32)], 1)
    state[2 * h : 3 * h, :] = top.reshape(h, D)
    state[3 * h : 4 * h, :] = bottom.reshape(h, D)
    done = block_body(
        1, state[...], bias[...], gains, (vq, vp, vu, vd), copies, qkv, mixed
    )
    one = done[:BLK].reshape(WIN, WIN, D)
    two = done[BLK:].reshape(WIN, WIN, D)
    diagonal[...] = two[HALF:, HALF:]
    left[...] = two[:HALF, HALF:]
    above[:, :WIN, :] = one[HALF:]
    above[:, WIN:, :] = two[HALF:, :HALF]
    keep[:, :WIN, :] = one[:HALF]
    keep[:, WIN:, :] = two[:HALF, :HALF]


def shift_block(last, mine, below, right, corner, gains, *weights):
    return pl.pallas_call(
        shift_kernel,
        out_shape=PIECES,
        in_specs=[SMEM] + [VMEM] * 5 + [HBM] * 4,
        out_specs=[VMEM] * 4,
        scratch_shapes=WEIGHT_SCRATCH
        + BLOCK_SCRATCH
        + [pltpu.VMEM((WIN * WIN, WIN * WIN), F32), WEIGHT_SEMS],
        compiler_params=pltpu.CompilerParams(vmem_limit_bytes=SHIFT_VMEM),
        cost_estimate=BLOCK_COST,
        name="shift_block",
    )(last, mine, below, right, corner, gains, *weights)


def moved(block, lat_step, lon_step):
    lat_count = lax.axis_size("lat")
    lon_count = lax.axis_size("lon")
    route = [
        (
            i * lon_count + j,
            (i + lat_step) % lat_count * lon_count + (j + lon_step) % lon_count,
        )
        for i in range(lat_count)
        for j in range(lon_count)
    ]
    return lax.ppermute(block, ("lat", "lon"), route)


def on_device(
    obs_rows,
    obs_dest,
    obs_token,
    obs_count,
    background,
    w_obs_in,
    w_obs_out,
    w_qkv,
    w_proj,
    w_up,
    w_down,
    norm_gain,
):
    lat = lax.axis_index("lat")
    place = (lat * lax.axis_size("lon") + lax.axis_index("lon")).astype(jnp.int32).reshape(1)
    slab = encode(
        place,
        obs_count,
        obs_dest.reshape(1, OBS_DEV),
        obs_token.reshape(1, OBS_DEV),
        obs_rows,
        w_obs_in,
        w_obs_out,
    )
    arrived = lax.all_to_all(slab, ("lat", "lon"), split_axis=0, concat_axis=0, tiled=True)
    weights = (w_qkv, w_proj, w_up, w_down)
    mine, below, right, corner = bin_block(arrived, background, norm_gain, *weights)
    below = moved(below, -1, 0)
    right = moved(right, 0, -1)
    corner = moved(corner, -1, -1)
    last = (lat == lax.axis_size("lat") - 1).astype(jnp.int32).reshape(1)
    mine, above, left, corner = shift_block(
        last, mine, below, right, corner, norm_gain, *weights
    )
    above = moved(above, 1, 0)
    left = moved(left, 0, 1)
    corner = moved(corner, 1, 1)
    top = jnp.concatenate([corner, above], 1)
    bottom = jnp.concatenate([left, mine], 1)
    return jnp.concatenate([top, bottom], 0)


def solution(mesh):
    both = P(("lat", "lon"))
    rows = P(("lat", "lon"), None)
    grid = P("lat", "lon", None)
    return jax.shard_map(
        on_device,
        mesh=mesh,
        in_specs=(rows, rows, both, both, grid) + (P(),) * 7,
        out_specs=grid,
        check_vma=False,
    )
```

```python
import jax
import jax.numpy as jnp
from jax import lax
from jax.experimental import pallas as pl
from jax.experimental.pallas import tpu as pltpu
from jax.sharding import PartitionSpec as P

D = 512
FF = 2048
HEADS = 8
WIN = 16
HALF = 8
CLAT = 16
CLON = 32
CELLS = CLAT * CLON
OBS_DEV = 1024
OWNERS = 128
CAP = 16
LANES = 128
SLAB = 4 * CAP + 8
BLK = 256
TILE = 512
ENC_TILE = 1024
PUT = 512
EPS = 1e-5
ENCODE_VMEM = 67043328 - (100 << 10)
BIN_VMEM = (64 << 20) - (16000 << 10)
SHIFT_VMEM = (64 << 20) - (12000 << 10)
BF = jnp.bfloat16
F32 = jnp.float32
VMEM = pl.BlockSpec(memory_space=pltpu.VMEM)
HBM = pl.BlockSpec(memory_space=pltpu.HBM)
SMEM = pl.BlockSpec(memory_space=pltpu.SMEM)


def gelu(v):
    c = 0.7978845608028654
    inner = v * (c + (c * 0.044715) * (v * v))
    half = 0.5 * v
    return half + half * jnp.tanh(inner)


def dot(a, b):
    return jnp.dot(a, b, preferred_element_type=F32)


def dot_nt(a, b):
    return lax.dot_general(a, b, (((1,), (1,)), ((), ())), preferred_element_type=F32)


def normed(x, gain):
    mean = jnp.mean(x, -1, keepdims=True)
    centred = x - mean
    var = jnp.mean(centred * centred, -1, keepdims=True)
    return (centred * lax.rsqrt(var + EPS) * gain).astype(BF)


def iota(shape, axis):
    return lax.broadcasted_iota(jnp.int32, shape, axis)


def encode_kernel(
    place, count, dest, token, rows_hbm, w_in_hbm, w_out_hbm, slab_hbm,
    rows, w_in, w_out, slab, encoded, total, slots, in_sems, out_sems,
):
    tiles = FF // ENC_TILE
    rows_copy = pltpu.make_async_copy(rows_hbm, rows, in_sems.at[2 * tiles])
    w_in_copies = []
    w_out_copies = []
    for t in range(tiles):
        f = slice(t * ENC_TILE, (t + 1) * ENC_TILE)
        w_in_copies.append(pltpu.make_async_copy(w_in_hbm.at[:, f], w_in.at[:, f], in_sems.at[t]))
        w_out_copies.append(
            pltpu.make_async_copy(w_out_hbm.at[f, :], w_out.at[f, :], in_sems.at[tiles + t])
        )
    rows_copy.start()
    w_in_copies[0].start()

    live_count = count[0]
    lane_base = (place[0] % 8) * CAP
    before = iota((BLK, BLK), 0) < iota((BLK, BLK), 1)
    upper = jnp.where(before, 1.0, 0.0).astype(BF)
    owner_col = iota((OWNERS, BLK), 0)
    lane_col = iota((LANES, BLK), 0)
    carry = jnp.zeros((OWNERS, 1), F32)
    high = jnp.zeros((OWNERS, LANES), F32)
    low = jnp.zeros((OWNERS, LANES), F32)
    for b in range(OBS_DEV // BLK):
        cols = slice(b * BLK, (b + 1) * BLK)
        target = dest[:, cols]
        live = (iota((1, BLK), 1) + b * BLK) < live_count
        hits = jnp.where((owner_col == target) & live, 1.0, 0.0)
        hits_bf = hits.astype(BF)
        earlier = dot(hits_bf, upper) + carry
        carry = carry + jnp.sum(hits, 1, keepdims=True)
        rank = jnp.sum(earlier * hits, 0, keepdims=True).astype(jnp.int32)
        slots[:, cols] = jnp.where(live, target * CAP + rank, -1)
        cell = token[:, cols]
        spread = lane_col == (rank + lane_base)
        row_part = jnp.where(spread, (cell // CLON).astype(F32), 0.0).astype(BF)
        col_part = jnp.where(spread, (cell % CLON + 1).astype(F32), 0.0).astype(BF)
        high = high + dot_nt(hits_bf, row_part)
        low = low + dot_nt(hits_bf, col_part)
    sub = iota((OWNERS, 8, LANES), 1)
    marks = jnp.where(sub == 0, high[:, None, :], jnp.where(sub == 1, low[:, None, :], 0.0))
    slab[:, 4 * CAP : SLAB, :] = marks.astype(BF)
    rows_copy.wait()
    for t in range(tiles):
        w_in_copies[t].wait()
        if t == 0:
            w_out_copies[0].start()
        if t + 1 < tiles:
            w_in_copies[t + 1].start()
        f = slice(t * ENC_TILE, (t + 1) * ENC_TILE)

        hidden = gelu(dot(rows[...], w_in[:, f])).astype(BF)
        w_out_copies[t].wait()
        if t + 1 < tiles:
            w_out_copies[t + 1].start()
        part = dot(hidden, w_out[f, :])
        if t > 0:
            part = total[...] + part
        if t + 1 < tiles:
            total[...] = part
        else:
            encoded[...] = part.astype(BF)
    step = PUT // CAP

    def slab_copy(b):
        d = pl.ds(b * step, step)
        return pltpu.make_async_copy(slab.at[d], slab_hbm.at[d], out_sems.at[b])

    def place_block(b, _):
        wanted = iota((PUT, OBS_DEV), 0) + b * PUT
        pick = jnp.where(slots[...] == wanted, 1.0, 0.0).astype(BF)
        moved = dot(pick, encoded[...]).astype(BF).reshape(step, CAP, D)
        d = pl.ds(b * step, step)
        for k in range(4):
            slab[d, k * CAP : (k + 1) * CAP, :] = moved[:, :, k * LANES : (k + 1) * LANES]
        slab_copy(b).start()
        return 0

    lax.fori_loop(0, OWNERS // step, place_block, 0)
    for b in range(OWNERS // step):
        slab_copy(b).wait()


def encode(place, count, dest, token, rows, w_in, w_out):
    return pl.pallas_call(
        encode_kernel,
        out_shape=jax.ShapeDtypeStruct((OWNERS, SLAB, LANES), BF),
        in_specs=[SMEM, SMEM, VMEM, VMEM, HBM, HBM, HBM],
        out_specs=HBM,
        scratch_shapes=[
            pltpu.VMEM((OBS_DEV, D), BF),
            pltpu.VMEM((D, FF), BF),
            pltpu.VMEM((FF, D), BF),
            pltpu.VMEM((OWNERS, SLAB, LANES), BF),
            pltpu.VMEM((OBS_DEV, D), BF),
            pltpu.VMEM((OBS_DEV, D), F32),
            pltpu.VMEM((1, OBS_DEV), jnp.int32),
            pltpu.SemaphoreType.DMA((2 * FF // ENC_TILE + 1,)),
            pltpu.SemaphoreType.DMA((OWNERS * CAP // PUT,)),
        ],
        compiler_params=pltpu.CompilerParams(vmem_limit_bytes=ENCODE_VMEM),
        cost_estimate=pl.CostEstimate(
            flops=7 << 30, transcendentals=OBS_DEV * FF, bytes_accessed=8 << 20
        ),
        name="encode",
    )(place, count, dest, token, rows, w_in, w_out)


def weight_copies(layer, hbm, vmem, sems):
    w_qkv, w_proj, w_up, w_down = hbm
    v_qkv, v_proj, v_up, v_down = vmem
    pairs = [(w_qkv.at[layer], v_qkv), (w_proj.at[layer], v_proj)]
    for t in range(FF // TILE):
        f = slice(t * TILE, (t + 1) * TILE)
        pairs.append((w_up.at[layer, :, f], v_up.at[:, f]))
        pairs.append((w_down.at[layer, f, :], v_down.at[f, :]))
    return [pltpu.make_async_copy(a, b, sems.at[i]) for i, (a, b) in enumerate(pairs)]


def block_body(layer, x, bias, gains, weights, copies, qkv, mixed):
    w_qkv, w_proj, w_up, w_down = weights
    count = x.shape[0]
    area = WIN * WIN
    h = normed(x, gains[layer, 0:1, :])
    copies[0].wait()
    for copy in copies[1:]:
        copy.start()
    qkv[...] = dot(h, w_qkv[...]).astype(BF)
    first = iota((area, LANES), 1) < 64
    ones = jnp.ones((area, LANES), BF)
    for w in range(count // area):
        r = slice(w * area, (w + 1) * area)
        for pair in range(HEADS // 2):
            c = pair * LANES
            q = qkv[r, c : c + LANES] * BF(0.125)
            k = qkv[r, D + c : D + c + LANES]
            v = jnp.concatenate([qkv[r, 2 * D + c : 2 * D + c + LANES], ones], 1)
            out = []
            for head in range(2):
                mine = first if head == 0 else jnp.logical_not(first)
                scores = dot_nt(jnp.where(mine, q, BF(0)), k)
                if bias is not None:
                    scores = scores + bias[w]
                probs = jnp.exp(scores - jnp.max(scores, -1, keepdims=True)).astype(BF)
                both = dot(probs, v)
                out.append(both[:, :LANES] / both[:, LANES:])
            mixed[r, c : c + LANES] = jnp.where(first, out[0], out[1]).astype(BF)
    copies[1].wait()
    attended = x + dot(mixed[...], w_proj[...])
    h = normed(attended, gains[layer, 1:2, :])
    total = attended
    for t in range(FF // TILE):
        copies[2 * t + 2].wait()
        copies[2 * t + 3].wait()
        f = slice(t * TILE, (t + 1) * TILE)
        total = total + dot(gelu(dot(h, w_up[:, f])).astype(BF), w_down[f, :])
    return total.astype(BF)


def bin_kernel(
    arrived, background, gains, wq, wp, wu, wd,
    mid, edge, to_up, to_down, to_down_left, to_left,
    lined, pick, vq, vp, vu, vd, qkv, mixed, state, sems,
):
    copies = weight_copies(0, (wq, wp, wu, wd), (vq, vp, vu, vd), sems)
    copies[0].start()
    for k in range(4):
        lined[:, k * LANES : (k + 1) * LANES] = arrived[:, k * CAP : (k + 1) * CAP, :].reshape(
            OWNERS * CAP, LANES
        )
    sub = iota((OWNERS, 8, LANES), 1)
    weight = jnp.where(sub == 0, float(CLON), 1.0)
    marks = arrived[:, 4 * CAP : SLAB, :].astype(F32) * weight
    marks = jnp.sum(marks.reshape(OWNERS // 8, 64, LANES), 1).astype(jnp.int32)
    row = iota((CELLS, LANES), 0)
    inner = row % BLK
    cell = (inner // WIN) * CLON + (row // BLK) * WIN + inner % WIN + 1
    tally = jnp.zeros((CELLS, LANES), F32)
    for g in range(OWNERS // 8):
        hit = jnp.where(cell == marks[g : g + 1, :], 1.0, 0.0)
        tally = tally + hit
        pick[:, g * LANES : (g + 1) * LANES] = hit.astype(BF)
    tally = jnp.sum(tally, 1, keepdims=True)
    sums = dot(pick[...], lined[...]) / jnp.maximum(tally, 1.0)
    for w in range(2):
        r = slice(w * BLK, (w + 1) * BLK)
        back = background[:, w * WIN : (w + 1) * WIN, :].astype(F32).reshape(BLK, D)
        state[r, :] = (back + sums[r, :]).astype(BF).astype(F32)
    done = block_body(0, state[...], None, gains, (vq, vp, vu, vd), copies, qkv, mixed)
    one = done[:BLK].reshape(WIN, WIN, D)
    two = done[BLK:].reshape(WIN, WIN, D)
    mid[:, :HALF, :] = one[HALF:, HALF:]
    mid[:, HALF:, :] = two[HALF:, :HALF]
    edge[...] = two[:HALF, HALF:]
    to_up[:, :HALF, :] = one[:HALF, HALF:]
    to_up[:, HALF:, :] = two[:HALF, :HALF]
    to_down[...] = two[HALF:, HALF:]
    to_down_left[...] = one[HALF:, :HALF]
    to_left[...] = one[:HALF, :HALF]


WEIGHT_SCRATCH = [
    pltpu.VMEM((D, 3 * D), BF),
    pltpu.VMEM((D, D), BF),
    pltpu.VMEM((D, FF), BF),
    pltpu.VMEM((FF, D), BF),
]
WEIGHT_SEMS = pltpu.SemaphoreType.DMA((2 + 2 * FF // TILE,))
BLOCK_SCRATCH = [
    pltpu.VMEM((CELLS, 3 * D), BF),
    pltpu.VMEM((CELLS, D), BF),
    pltpu.VMEM((CELLS, D), F32),
]
BLOCK_COST = pl.CostEstimate(flops=4 << 30, transcendentals=2 << 20, bytes_accessed=8 << 20)
WIDE = jax.ShapeDtypeStruct((HALF, WIN, D), BF)
NARROW = jax.ShapeDtypeStruct((HALF, HALF, D), BF)
PIECES = (WIDE, NARROW, WIDE, NARROW, NARROW, NARROW)


def bin_block(arrived, background, gains, *weights):
    return pl.pallas_call(
        bin_kernel,
        out_shape=PIECES,
        in_specs=[VMEM] * 3 + [HBM] * 4,
        out_specs=[VMEM] * 6,
        scratch_shapes=[
            pltpu.VMEM((OWNERS * CAP, D), BF),
            pltpu.VMEM((CELLS, OWNERS * CAP), BF),
        ]
        + WEIGHT_SCRATCH
        + BLOCK_SCRATCH
        + [WEIGHT_SEMS],
        compiler_params=pltpu.CompilerParams(vmem_limit_bytes=BIN_VMEM),
        cost_estimate=BLOCK_COST,
        name="bin_block",
    )(arrived, background, gains, *weights)


def shift_kernel(
    ends, mid, edge, below, above, above_right, right, gains, wq, wp, wu, wd,
    own_mid, own_edge, to_down, to_up, to_up_right, to_right,
    vq, vp, vu, vd, qkv, mixed, state, bias, sems,
):
    copies = weight_copies(1, (wq, wp, wu, wd), (vq, vp, vu, vd), sems)
    copies[0].start()
    area = WIN * WIN
    h = area // 2
    split = (iota((area, area), 0) < h) != (iota((area, area), 1) < h)
    for w in range(2):
        bias[w] = jnp.where(split & (ends[0] == w + 1), -1e30, 0.0)
    state[0:h, :] = mid[...].astype(F32).reshape(h, D)
    state[h : 2 * h, :] = below[...].astype(F32).reshape(h, D)
    top = jnp.concatenate([above[...].astype(F32), above_right[...].astype(F32)], 1)
    bottom = jnp.concatenate([edge[...].astype(F32), right[...].astype(F32)], 1)
    state[2 * h : 3 * h, :] = top.reshape(h, D)
    state[3 * h : 4 * h, :] = bottom.reshape(h, D)
    done = block_body(1, state[...], bias, gains, (vq, vp, vu, vd), copies, qkv, mixed)
    one = done[:BLK].reshape(WIN, WIN, D)
    two = done[BLK:].reshape(WIN, WIN, D)
    own_mid[...] = one[:HALF]
    own_edge[...] = two[HALF:, :HALF]
    to_down[...] = one[HALF:]
    to_up[...] = two[:HALF, :HALF]
    to_up_right[...] = two[:HALF, HALF:]
    to_right[...] = two[HALF:, HALF:]


def shift_block(ends, pieces, gains, *weights):
    return pl.pallas_call(
        shift_kernel,
        out_shape=PIECES,
        in_specs=[SMEM] + [VMEM] * 7 + [HBM] * 4,
        out_specs=[VMEM] * 6,
        scratch_shapes=WEIGHT_SCRATCH
        + BLOCK_SCRATCH
        + [pltpu.VMEM((2, WIN * WIN, WIN * WIN), F32), WEIGHT_SEMS],
        compiler_params=pltpu.CompilerParams(vmem_limit_bytes=SHIFT_VMEM),
        cost_estimate=BLOCK_COST,
        name="shift_block",
    )(ends, *pieces, gains, *weights)


def moved(block, lat_step, lon_step):
    lat_count = lax.axis_size("lat")
    lon_count = lax.axis_size("lon")
    route = [
        (
            i * lon_count + j,
            (i + lat_step) % lat_count * lon_count + (j + lon_step) % lon_count,
        )
        for i in range(lat_count)
        for j in range(lon_count)
    ]
    return lax.ppermute(block, ("lat", "lon"), route)


def on_device(
    obs_rows,
    obs_dest,
    obs_token,
    obs_count,
    background,
    w_obs_in,
    w_obs_out,
    w_qkv,
    w_proj,
    w_up,
    w_down,
    norm_gain,
):
    lat = lax.axis_index("lat")
    place = (lat * lax.axis_size("lon") + lax.axis_index("lon")).astype(jnp.int32).reshape(1)
    slab = encode(
        place,
        obs_count,
        obs_dest.reshape(1, OBS_DEV),
        obs_token.reshape(1, OBS_DEV),
        obs_rows,
        w_obs_in,
        w_obs_out,
    )
    arrived = lax.all_to_all(slab, ("lat", "lon"), split_axis=0, concat_axis=0, tiled=True)
    weights = (w_qkv, w_proj, w_up, w_down)
    mid, edge, up, down, down_left, left = bin_block(arrived, background, norm_gain, *weights)
    below = moved(up, -1, 0)
    above = moved(down, 1, 0)
    above_right = moved(down_left, 1, -1)
    right = moved(left, 0, -1)
    ends = jnp.where(lat == lax.axis_size("lat") - 1, 1, jnp.where(lat == 0, 2, 0))
    ends = ends.astype(jnp.int32).reshape(1)
    mid, edge, down, up, up_right, right = shift_block(
        ends, (mid, edge, below, above, above_right, right), norm_gain, *weights
    )
    above = moved(down, 1, 0)
    below = moved(up, -1, 0)
    below_left = moved(up_right, -1, 1)
    left = moved(right, 0, 1)
    top = jnp.concatenate([left, above, edge], 1)
    bottom = jnp.concatenate([below_left, mid, below], 1)
    return jnp.concatenate([top, bottom], 0)


def solution(mesh):
    both = P(("lat", "lon"))
    rows = P(("lat", "lon"), None)
    grid = P("lat", "lon", None)
    return jax.shard_map(
        on_device,
        mesh=mesh,
        in_specs=(rows, rows, both, both, grid) + (P(),) * 7,
        out_specs=grid,
        check_vma=False,
    )
```

```python
import jax
import jax.numpy as jnp
from jax import lax
from jax.experimental import pallas as pl
from jax.experimental.pallas import tpu as pltpu
from jax.sharding import PartitionSpec as P

D = 512
FF = 2048
HEADS = 8
WIN = 16
HALF = 8
CLAT = 16
CLON = 32
CELLS = CLAT * CLON
OBS_DEV = 1024
OWNERS = 128
CAP = 16
LANES = 128
SLAB = 4 * CAP + 8
BLK = 256
TILE = 1024
ENC_TILES = (1024, 1024)
AHEAD = 5
ENC = 1024
PUT = 1024
EPS = 1e-5
ENCODE_VMEM = 67043328 - (100 << 10)
BIN_VMEM = (64 << 20) - (16000 << 10)
SHIFT_VMEM = 16 << 20
FETCH_VMEM = (64 << 20) - (18500 << 10)
BF = jnp.bfloat16
F32 = jnp.float32
VMEM = pl.BlockSpec(memory_space=pltpu.VMEM)
HBM = pl.BlockSpec(memory_space=pltpu.HBM)
SMEM = pl.BlockSpec(memory_space=pltpu.SMEM)


def gelu(v):
    c = 0.7978845608028654
    inner = v * (c + (c * 0.044715) * (v * v))
    half = 0.5 * v
    return half + half * jnp.tanh(inner)


def dot(a, b):
    return jnp.dot(a, b, preferred_element_type=F32)


def dot_nt(a, b):
    return lax.dot_general(a, b, (((1,), (1,)), ((), ())), preferred_element_type=F32)


def normed(x, gain):
    mean = jnp.mean(x, -1, keepdims=True)
    centred = x - mean
    var = jnp.mean(centred * centred, -1, keepdims=True)
    return (centred * lax.rsqrt(var + EPS) * gain).astype(BF)


def iota(shape, axis):
    return lax.broadcasted_iota(jnp.int32, shape, axis)


def encode_kernel(
    place, count, dest, token, rows_hbm, w_in_hbm, w_out_hbm, slab_hbm,
    rows, w_in, w_out, slab, encoded, total, slots, in_sems, out_sems,
):
    copies = [pltpu.make_async_copy(rows_hbm, rows, in_sems.at[0])]
    spans = []
    for t, width in enumerate(ENC_TILES):
        f = slice(sum(ENC_TILES[:t]), sum(ENC_TILES[: t + 1]))
        spans.append(f)
        copies.append(pltpu.make_async_copy(w_in_hbm.at[:, f], w_in.at[:, f], in_sems.at[2 * t + 1]))
        copies.append(pltpu.make_async_copy(w_out_hbm.at[f, :], w_out.at[f, :], in_sems.at[2 * t + 2]))
    for copy in copies[:AHEAD]:
        copy.start()

    def arrive(i):
        copies[i].wait()
        if i + AHEAD < len(copies):
            copies[i + AHEAD].start()

    live_count = count[0]
    lane_base = (place[0] % 8) * CAP
    before = iota((BLK, BLK), 0) < iota((BLK, BLK), 1)
    upper = jnp.where(before, 1.0, 0.0).astype(BF)
    owner_col = iota((OWNERS, BLK), 0)
    lane_col = iota((LANES, BLK), 0)
    carry = jnp.zeros((OWNERS, 1), F32)
    high = jnp.zeros((OWNERS, LANES), F32)
    low = jnp.zeros((OWNERS, LANES), F32)
    for b in range(OBS_DEV // BLK):
        cols = slice(b * BLK, (b + 1) * BLK)
        target = dest[:, cols]
        live = (iota((1, BLK), 1) + b * BLK) < live_count
        hits = jnp.where((owner_col == target) & live, 1.0, 0.0)
        hits_bf = hits.astype(BF)
        earlier = dot(hits_bf, upper) + carry
        carry = carry + jnp.sum(hits, 1, keepdims=True)
        rank = jnp.sum(earlier * hits, 0, keepdims=True).astype(jnp.int32)
        slots[:, cols] = jnp.where(live, target * CAP + rank, -1)
        cell = token[:, cols]
        spread = lane_col == (rank + lane_base)
        row_part = jnp.where(spread, (cell // CLON).astype(F32), 0.0).astype(BF)
        col_part = jnp.where(spread, (cell % CLON + 1).astype(F32), 0.0).astype(BF)
        high = high + dot_nt(hits_bf, row_part)
        low = low + dot_nt(hits_bf, col_part)
    sub = iota((OWNERS, 8, LANES), 1)
    marks = jnp.where(sub == 0, high[:, None, :], jnp.where(sub == 1, low[:, None, :], 0.0))
    slab[:, 4 * CAP : SLAB, :] = marks.astype(BF)
    arrive(0)
    for t, f in enumerate(spans):
        arrive(2 * t + 1)
        arrive(2 * t + 2)

        def encode_block(b, _):
            r = pl.ds(pl.multiple_of(b * ENC, ENC), ENC)
            hidden = gelu(dot(rows[r, :], w_in[:, f])).astype(BF)
            part = dot(hidden, w_out[f, :])
            if t > 0:
                part = total[r, :] + part
            if t + 1 < len(spans):
                total[r, :] = part
            else:
                encoded[r, :] = part.astype(BF)
            return 0

        lax.fori_loop(0, OBS_DEV // ENC, encode_block, 0)
    step = PUT // CAP

    def slab_copy(b):
        d = pl.ds(b * step, step)
        return pltpu.make_async_copy(slab.at[d], slab_hbm.at[d], out_sems.at[b])

    def place_block(b, _):
        wanted = iota((PUT, OBS_DEV), 0) + b * PUT
        pick = jnp.where(slots[...] == wanted, 1.0, 0.0).astype(BF)
        moved = dot(pick, encoded[...]).astype(BF).reshape(step, CAP, D)
        d = pl.ds(b * step, step)
        for k in range(4):
            slab[d, k * CAP : (k + 1) * CAP, :] = moved[:, :, k * LANES : (k + 1) * LANES]
        slab_copy(b).start()
        return 0

    lax.fori_loop(0, OWNERS // step, place_block, 0)
    for b in range(OWNERS // step):
        slab_copy(b).wait()


def encode(place, count, dest, token, rows, w_in, w_out):
    return pl.pallas_call(
        encode_kernel,
        out_shape=jax.ShapeDtypeStruct((OWNERS, SLAB, LANES), BF),
        in_specs=[SMEM, SMEM, VMEM, VMEM, HBM, HBM, HBM],
        out_specs=HBM,
        scratch_shapes=[
            pltpu.VMEM((OBS_DEV, D), BF),
            pltpu.VMEM((D, FF), BF),
            pltpu.VMEM((FF, D), BF),
            pltpu.VMEM((OWNERS, SLAB, LANES), BF),
            pltpu.VMEM((OBS_DEV, D), BF),
            pltpu.VMEM((OBS_DEV, D), F32),
            pltpu.VMEM((1, OBS_DEV), jnp.int32),
            pltpu.SemaphoreType.DMA((2 * len(ENC_TILES) + 1,)),
            pltpu.SemaphoreType.DMA((OWNERS * CAP // PUT,)),
        ],
        compiler_params=pltpu.CompilerParams(vmem_limit_bytes=ENCODE_VMEM),
        cost_estimate=pl.CostEstimate(
            flops=7 << 30, transcendentals=OBS_DEV * FF, bytes_accessed=8 << 20
        ),
        name="encode",
    )(place, count, dest, token, rows, w_in, w_out)


def weight_copies(layer, hbm, vmem, sems):
    w_qkv, w_proj, w_up, w_down = hbm
    v_qkv, v_proj, v_up, v_down = vmem
    pairs = []
    for part in range(3):
        c = slice(part * D, (part + 1) * D)
        pairs.append((w_qkv.at[layer, :, c], v_qkv.at[:, c]))
    pairs.append((w_proj.at[layer], v_proj))
    for t in range(FF // TILE):
        f = slice(t * TILE, (t + 1) * TILE)
        pairs.append((w_up.at[layer, :, f], v_up.at[:, f]))
        pairs.append((w_down.at[layer, f, :], v_down.at[f, :]))
    return [pltpu.make_async_copy(a, b, sems.at[i]) for i, (a, b) in enumerate(pairs)]


def fetch_kernel(after, wq, wp, wu, wd, vq, vp, vu, vd, sems):
    copies = []
    for i, (a, b) in enumerate(((wq, vq), (wp, vp), (wu, vu), (wd, vd))):
        copies.append(pltpu.make_async_copy(a.at[1], b, sems.at[i]))
        copies[-1].start()
    for copy in copies:
        copy.wait()


def fetch(after, *arrays):
    size = sum(a.size * a.dtype.itemsize for a in arrays)
    return pl.pallas_call(
        fetch_kernel,
        out_shape=[jax.ShapeDtypeStruct(a.shape[1:], a.dtype) for a in arrays],
        in_specs=[HBM] * 5,
        out_specs=[VMEM] * 4,
        scratch_shapes=[pltpu.SemaphoreType.DMA((4,))],
        compiler_params=pltpu.CompilerParams(vmem_limit_bytes=FETCH_VMEM),
        cost_estimate=pl.CostEstimate(flops=0, transcendentals=0, bytes_accessed=2 * size),
        name="fetch",
    )(after, *arrays)


def block_body(layer, x, bias, gains, weights, copies, qkv, mixed):
    w_qkv, w_proj, w_up, w_down = weights
    count = x.shape[0]
    area = WIN * WIN
    h = normed(x, gains[layer, 0:1, :])
    for part in range(3):
        c = slice(part * D, (part + 1) * D)
        if copies:
            copies[part].wait()
            copies[part + 3].start()
        qkv[:, c] = dot(h, w_qkv[:, c]).astype(BF)
    for copy in copies[6:]:
        copy.start()
    first = iota((area, LANES), 1) < 64
    ones = jnp.ones((area, LANES), BF)
    for w in range(count // area):
        r = slice(w * area, (w + 1) * area)
        for pair in range(HEADS // 2):
            c = pair * LANES
            q = qkv[r, c : c + LANES] * BF(0.125)
            k = qkv[r, D + c : D + c + LANES]
            v = jnp.concatenate([qkv[r, 2 * D + c : 2 * D + c + LANES], ones], 1)
            out = []
            for head in range(2):
                mine = first if head == 0 else jnp.logical_not(first)
                scores = dot_nt(jnp.where(mine, q, BF(0)), k)
                if bias is not None:
                    scores = scores + bias
                probs = jnp.exp(scores - jnp.max(scores, -1, keepdims=True)).astype(BF)
                both = dot(probs, v)
                out.append(both[:, :LANES] / both[:, LANES:])
            mixed[r, c : c + LANES] = jnp.where(first, out[0], out[1]).astype(BF)
    if copies:
        copies[3].wait()
    attended = x + dot(mixed[...], w_proj[...])
    h = normed(attended, gains[layer, 1:2, :])
    total = attended
    for t in range(FF // TILE):
        if copies:
            copies[2 * t + 4].wait()
            copies[2 * t + 5].wait()
        f = slice(t * TILE, (t + 1) * TILE)
        total = total + dot(gelu(dot(h, w_up[:, f])).astype(BF), w_down[f, :])
    return total.astype(BF)


def bin_kernel(
    arrived, background, gains, wq, wp, wu, wd,
    keep, below, right, corner,
    lined, pick, vq, vp, vu, vd, qkv, mixed, state, sems,
):
    copies = weight_copies(0, (wq, wp, wu, wd), (vq, vp, vu, vd), sems)
    for copy in copies[:3]:
        copy.start()
    for k in range(4):
        lined[:, k * LANES : (k + 1) * LANES] = arrived[:, k * CAP : (k + 1) * CAP, :].reshape(
            OWNERS * CAP, LANES
        )
    sub = iota((OWNERS, 8, LANES), 1)
    weight = jnp.where(sub == 0, float(CLON), 1.0)
    marks = arrived[:, 4 * CAP : SLAB, :].astype(F32) * weight
    marks = jnp.sum(marks.reshape(OWNERS // 8, 64, LANES), 1).astype(jnp.int32)
    row = iota((CELLS, LANES), 0)
    inner = row % BLK
    cell = (inner // WIN) * CLON + (row // BLK) * WIN + inner % WIN + 1
    tally = jnp.zeros((CELLS, LANES), F32)
    for g in range(OWNERS // 8):
        hit = jnp.where(cell == marks[g : g + 1, :], 1.0, 0.0)
        tally = tally + hit
        pick[:, g * LANES : (g + 1) * LANES] = hit.astype(BF)
    tally = jnp.sum(tally, 1, keepdims=True)
    sums = dot(pick[...], lined[...]) / jnp.maximum(tally, 1.0)
    for w in range(2):
        r = slice(w * BLK, (w + 1) * BLK)
        back = background[:, w * WIN : (w + 1) * WIN, :].astype(F32).reshape(BLK, D)
        state[r, :] = (back + sums[r, :]).astype(BF).astype(F32)
    done = block_body(0, state[...], None, gains, (vq, vp, vu, vd), copies, qkv, mixed)
    one = done[:BLK].reshape(WIN, WIN, D)
    two = done[BLK:].reshape(WIN, WIN, D)
    corner[...] = one[:HALF, :HALF]
    right[...] = one[HALF:, :HALF]
    below[:, :HALF, :] = one[:HALF, HALF:]
    below[:, HALF:, :] = two[:HALF]
    keep[:, :HALF, :] = one[HALF:, HALF:]
    keep[:, HALF:, :] = two[HALF:]


WEIGHT_SCRATCH = [
    pltpu.VMEM((D, 3 * D), BF),
    pltpu.VMEM((D, D), BF),
    pltpu.VMEM((D, FF), BF),
    pltpu.VMEM((FF, D), BF),
]
WEIGHT_SEMS = pltpu.SemaphoreType.DMA((4 + 2 * FF // TILE,))
BLOCK_SCRATCH = [
    pltpu.VMEM((CELLS, 3 * D), BF),
    pltpu.VMEM((CELLS, D), BF),
    pltpu.VMEM((CELLS, D), F32),
]
BLOCK_COST = pl.CostEstimate(flops=4 << 30, transcendentals=2 << 20, bytes_accessed=8 << 20)
WIDE = jax.ShapeDtypeStruct((HALF, CLON - HALF, D), BF)
NARROW = jax.ShapeDtypeStruct((HALF, HALF, D), BF)
PIECES = (WIDE, WIDE, NARROW, NARROW)


def bin_block(arrived, background, gains, *weights):
    return pl.pallas_call(
        bin_kernel,
        out_shape=PIECES,
        in_specs=[VMEM] * 3 + [HBM] * 4,
        out_specs=[VMEM] * 4,
        scratch_shapes=[
            pltpu.VMEM((OWNERS * CAP, D), BF),
            pltpu.VMEM((CELLS, OWNERS * CAP), BF),
        ]
        + WEIGHT_SCRATCH
        + BLOCK_SCRATCH
        + [WEIGHT_SEMS],
        compiler_params=pltpu.CompilerParams(vmem_limit_bytes=BIN_VMEM),
        cost_estimate=BLOCK_COST,
        name="bin_block",
    )(arrived, background, gains, *weights)


def shift_kernel(
    last, mine, below, right, corner, gains, wq, wp, wu, wd,
    keep, above, left, diagonal, qkv, mixed, state, bias,
):
    area = WIN * WIN
    h = area // 2
    split = (iota((area, area), 0) < h) != (iota((area, area), 1) < h)
    bias[...] = jnp.where(split & (last[0] == 1), -1e30, 0.0)
    top = mine[...].astype(F32)
    bottom = below[...].astype(F32)
    state[0:h, :] = top[:, :WIN, :].reshape(h, D)
    state[h : 2 * h, :] = bottom[:, :WIN, :].reshape(h, D)
    top = jnp.concatenate([top[:, WIN:, :], right[...].astype(F32)], 1)
    bottom = jnp.concatenate([bottom[:, WIN:, :], corner[...].astype(F32)], 1)
    state[2 * h : 3 * h, :] = top.reshape(h, D)
    state[3 * h : 4 * h, :] = bottom.reshape(h, D)
    done = block_body(1, state[...], bias[...], gains, (wq, wp, wu, wd), (), qkv, mixed)
    one = done[:BLK].reshape(WIN, WIN, D)
    two = done[BLK:].reshape(WIN, WIN, D)
    diagonal[...] = two[HALF:, HALF:]
    left[...] = two[:HALF, HALF:]
    above[:, :WIN, :] = one[HALF:]
    above[:, WIN:, :] = two[HALF:, :HALF]
    keep[:, :WIN, :] = one[:HALF]
    keep[:, WIN:, :] = two[:HALF, :HALF]


def shift_block(last, pieces, gains, *weights):
    return pl.pallas_call(
        shift_kernel,
        out_shape=PIECES,
        in_specs=[SMEM] + [VMEM] * 9,
        out_specs=[VMEM] * 4,
        scratch_shapes=BLOCK_SCRATCH + [pltpu.VMEM((WIN * WIN, WIN * WIN), F32)],
        compiler_params=pltpu.CompilerParams(vmem_limit_bytes=SHIFT_VMEM),
        cost_estimate=BLOCK_COST,
        name="shift_block",
    )(last, *pieces, gains, *weights)


def moved(block, lat_step, lon_step):
    lat_count = lax.axis_size("lat")
    lon_count = lax.axis_size("lon")
    route = [
        (
            i * lon_count + j,
            (i + lat_step) % lat_count * lon_count + (j + lon_step) % lon_count,
        )
        for i in range(lat_count)
        for j in range(lon_count)
    ]
    return lax.ppermute(block, ("lat", "lon"), route)


def on_device(
    obs_rows,
    obs_dest,
    obs_token,
    obs_count,
    background,
    w_obs_in,
    w_obs_out,
    w_qkv,
    w_proj,
    w_up,
    w_down,
    norm_gain,
):
    lat = lax.axis_index("lat")
    place = (lat * lax.axis_size("lon") + lax.axis_index("lon")).astype(jnp.int32).reshape(1)
    slab = encode(
        place,
        obs_count,
        obs_dest.reshape(1, OBS_DEV),
        obs_token.reshape(1, OBS_DEV),
        obs_rows,
        w_obs_in,
        w_obs_out,
    )
    arrived = lax.all_to_all(slab, ("lat", "lon"), split_axis=0, concat_axis=0, tiled=True)
    weights = (w_qkv, w_proj, w_up, w_down)
    mine, below, right, corner = bin_block(arrived, background, norm_gain, *weights)
    late = fetch(mine, *weights)
    below = moved(below, -1, 0)
    right = moved(right, 0, -1)
    corner = moved(corner, -1, -1)
    last = (lat == lax.axis_size("lat") - 1).astype(jnp.int32).reshape(1)
    mine, above, left, corner = shift_block(last, (mine, below, right, corner), norm_gain, *late)
    above = moved(above, 1, 0)
    left = moved(left, 0, 1)
    corner = moved(corner, 1, 1)
    top = jnp.concatenate([corner, above], 1)
    bottom = jnp.concatenate([left, mine], 1)
    return jnp.concatenate([top, bottom], 0)


def solution(mesh):
    both = P(("lat", "lon"))
    rows = P(("lat", "lon"), None)
    grid = P("lat", "lon", None)
    return jax.shard_map(
        on_device,
        mesh=mesh,
        in_specs=(rows, rows, both, both, grid) + (P(),) * 7,
        out_specs=grid,
        check_vma=False,
    )
```

```python
import jax
import jax.numpy as jnp
from jax import lax
from jax.experimental import pallas as pl
from jax.experimental.pallas import tpu as pltpu
from jax.sharding import PartitionSpec as P

D = 512
FF = 2048
HEADS = 8
WIN = 16
HALF = 8
CLAT = 16
CLON = 32
CELLS = CLAT * CLON
OBS_DEV = 1024
OWNERS = 128
CAP = 16
LANES = 128
SLAB = 4 * CAP + 8
BLK = 256
TILE = 1024
ENC_TILES = (1024, 1024)
AHEAD = 5
ENC = 1024
PUT = 1024
EPS = 1e-5
ENCODE_VMEM = 67043328 - (100 << 10)
BIN_VMEM = (64 << 20) - (16000 << 10)
SHIFT_VMEM = 16 << 20
FETCH_VMEM = (64 << 20) - (18500 << 10)
BF = jnp.bfloat16
F32 = jnp.float32
VMEM = pl.BlockSpec(memory_space=pltpu.VMEM)
HBM = pl.BlockSpec(memory_space=pltpu.HBM)
SMEM = pl.BlockSpec(memory_space=pltpu.SMEM)


def gelu(v):
    c = 0.7978845608028654
    inner = v * (c + (c * 0.044715) * (v * v))
    half = 0.5 * v
    return half + half * jnp.tanh(inner)


def dot(a, b):
    return jnp.dot(a, b, preferred_element_type=F32)


def dot_nt(a, b):
    return lax.dot_general(a, b, (((1,), (1,)), ((), ())), preferred_element_type=F32)


def normed(x, gain):
    mean = jnp.mean(x, -1, keepdims=True)
    centred = x - mean
    var = jnp.mean(centred * centred, -1, keepdims=True)
    return (centred * lax.rsqrt(var + EPS) * gain).astype(BF)


def iota(shape, axis):
    return lax.broadcasted_iota(jnp.int32, shape, axis)


def encode_kernel(
    place, count, dest, token, rows_hbm, w_in_hbm, w_out_hbm, slab_hbm,
    rows, w_in, w_out, slab, encoded, total, slots, in_sems, out_sems,
):
    copies = [pltpu.make_async_copy(rows_hbm, rows, in_sems.at[0])]
    spans = []
    for t, width in enumerate(ENC_TILES):
        f = slice(sum(ENC_TILES[:t]), sum(ENC_TILES[: t + 1]))
        spans.append(f)
        copies.append(pltpu.make_async_copy(w_in_hbm.at[:, f], w_in.at[:, f], in_sems.at[2 * t + 1]))
        copies.append(pltpu.make_async_copy(w_out_hbm.at[f, :], w_out.at[f, :], in_sems.at[2 * t + 2]))
    for copy in copies[:AHEAD]:
        copy.start()

    def arrive(i):
        copies[i].wait()
        if i + AHEAD < len(copies):
            copies[i + AHEAD].start()

    live_count = count[0]
    lane_base = (place[0] % 8) * CAP
    before = iota((BLK, BLK), 0) < iota((BLK, BLK), 1)
    upper = jnp.where(before, 1.0, 0.0).astype(BF)
    owner_col = iota((OWNERS, BLK), 0)
    lane_col = iota((LANES, BLK), 0)
    carry = jnp.zeros((OWNERS, 1), F32)
    high = jnp.zeros((OWNERS, LANES), F32)
    low = jnp.zeros((OWNERS, LANES), F32)
    for b in range(OBS_DEV // BLK):
        cols = slice(b * BLK, (b + 1) * BLK)
        target = dest[:, cols]
        live = (iota((1, BLK), 1) + b * BLK) < live_count
        hits = jnp.where((owner_col == target) & live, 1.0, 0.0)
        hits_bf = hits.astype(BF)
        earlier = dot(hits_bf, upper) + carry
        carry = carry + jnp.sum(hits, 1, keepdims=True)
        rank = jnp.sum(earlier * hits, 0, keepdims=True).astype(jnp.int32)
        slots[:, cols] = jnp.where(live, target * CAP + rank, -1)
        cell = token[:, cols]
        spread = lane_col == (rank + lane_base)
        row_part = jnp.where(spread, (cell // CLON).astype(F32), 0.0).astype(BF)
        col_part = jnp.where(spread, (cell % CLON + 1).astype(F32), 0.0).astype(BF)
        high = high + dot_nt(hits_bf, row_part)
        low = low + dot_nt(hits_bf, col_part)
    sub = iota((OWNERS, 8, LANES), 1)
    marks = jnp.where(sub == 0, high[:, None, :], jnp.where(sub == 1, low[:, None, :], 0.0))
    slab[:, 4 * CAP : SLAB, :] = marks.astype(BF)
    arrive(0)
    for t, f in enumerate(spans):
        arrive(2 * t + 1)
        arrive(2 * t + 2)

        def encode_block(b, _):
            r = pl.ds(pl.multiple_of(b * ENC, ENC), ENC)
            hidden = gelu(dot(rows[r, :], w_in[:, f])).astype(BF)
            part = dot(hidden, w_out[f, :])
            if t > 0:
                part = total[r, :] + part
            if t + 1 < len(spans):
                total[r, :] = part
            else:
                encoded[r, :] = part.astype(BF)
            return 0

        lax.fori_loop(0, OBS_DEV // ENC, encode_block, 0)
    step = PUT // CAP

    def slab_copy(b):
        d = pl.ds(b * step, step)
        return pltpu.make_async_copy(slab.at[d], slab_hbm.at[d], out_sems.at[b])

    def place_block(b, _):
        wanted = iota((PUT, OBS_DEV), 0) + b * PUT
        pick = jnp.where(slots[...] == wanted, 1.0, 0.0).astype(BF)
        moved = dot(pick, encoded[...]).astype(BF).reshape(step, CAP, D)
        d = pl.ds(b * step, step)
        for k in range(4):
            slab[d, k * CAP : (k + 1) * CAP, :] = moved[:, :, k * LANES : (k + 1) * LANES]
        slab_copy(b).start()
        return 0

    lax.fori_loop(0, OWNERS // step, place_block, 0)
    for b in range(OWNERS // step):
        slab_copy(b).wait()


def encode(place, count, dest, token, rows, w_in, w_out):
    return pl.pallas_call(
        encode_kernel,
        out_shape=jax.ShapeDtypeStruct((OWNERS, SLAB, LANES), BF),
        in_specs=[SMEM, SMEM, VMEM, VMEM, HBM, HBM, HBM],
        out_specs=HBM,
        scratch_shapes=[
            pltpu.VMEM((OBS_DEV, D), BF),
            pltpu.VMEM((D, FF), BF),
            pltpu.VMEM((FF, D), BF),
            pltpu.VMEM((OWNERS, SLAB, LANES), BF),
            pltpu.VMEM((OBS_DEV, D), BF),
            pltpu.VMEM((OBS_DEV, D), F32),
            pltpu.VMEM((1, OBS_DEV), jnp.int32),
            pltpu.SemaphoreType.DMA((2 * len(ENC_TILES) + 1,)),
            pltpu.SemaphoreType.DMA((OWNERS * CAP // PUT,)),
        ],
        compiler_params=pltpu.CompilerParams(vmem_limit_bytes=ENCODE_VMEM),
        cost_estimate=pl.CostEstimate(
            flops=7 << 30, transcendentals=OBS_DEV * FF, bytes_accessed=8 << 20
        ),
        name="encode",
    )(place, count, dest, token, rows, w_in, w_out)


def weight_copies(layer, hbm, vmem, sems):
    w_qkv, w_proj, w_up, w_down = hbm
    v_qkv, v_proj, v_up, v_down = vmem
    pairs = []
    for part in range(3):
        c = slice(part * D, (part + 1) * D)
        pairs.append((w_qkv.at[layer, :, c], v_qkv.at[:, c]))
    pairs.append((w_proj.at[layer], v_proj))
    for t in range(FF // TILE):
        f = slice(t * TILE, (t + 1) * TILE)
        pairs.append((w_up.at[layer, :, f], v_up.at[:, f]))
        pairs.append((w_down.at[layer, f, :], v_down.at[f, :]))
    return [pltpu.make_async_copy(a, b, sems.at[i]) for i, (a, b) in enumerate(pairs)]


def fetch_kernel(after, wq, wp, wu, wd, vq, vp, vu, vd, sems):
    copies = []
    for i, (a, b) in enumerate(((wq, vq), (wp, vp), (wu, vu), (wd, vd))):
        copies.append(pltpu.make_async_copy(a.at[1], b, sems.at[i]))
        copies[-1].start()
    for copy in copies:
        copy.wait()


def fetch(after, *arrays):
    size = sum(a.size * a.dtype.itemsize for a in arrays)
    return pl.pallas_call(
        fetch_kernel,
        out_shape=[jax.ShapeDtypeStruct(a.shape[1:], a.dtype) for a in arrays],
        in_specs=[HBM] * 5,
        out_specs=[VMEM] * 4,
        scratch_shapes=[pltpu.SemaphoreType.DMA((4,))],
        compiler_params=pltpu.CompilerParams(vmem_limit_bytes=FETCH_VMEM),
        cost_estimate=pl.CostEstimate(flops=0, transcendentals=0, bytes_accessed=2 * size),
        name="fetch",
    )(after, *arrays)


def block_body(layer, x, bias, gains, weights, copies, qkv, mixed):
    w_qkv, w_proj, w_up, w_down = weights
    count = x.shape[0]
    area = WIN * WIN
    h = normed(x, gains[layer, 0:1, :])
    for part in range(3):
        c = slice(part * D, (part + 1) * D)
        if copies:
            copies[part].wait()
        qkv[:, c] = dot(h, w_qkv[:, c]).astype(BF)
    first = iota((area, LANES), 1) < 64
    ones = jnp.ones((area, LANES), BF)
    for w in range(count // area):
        r = slice(w * area, (w + 1) * area)
        for pair in range(HEADS // 2):
            c = pair * LANES
            q = qkv[r, c : c + LANES] * BF(0.125)
            k = qkv[r, D + c : D + c + LANES]
            v = jnp.concatenate([qkv[r, 2 * D + c : 2 * D + c + LANES], ones], 1)
            out = []
            for head in range(2):
                mine = first if head == 0 else jnp.logical_not(first)
                scores = dot_nt(jnp.where(mine, q, BF(0)), k)
                if bias is not None:
                    scores = scores + bias
                probs = jnp.exp(scores - jnp.max(scores, -1, keepdims=True)).astype(BF)
                both = dot(probs, v)
                out.append(both[:, :LANES] / both[:, LANES:])
            mixed[r, c : c + LANES] = jnp.where(first, out[0], out[1]).astype(BF)
    if copies:
        copies[3].wait()
    attended = x + dot(mixed[...], w_proj[...])
    h = normed(attended, gains[layer, 1:2, :])
    total = attended
    for t in range(FF // TILE):
        if copies:
            copies[2 * t + 4].wait()
            copies[2 * t + 5].wait()
        f = slice(t * TILE, (t + 1) * TILE)
        total = total + dot(gelu(dot(h, w_up[:, f])).astype(BF), w_down[f, :])
    return total.astype(BF)


def bin_kernel(
    arrived, background, gains, wq, wp, wu, wd,
    keep, above, right, corner,
    lined, pick, vq, vp, vu, vd, qkv, mixed, state, sems,
):
    copies = weight_copies(0, (wq, wp, wu, wd), (vq, vp, vu, vd), sems)
    for copy in copies:
        copy.start()
    for k in range(4):
        lined[:, k * LANES : (k + 1) * LANES] = arrived[:, k * CAP : (k + 1) * CAP, :].reshape(
            OWNERS * CAP, LANES
        )
    sub = iota((OWNERS, 8, LANES), 1)
    weight = jnp.where(sub == 0, float(CLON), 1.0)
    marks = arrived[:, 4 * CAP : SLAB, :].astype(F32) * weight
    marks = jnp.sum(marks.reshape(OWNERS // 8, 64, LANES), 1).astype(jnp.int32)
    row = iota((CELLS, LANES), 0)
    inner = row % BLK
    cell = (inner // WIN) * CLON + (row // BLK) * WIN + inner % WIN + 1
    tally = jnp.zeros((CELLS, LANES), F32)
    for g in range(OWNERS // 8):
        hit = jnp.where(cell == marks[g : g + 1, :], 1.0, 0.0)
        tally = tally + hit
        pick[:, g * LANES : (g + 1) * LANES] = hit.astype(BF)
    tally = jnp.sum(tally, 1, keepdims=True)
    sums = dot(pick[...], lined[...]) / jnp.maximum(tally, 1.0)
    for w in range(2):
        r = slice(w * BLK, (w + 1) * BLK)
        back = background[:, w * WIN : (w + 1) * WIN, :].astype(F32).reshape(BLK, D)
        state[r, :] = (back + sums[r, :]).astype(BF).astype(F32)
    done = block_body(0, state[...], None, gains, (vq, vp, vu, vd), copies, qkv, mixed)
    one = done[:BLK].reshape(WIN, WIN, D)
    two = done[BLK:].reshape(WIN, WIN, D)
    corner[...] = one[HALF:, :HALF]
    right[...] = one[:HALF, :HALF]
    above[:, :HALF, :] = one[HALF:, HALF:]
    above[:, HALF:, :] = two[HALF:]
    keep[:, :HALF, :] = one[:HALF, HALF:]
    keep[:, HALF:, :] = two[:HALF]


WEIGHT_SCRATCH = [
    pltpu.VMEM((D, 3 * D), BF),
    pltpu.VMEM((D, D), BF),
    pltpu.VMEM((D, FF), BF),
    pltpu.VMEM((FF, D), BF),
]
WEIGHT_SEMS = pltpu.SemaphoreType.DMA((4 + 2 * FF // TILE,))
BLOCK_SCRATCH = [
    pltpu.VMEM((CELLS, 3 * D), BF),
    pltpu.VMEM((CELLS, D), BF),
    pltpu.VMEM((CELLS, D), F32),
]
BLOCK_COST = pl.CostEstimate(flops=4 << 30, transcendentals=2 << 20, bytes_accessed=8 << 20)
WIDE = jax.ShapeDtypeStruct((HALF, CLON - HALF, D), BF)
NARROW = jax.ShapeDtypeStruct((HALF, HALF, D), BF)
PIECES = (WIDE, WIDE, NARROW, NARROW)


def bin_block(arrived, background, gains, *weights):
    return pl.pallas_call(
        bin_kernel,
        out_shape=PIECES,
        in_specs=[VMEM] * 3 + [HBM] * 4,
        out_specs=[VMEM] * 4,
        scratch_shapes=[
            pltpu.VMEM((OWNERS * CAP, D), BF),
            pltpu.VMEM((CELLS, OWNERS * CAP), BF),
        ]
        + WEIGHT_SCRATCH
        + BLOCK_SCRATCH
        + [WEIGHT_SEMS],
        compiler_params=pltpu.CompilerParams(vmem_limit_bytes=BIN_VMEM),
        cost_estimate=BLOCK_COST,
        name="bin_block",
    )(arrived, background, gains, *weights)


def shift_kernel(
    first, mine, above, right, corner, gains, wq, wp, wu, wd,
    keep, back, left, diagonal, qkv, mixed, state, bias,
):
    area = WIN * WIN
    h = area // 2
    split = (iota((area, area), 0) < h) != (iota((area, area), 1) < h)
    bias[...] = jnp.where(split & (first[0] == 1), -1e30, 0.0)
    top = above[...].astype(F32)
    bottom = mine[...].astype(F32)
    state[0:h, :] = top[:, :WIN, :].reshape(h, D)
    state[h : 2 * h, :] = bottom[:, :WIN, :].reshape(h, D)
    top = jnp.concatenate([top[:, WIN:, :], corner[...].astype(F32)], 1)
    bottom = jnp.concatenate([bottom[:, WIN:, :], right[...].astype(F32)], 1)
    state[2 * h : 3 * h, :] = top.reshape(h, D)
    state[3 * h : 4 * h, :] = bottom.reshape(h, D)
    done = block_body(1, state[...], bias[...], gains, (wq, wp, wu, wd), (), qkv, mixed)
    one = done[:BLK].reshape(WIN, WIN, D)
    two = done[BLK:].reshape(WIN, WIN, D)
    diagonal[...] = two[:HALF, HALF:]
    left[...] = two[HALF:, HALF:]
    back[:, :WIN, :] = one[:HALF]
    back[:, WIN:, :] = two[:HALF, :HALF]
    keep[:, :WIN, :] = one[HALF:]
    keep[:, WIN:, :] = two[HALF:, :HALF]


def shift_block(first, pieces, gains, *weights):
    return pl.pallas_call(
        shift_kernel,
        out_shape=PIECES,
        in_specs=[SMEM] + [VMEM] * 9,
        out_specs=[VMEM] * 4,
        scratch_shapes=BLOCK_SCRATCH + [pltpu.VMEM((WIN * WIN, WIN * WIN), F32)],
        compiler_params=pltpu.CompilerParams(vmem_limit_bytes=SHIFT_VMEM),
        cost_estimate=BLOCK_COST,
        name="shift_block",
    )(first, *pieces, gains, *weights)


def moved(block, lat_step, lon_step):
    lat_count = lax.axis_size("lat")
    lon_count = lax.axis_size("lon")
    route = [
        (
            i * lon_count + j,
            (i + lat_step) % lat_count * lon_count + (j + lon_step) % lon_count,
        )
        for i in range(lat_count)
        for j in range(lon_count)
    ]
    return lax.ppermute(block, ("lat", "lon"), route)


def on_device(
    obs_rows,
    obs_dest,
    obs_token,
    obs_count,
    background,
    w_obs_in,
    w_obs_out,
    w_qkv,
    w_proj,
    w_up,
    w_down,
    norm_gain,
):
    lat = lax.axis_index("lat")
    place = (lat * lax.axis_size("lon") + lax.axis_index("lon")).astype(jnp.int32).reshape(1)
    slab = encode(
        place,
        obs_count,
        obs_dest.reshape(1, OBS_DEV),
        obs_token.reshape(1, OBS_DEV),
        obs_rows,
        w_obs_in,
        w_obs_out,
    )
    arrived = lax.all_to_all(slab, ("lat", "lon"), split_axis=0, concat_axis=0, tiled=True)
    weights = (w_qkv, w_proj, w_up, w_down)
    mine, above, right, corner = bin_block(arrived, background, norm_gain, *weights)
    late = fetch(mine, *weights)
    above = moved(above, 1, 0)
    right = moved(right, 0, -1)
    corner = moved(corner, 1, -1)
    first = (lat == 0).astype(jnp.int32).reshape(1)
    mine, back, left, corner = shift_block(first, (mine, above, right, corner), norm_gain, *late)
    below = moved(back, -1, 0)
    left = moved(left, 0, 1)
    corner = moved(corner, -1, 1)
    top = jnp.concatenate([left, mine], 1)
    bottom = jnp.concatenate([corner, below], 1)
    return jnp.concatenate([top, bottom], 0)


def solution(mesh):
    both = P(("lat", "lon"))
    rows = P(("lat", "lon"), None)
    grid = P("lat", "lon", None)
    return jax.shard_map(
        on_device,
        mesh=mesh,
        in_specs=(rows, rows, both, both, grid) + (P(),) * 7,
        out_specs=grid,
        check_vma=False,
    )
```

```python
import jax
import jax.numpy as jnp
from jax import lax
from jax.experimental import pallas as pl
from jax.experimental.pallas import tpu as pltpu
from jax.sharding import PartitionSpec as P

D = 512
FF = 2048
HEADS = 8
WIN = 16
HALF = 8
CLAT = 16
CLON = 32
CELLS = CLAT * CLON
OBS_DEV = 1024
OWNERS = 128
N_LAT = 8
N_LON = 16
CAP = 16
LANES = 128
SLAB = 4 * CAP + 8
BLK = 256
TILE = 1024
ENC_TILES = (1024, 1024)
AHEAD = 5
ENC = 1024
PUT = 1024
EPS = 1e-5
ENCODE_VMEM = 67043328 - (100 << 10)
BIN_VMEM = (64 << 20) - (16000 << 10)
SHIFT_VMEM = 16 << 20
LATE_VMEM = 8 << 20
FETCH_VMEM = (64 << 20) - (18500 << 10)
BF = jnp.bfloat16
F32 = jnp.float32
VMEM = pl.BlockSpec(memory_space=pltpu.VMEM)
HBM = pl.BlockSpec(memory_space=pltpu.HBM)
SMEM = pl.BlockSpec(memory_space=pltpu.SMEM)


def gelu(v):
    c = 0.7978845608028654
    inner = v * (c + (c * 0.044715) * (v * v))
    half = 0.5 * v
    return half + half * jnp.tanh(inner)


def dot(a, b):
    return jnp.dot(a, b, preferred_element_type=F32)


def dot_nt(a, b):
    return lax.dot_general(a, b, (((1,), (1,)), ((), ())), preferred_element_type=F32)


def normed(x, gain):
    mean = jnp.mean(x, -1, keepdims=True)
    centred = x - mean
    var = jnp.mean(centred * centred, -1, keepdims=True)
    return (centred * lax.rsqrt(var + EPS) * gain).astype(BF)


def iota(shape, axis):
    return lax.broadcasted_iota(jnp.int32, shape, axis)


def encode_kernel(
    place, count, dest, token, rows_hbm, w_in_hbm, w_out_hbm, slab_hbm,
    rows, w_in, w_out, slab, encoded, total, slots, in_sems, out_sems,
):
    copies = [pltpu.make_async_copy(rows_hbm, rows, in_sems.at[0])]
    spans = []
    for t, width in enumerate(ENC_TILES):
        f = slice(sum(ENC_TILES[:t]), sum(ENC_TILES[: t + 1]))
        spans.append(f)
        copies.append(pltpu.make_async_copy(w_in_hbm.at[:, f], w_in.at[:, f], in_sems.at[2 * t + 1]))
        copies.append(pltpu.make_async_copy(w_out_hbm.at[f, :], w_out.at[f, :], in_sems.at[2 * t + 2]))
    for copy in copies[:AHEAD]:
        copy.start()

    def arrive(i):
        copies[i].wait()
        if i + AHEAD < len(copies):
            copies[i + AHEAD].start()

    live_count = count[0]
    lane_base = (place[0] % 8) * CAP
    before = iota((BLK, BLK), 0) < iota((BLK, BLK), 1)
    upper = jnp.where(before, 1.0, 0.0).astype(BF)
    owner_col = iota((OWNERS, BLK), 0)
    lane_col = iota((LANES, BLK), 0)
    carry = jnp.zeros((OWNERS, 1), F32)
    high = jnp.zeros((OWNERS, LANES), F32)
    low = jnp.zeros((OWNERS, LANES), F32)
    for b in range(OBS_DEV // BLK):
        cols = slice(b * BLK, (b + 1) * BLK)
        owner = dest[:, cols]
        target = owner % N_LON * N_LAT + owner // N_LON
        live = (iota((1, BLK), 1) + b * BLK) < live_count
        hits = jnp.where((owner_col == target) & live, 1.0, 0.0)
        hits_bf = hits.astype(BF)
        earlier = dot(hits_bf, upper) + carry
        carry = carry + jnp.sum(hits, 1, keepdims=True)
        rank = jnp.sum(earlier * hits, 0, keepdims=True).astype(jnp.int32)
        slots[:, cols] = jnp.where(live, target * CAP + rank, -1)
        cell = token[:, cols]
        spread = lane_col == (rank + lane_base)
        row_part = jnp.where(spread, (cell // CLON).astype(F32), 0.0).astype(BF)
        col_part = jnp.where(spread, (cell % CLON + 1).astype(F32), 0.0).astype(BF)
        high = high + dot_nt(hits_bf, row_part)
        low = low + dot_nt(hits_bf, col_part)
    sub = iota((OWNERS, 8, LANES), 1)
    marks = jnp.where(sub == 0, high[:, None, :], jnp.where(sub == 1, low[:, None, :], 0.0))
    slab[:, 4 * CAP : SLAB, :] = marks.astype(BF)
    arrive(0)
    for t, f in enumerate(spans):
        arrive(2 * t + 1)
        arrive(2 * t + 2)

        def encode_block(b, _):
            r = pl.ds(pl.multiple_of(b * ENC, ENC), ENC)
            hidden = gelu(dot(rows[r, :], w_in[:, f])).astype(BF)
            part = dot(hidden, w_out[f, :])
            if t > 0:
                part = total[r, :] + part
            if t + 1 < len(spans):
                total[r, :] = part
            else:
                encoded[r, :] = part.astype(BF)
            return 0

        lax.fori_loop(0, OBS_DEV // ENC, encode_block, 0)
    step = PUT // CAP

    def slab_copy(b):
        d = pl.ds(b * step, step)
        return pltpu.make_async_copy(slab.at[d], slab_hbm.at[d], out_sems.at[b])

    def place_block(b, _):
        wanted = iota((PUT, OBS_DEV), 0) + b * PUT
        pick = jnp.where(slots[...] == wanted, 1.0, 0.0).astype(BF)
        moved = dot(pick, encoded[...]).astype(BF).reshape(step, CAP, D)
        d = pl.ds(b * step, step)
        for k in range(4):
            slab[d, k * CAP : (k + 1) * CAP, :] = moved[:, :, k * LANES : (k + 1) * LANES]
        slab_copy(b).start()
        return 0

    lax.fori_loop(0, OWNERS // step, place_block, 0)
    for b in range(OWNERS // step):
        slab_copy(b).wait()


def encode(place, count, dest, token, rows, w_in, w_out):
    return pl.pallas_call(
        encode_kernel,
        out_shape=jax.ShapeDtypeStruct((OWNERS, SLAB, LANES), BF),
        in_specs=[SMEM, SMEM, VMEM, VMEM, HBM, HBM, HBM],
        out_specs=HBM,
        scratch_shapes=[
            pltpu.VMEM((OBS_DEV, D), BF),
            pltpu.VMEM((D, FF), BF),
            pltpu.VMEM((FF, D), BF),
            pltpu.VMEM((OWNERS, SLAB, LANES), BF),
            pltpu.VMEM((OBS_DEV, D), BF),
            pltpu.VMEM((OBS_DEV, D), F32),
            pltpu.VMEM((1, OBS_DEV), jnp.int32),
            pltpu.SemaphoreType.DMA((2 * len(ENC_TILES) + 1,)),
            pltpu.SemaphoreType.DMA((OWNERS * CAP // PUT,)),
        ],
        compiler_params=pltpu.CompilerParams(vmem_limit_bytes=ENCODE_VMEM),
        cost_estimate=pl.CostEstimate(
            flops=7 << 30, transcendentals=OBS_DEV * FF, bytes_accessed=8 << 20
        ),
        name="encode",
    )(place, count, dest, token, rows, w_in, w_out)


def weight_copies(layer, hbm, vmem, sems):
    w_qkv, w_proj, w_up, w_down = hbm
    v_qkv, v_proj, v_up, v_down = vmem
    pairs = []
    for part in range(3):
        c = slice(part * D, (part + 1) * D)
        pairs.append((w_qkv.at[layer, :, c], v_qkv.at[:, c]))
    pairs.append((w_proj.at[layer], v_proj))
    for t in range(FF // TILE):
        f = slice(t * TILE, (t + 1) * TILE)
        pairs.append((w_up.at[layer, :, f], v_up.at[:, f]))
        pairs.append((w_down.at[layer, f, :], v_down.at[f, :]))
    return [pltpu.make_async_copy(a, b, sems.at[i]) for i, (a, b) in enumerate(pairs)]


def fetch_kernel(after, wq, wp, wu, wd, vq, vp, vu, vd, sems):
    copies = []
    for i, (a, b) in enumerate(((wq, vq), (wp, vp), (wu, vu), (wd, vd))):
        copies.append(pltpu.make_async_copy(a.at[1], b, sems.at[i]))
        copies[-1].start()
    for copy in copies:
        copy.wait()


def fetch(after, *arrays):
    size = sum(a.size * a.dtype.itemsize for a in arrays)
    return pl.pallas_call(
        fetch_kernel,
        out_shape=[jax.ShapeDtypeStruct(a.shape[1:], a.dtype) for a in arrays],
        in_specs=[HBM] * 5,
        out_specs=[VMEM] * 4,
        scratch_shapes=[pltpu.SemaphoreType.DMA((4,))],
        compiler_params=pltpu.CompilerParams(vmem_limit_bytes=FETCH_VMEM),
        cost_estimate=pl.CostEstimate(flops=0, transcendentals=0, bytes_accessed=2 * size),
        name="fetch",
    )(after, *arrays)


def project(layer, x, gains, w_qkv, copies, qkv):
    h = normed(x, gains[layer, 0:1, :])
    for part in range(3):
        c = slice(part * D, (part + 1) * D)
        if copies:
            copies[part].wait()
        qkv[:, c] = dot(h, w_qkv[:, c]).astype(BF)


def attend(queries, keys, values, bias, mixed):
    count = queries.shape[0]
    first = iota((count, LANES), 1) < 64
    ones = jnp.ones((WIN * WIN, LANES), BF)
    for pair in range(HEADS // 2):
        c = slice(pair * LANES, (pair + 1) * LANES)
        q = queries[:, c] * BF(0.125)
        k = keys[:, c]
        v = jnp.concatenate([values[:, c], ones], 1)
        out = []
        for head in range(2):
            mine = first if head == 0 else jnp.logical_not(first)
            scores = dot_nt(jnp.where(mine, q, BF(0)), k)
            if bias is not None:
                scores = scores + bias
            probs = jnp.exp(scores - jnp.max(scores, -1, keepdims=True)).astype(BF)
            both = dot(probs, v)
            out.append(both[:, :LANES] / both[:, LANES:])
        mixed[:, c] = jnp.where(first, out[0], out[1]).astype(BF)


def finish(layer, x, mixed, gains, w_proj, w_up, w_down, copies):
    if copies:
        copies[3].wait()
    attended = x + dot(mixed, w_proj[...])
    h = normed(attended, gains[layer, 1:2, :])
    total = attended
    for t in range(FF // TILE):
        if copies:
            copies[2 * t + 4].wait()
            copies[2 * t + 5].wait()
        f = slice(t * TILE, (t + 1) * TILE)
        total = total + dot(gelu(dot(h, w_up[:, f])).astype(BF), w_down[f, :])
    return total.astype(BF)


def bin_kernel(
    arrived, background, gains, wq, wp, wu, wd,
    keep, above, right, corner,
    lined, pick, vq, vp, vu, vd, qkv, mixed, state, sems,
):
    copies = weight_copies(0, (wq, wp, wu, wd), (vq, vp, vu, vd), sems)
    for copy in copies:
        copy.start()
    for k in range(4):
        lined[:, k * LANES : (k + 1) * LANES] = arrived[:, k * CAP : (k + 1) * CAP, :].reshape(
            OWNERS * CAP, LANES
        )
    sub = iota((OWNERS, 8, LANES), 1)
    weight = jnp.where(sub == 0, float(CLON), 1.0)
    marks = arrived[:, 4 * CAP : SLAB, :].astype(F32) * weight
    marks = jnp.sum(marks.reshape(OWNERS // 8, 64, LANES), 1).astype(jnp.int32)
    row = iota((CELLS, LANES), 0)
    inner = row % BLK
    cell = (inner // WIN) * CLON + (row // BLK) * WIN + inner % WIN + 1
    tally = jnp.zeros((CELLS, LANES), F32)
    for g in range(OWNERS // 8):
        hit = jnp.where(cell == marks[g : g + 1, :], 1.0, 0.0)
        tally = tally + hit
        pick[:, g * LANES : (g + 1) * LANES] = hit.astype(BF)
    tally = jnp.sum(tally, 1, keepdims=True)
    sums = dot(pick[...], lined[...]) / jnp.maximum(tally, 1.0)
    for w in range(2):
        r = slice(w * BLK, (w + 1) * BLK)
        back = background[:, w * WIN : (w + 1) * WIN, :].astype(F32).reshape(BLK, D)
        state[r, :] = (back + sums[r, :]).astype(BF).astype(F32)
    project(0, state[...], gains, vq, copies, qkv)
    for w in range(2):
        r = pl.ds(w * BLK, BLK)
        parts = [qkv.at[r, pl.ds(part * D, D)] for part in range(3)]
        attend(*parts, None, mixed.at[r])
    done = finish(0, state[...], mixed[...], gains, vp, vu, vd, copies)
    one = done[:BLK].reshape(WIN, WIN, D)
    two = done[BLK:].reshape(WIN, WIN, D)
    corner[...] = one[HALF:, :HALF]
    right[...] = one[:HALF, :HALF]
    above[:, :HALF, :] = one[HALF:, HALF:]
    above[:, HALF:, :] = two[HALF:]
    keep[:, :HALF, :] = one[:HALF, HALF:]
    keep[:, HALF:, :] = two[:HALF]


WEIGHT_SCRATCH = [
    pltpu.VMEM((D, 3 * D), BF),
    pltpu.VMEM((D, D), BF),
    pltpu.VMEM((D, FF), BF),
    pltpu.VMEM((FF, D), BF),
]
WEIGHT_SEMS = pltpu.SemaphoreType.DMA((4 + 2 * FF // TILE,))
BLOCK_SCRATCH = [
    pltpu.VMEM((CELLS, 3 * D), BF),
    pltpu.VMEM((CELLS, D), BF),
    pltpu.VMEM((CELLS, D), F32),
]
BLOCK_COST = pl.CostEstimate(flops=4 << 30, transcendentals=2 << 20, bytes_accessed=8 << 20)
WIDE = jax.ShapeDtypeStruct((HALF, CLON - HALF, D), BF)
NARROW = jax.ShapeDtypeStruct((HALF, HALF, D), BF)
PIECES = (WIDE, WIDE, NARROW, NARROW)


def bin_block(arrived, background, gains, *weights):
    return pl.pallas_call(
        bin_kernel,
        out_shape=PIECES,
        in_specs=[VMEM] * 3 + [HBM] * 4,
        out_specs=[VMEM] * 4,
        scratch_shapes=[
            pltpu.VMEM((OWNERS * CAP, D), BF),
            pltpu.VMEM((CELLS, OWNERS * CAP), BF),
        ]
        + WEIGHT_SCRATCH
        + BLOCK_SCRATCH
        + [WEIGHT_SEMS],
        compiler_params=pltpu.CompilerParams(vmem_limit_bytes=BIN_VMEM),
        cost_estimate=BLOCK_COST,
        name="bin_block",
    )(arrived, background, gains, *weights)


def region_bias(first):
    area = WIN * WIN
    split = (iota((area, area), 0) < BLK // 2) != (iota((area, area), 1) < BLK // 2)
    return jnp.where(split & (first == 1), -1e30, 0.0)


def shift_kernel(
    first, mine, above, right, corner, gains, wq, wp, wu, wd,
    edge, back, left, diagonal, late_q, late_kv, late_x, qkv, mixed, state, bias,
):
    h = BLK // 2
    bias[...] = region_bias(first[0])
    top = above[...].astype(F32)
    bottom = mine[...].astype(F32)
    state[0:h, :] = top[:, :WIN, :].reshape(h, D)
    state[h : 2 * h, :] = bottom[:, :WIN, :].reshape(h, D)
    top = jnp.concatenate([top[:, WIN:, :], corner[...].astype(F32)], 1)
    bottom = jnp.concatenate([bottom[:, WIN:, :], right[...].astype(F32)], 1)
    state[2 * h : 3 * h, :] = top.reshape(h, D)
    state[3 * h : 4 * h, :] = bottom.reshape(h, D)
    project(1, state[...], gains, wq, (), qkv)
    parts = [qkv.at[pl.ds(0, BLK), pl.ds(part * D, D)] for part in range(3)]
    attend(parts[0].at[pl.ds(0, h)], parts[1], parts[2], bias[0:h, :], mixed.at[pl.ds(0, h)])
    parts = [qkv.at[pl.ds(BLK, BLK), pl.ds(part * D, D)] for part in range(3)]
    attend(*parts, bias[...], mixed.at[pl.ds(h, BLK)])
    late_q[...] = qkv[h:BLK, :D]
    late_kv[...] = qkv[0:BLK, D:]
    late_x[...] = state[h:BLK, :].astype(BF)
    x = jnp.concatenate([state[0:h, :], state[BLK:, :]], 0)
    done = finish(1, x, mixed[...], gains, wp, wu, wd, ())
    one = done[:h].reshape(HALF, WIN, D)
    two = done[h:].reshape(WIN, WIN, D)
    diagonal[...] = two[:HALF, HALF:]
    left[...] = two[HALF:, HALF:]
    back[:, :WIN, :] = one
    back[:, WIN:, :] = two[:HALF, :HALF]
    edge[...] = two[HALF:, :HALF]


def shift_block(first, pieces, gains, *weights):
    h = BLK // 2
    return pl.pallas_call(
        shift_kernel,
        out_shape=(
            NARROW,
            WIDE,
            NARROW,
            NARROW,
            jax.ShapeDtypeStruct((h, D), BF),
            jax.ShapeDtypeStruct((BLK, 2 * D), BF),
            jax.ShapeDtypeStruct((h, D), BF),
        ),
        in_specs=[SMEM] + [VMEM] * 9,
        out_specs=[VMEM] * 7,
        scratch_shapes=[
            pltpu.VMEM((CELLS, 3 * D), BF),
            pltpu.VMEM((CELLS - h, D), BF),
            pltpu.VMEM((CELLS, D), F32),
            pltpu.VMEM((BLK, BLK), F32),
        ],
        compiler_params=pltpu.CompilerParams(vmem_limit_bytes=SHIFT_VMEM),
        cost_estimate=BLOCK_COST,
        name="shift_block",
    )(first, *pieces, gains, *weights)


def late_kernel(first, q, kv, x, gains, wp, wu, wd, out, mixed):
    h = BLK // 2
    bias = region_bias(first[0])[h:, :]
    attend(q, kv.at[:, pl.ds(0, D)], kv.at[:, pl.ds(D, D)], bias, mixed)
    done = finish(1, x[...].astype(F32), mixed[...], gains, wp, wu, wd, ())
    out[...] = done.reshape(HALF, WIN, D)


def late_block(first, q, kv, x, gains, *weights):
    return pl.pallas_call(
        late_kernel,
        out_shape=jax.ShapeDtypeStruct((HALF, WIN, D), BF),
        in_specs=[SMEM] + [VMEM] * 7,
        out_specs=VMEM,
        scratch_shapes=[pltpu.VMEM((BLK // 2, D), BF)],
        compiler_params=pltpu.CompilerParams(vmem_limit_bytes=LATE_VMEM),
        cost_estimate=pl.CostEstimate(
            flops=1 << 30, transcendentals=1 << 19, bytes_accessed=6 << 20
        ),
        name="late_block",
    )(first, q, kv, x, gains, *weights)


def moved(block, lat_step, lon_step):
    lat_count = lax.axis_size("lat")
    lon_count = lax.axis_size("lon")
    route = [
        (
            i * lon_count + j,
            (i + lat_step) % lat_count * lon_count + (j + lon_step) % lon_count,
        )
        for i in range(lat_count)
        for j in range(lon_count)
    ]
    return lax.ppermute(block, ("lat", "lon"), route)


def on_device(
    obs_rows,
    obs_dest,
    obs_token,
    obs_count,
    background,
    w_obs_in,
    w_obs_out,
    w_qkv,
    w_proj,
    w_up,
    w_down,
    norm_gain,
):
    lat = lax.axis_index("lat")
    place = (lax.axis_index("lon") * N_LAT + lat).astype(jnp.int32).reshape(1)
    slab = encode(
        place,
        obs_count,
        obs_dest.reshape(1, OBS_DEV),
        obs_token.reshape(1, OBS_DEV),
        obs_rows,
        w_obs_in,
        w_obs_out,
    )
    arrived = lax.all_to_all(slab, ("lon", "lat"), split_axis=0, concat_axis=0, tiled=True)
    weights = (w_qkv, w_proj, w_up, w_down)
    mine, above, right, corner = bin_block(arrived, background, norm_gain, *weights)
    late = fetch(mine, *weights)
    above = moved(above, 1, 0)
    right = moved(right, 0, -1)
    corner = moved(corner, 1, -1)
    first = (lat == 0).astype(jnp.int32).reshape(1)
    edge, back, left, corner, q, kv, x = shift_block(
        first, (mine, above, right, corner), norm_gain, *late
    )
    below = moved(back, -1, 0)
    left = moved(left, 0, 1)
    corner = moved(corner, -1, 1)
    mid = late_block(first, q, kv, x, norm_gain, *late[1:])
    top = jnp.concatenate([left, mid, edge], 1)
    bottom = jnp.concatenate([corner, below], 1)
    return jnp.concatenate([top, bottom], 0)


def solution(mesh):
    both = P(("lat", "lon"))
    rows = P(("lat", "lon"), None)
    grid = P("lat", "lon", None)
    return jax.shard_map(
        on_device,
        mesh=mesh,
        in_specs=(rows, rows, both, both, grid) + (P(),) * 7,
        out_specs=grid,
        check_vma=False,
    )
```

```python
import jax
import jax.numpy as jnp
from jax import lax
from jax.experimental import pallas as pl
from jax.experimental.pallas import tpu as pltpu
from jax.sharding import PartitionSpec as P

D = 512
FF = 2048
HEADS = 8
WIN = 16
HALF = 8
CLAT = 16
CLON = 32
CELLS = CLAT * CLON
OBS_DEV = 1024
OWNERS = 128
N_LAT = 8
N_LON = 16
CAP = 16
LANES = 128
SLAB = 4 * CAP + 8
BLK = 256
TILE = 1024
ENC_TILES = (1024, 1024)
AHEAD = 5
ENC = 1024
PUT = 1024
EPS = 1e-5
ENCODE_VMEM = 67043328 - (100 << 10)
BIN_VMEM = (64 << 20) - (16000 << 10)
SHIFT_VMEM = 16 << 20
LATE_VMEM = 8 << 20
FETCH_VMEM = (64 << 20) - (18500 << 10)
BF = jnp.bfloat16
F32 = jnp.float32
VMEM = pl.BlockSpec(memory_space=pltpu.VMEM)
HBM = pl.BlockSpec(memory_space=pltpu.HBM)
SMEM = pl.BlockSpec(memory_space=pltpu.SMEM)


def gelu(v):
    c = 0.7978845608028654
    inner = v * (c + (c * 0.044715) * (v * v))
    half = 0.5 * v
    return half + half * jnp.tanh(inner)


def dot(a, b):
    return jnp.dot(a, b, preferred_element_type=F32)


def dot_nt(a, b):
    return lax.dot_general(a, b, (((1,), (1,)), ((), ())), preferred_element_type=F32)


def normed(x, gain):
    mean = jnp.mean(x, -1, keepdims=True)
    centred = x - mean
    var = jnp.mean(centred * centred, -1, keepdims=True)
    return (centred * lax.rsqrt(var + EPS) * gain).astype(BF)


def iota(shape, axis):
    return lax.broadcasted_iota(jnp.int32, shape, axis)


def encode_kernel(
    place, count, dest, token, rows_hbm, w_in_hbm, w_out_hbm, slab_hbm,
    rows, w_in, w_out, slab, encoded, total, slots, in_sems, out_sems,
):
    copies = [pltpu.make_async_copy(rows_hbm, rows, in_sems.at[0])]
    spans = []
    for t, width in enumerate(ENC_TILES):
        f = slice(sum(ENC_TILES[:t]), sum(ENC_TILES[: t + 1]))
        spans.append(f)
        copies.append(pltpu.make_async_copy(w_in_hbm.at[:, f], w_in.at[:, f], in_sems.at[2 * t + 1]))
        copies.append(pltpu.make_async_copy(w_out_hbm.at[f, :], w_out.at[f, :], in_sems.at[2 * t + 2]))
    for copy in copies[:AHEAD]:
        copy.start()

    def arrive(i):
        copies[i].wait()
        if i + AHEAD < len(copies):
            copies[i + AHEAD].start()

    live_count = count[0]
    lane_base = (place[0] % 8) * CAP
    before = iota((BLK, BLK), 0) < iota((BLK, BLK), 1)
    upper = jnp.where(before, 1.0, 0.0).astype(BF)
    owner_col = iota((OWNERS, BLK), 0)
    lane_col = iota((LANES, BLK), 0)
    carry = jnp.zeros((OWNERS, 1), F32)
    high = jnp.zeros((OWNERS, LANES), F32)
    low = jnp.zeros((OWNERS, LANES), F32)
    for b in range(OBS_DEV // BLK):
        cols = slice(b * BLK, (b + 1) * BLK)
        owner = dest[:, cols]
        target = owner % N_LON * N_LAT + owner // N_LON
        live = (iota((1, BLK), 1) + b * BLK) < live_count
        hits = jnp.where((owner_col == target) & live, 1.0, 0.0)
        hits_bf = hits.astype(BF)
        earlier = dot(hits_bf, upper) + carry
        carry = carry + jnp.sum(hits, 1, keepdims=True)
        rank = jnp.sum(earlier * hits, 0, keepdims=True).astype(jnp.int32)
        slots[:, cols] = jnp.where(live, target * CAP + rank, -1)
        cell = token[:, cols]
        spread = lane_col == (rank + lane_base)
        row_part = jnp.where(spread, (cell // CLON).astype(F32), 0.0).astype(BF)
        col_part = jnp.where(spread, (cell % CLON + 1).astype(F32), 0.0).astype(BF)
        high = high + dot_nt(hits_bf, row_part)
        low = low + dot_nt(hits_bf, col_part)
    sub = iota((OWNERS, 8, LANES), 1)
    marks = jnp.where(sub == 0, high[:, None, :], jnp.where(sub == 1, low[:, None, :], 0.0))
    slab[:, 4 * CAP : SLAB, :] = marks.astype(BF)
    arrive(0)
    for t, f in enumerate(spans):
        arrive(2 * t + 1)
        arrive(2 * t + 2)

        def encode_block(b, _):
            r = pl.ds(pl.multiple_of(b * ENC, ENC), ENC)
            hidden = gelu(dot(rows[r, :], w_in[:, f])).astype(BF)
            part = dot(hidden, w_out[f, :])
            if t > 0:
                part = total[r, :] + part
            if t + 1 < len(spans):
                total[r, :] = part
            else:
                encoded[r, :] = part.astype(BF)
            return 0

        lax.fori_loop(0, OBS_DEV // ENC, encode_block, 0)
    step = PUT // CAP

    def slab_copy(b):
        d = pl.ds(b * step, step)
        return pltpu.make_async_copy(slab.at[d], slab_hbm.at[d], out_sems.at[b])

    def place_block(b, _):
        wanted = iota((PUT, OBS_DEV), 0) + b * PUT
        pick = jnp.where(slots[...] == wanted, 1.0, 0.0).astype(BF)
        moved = dot(pick, encoded[...]).astype(BF).reshape(step, CAP, D)
        d = pl.ds(b * step, step)
        for k in range(4):
            slab[d, k * CAP : (k + 1) * CAP, :] = moved[:, :, k * LANES : (k + 1) * LANES]
        slab_copy(b).start()
        return 0

    lax.fori_loop(0, OWNERS // step, place_block, 0)
    for b in range(OWNERS // step):
        slab_copy(b).wait()


def encode(place, count, dest, token, rows, w_in, w_out):
    return pl.pallas_call(
        encode_kernel,
        out_shape=jax.ShapeDtypeStruct((OWNERS, SLAB, LANES), BF),
        in_specs=[SMEM, SMEM, VMEM, VMEM, HBM, HBM, HBM],
        out_specs=HBM,
        scratch_shapes=[
            pltpu.VMEM((OBS_DEV, D), BF),
            pltpu.VMEM((D, FF), BF),
            pltpu.VMEM((FF, D), BF),
            pltpu.VMEM((OWNERS, SLAB, LANES), BF),
            pltpu.VMEM((OBS_DEV, D), BF),
            pltpu.VMEM((OBS_DEV, D), F32),
            pltpu.VMEM((1, OBS_DEV), jnp.int32),
            pltpu.SemaphoreType.DMA((2 * len(ENC_TILES) + 1,)),
            pltpu.SemaphoreType.DMA((OWNERS * CAP // PUT,)),
        ],
        compiler_params=pltpu.CompilerParams(vmem_limit_bytes=ENCODE_VMEM),
        cost_estimate=pl.CostEstimate(
            flops=7 << 30, transcendentals=OBS_DEV * FF, bytes_accessed=8 << 20
        ),
        name="encode",
    )(place, count, dest, token, rows, w_in, w_out)


def weight_copies(layer, hbm, vmem, sems):
    w_qkv, w_proj, w_up, w_down = hbm
    v_qkv, v_proj, v_up, v_down = vmem
    pairs = []
    for part in range(3):
        c = slice(part * D, (part + 1) * D)
        pairs.append((w_qkv.at[layer, :, c], v_qkv.at[:, c]))
    pairs.append((w_proj.at[layer], v_proj))
    for t in range(FF // TILE):
        f = slice(t * TILE, (t + 1) * TILE)
        pairs.append((w_up.at[layer, :, f], v_up.at[:, f]))
        pairs.append((w_down.at[layer, f, :], v_down.at[f, :]))
    return [pltpu.make_async_copy(a, b, sems.at[i]) for i, (a, b) in enumerate(pairs)]


def fetch_kernel(after, wq, wp, wu, wd, vq, vp, vu, vd, sems):
    copies = []
    for i, (a, b) in enumerate(((wq, vq), (wp, vp), (wu, vu), (wd, vd))):
        copies.append(pltpu.make_async_copy(a.at[1], b, sems.at[i]))
        copies[-1].start()
    for copy in copies:
        copy.wait()


def fetch(after, *arrays):
    size = sum(a.size * a.dtype.itemsize for a in arrays)
    return pl.pallas_call(
        fetch_kernel,
        out_shape=[jax.ShapeDtypeStruct(a.shape[1:], a.dtype) for a in arrays],
        in_specs=[HBM] * 5,
        out_specs=[VMEM] * 4,
        scratch_shapes=[pltpu.SemaphoreType.DMA((4,))],
        compiler_params=pltpu.CompilerParams(vmem_limit_bytes=FETCH_VMEM),
        cost_estimate=pl.CostEstimate(flops=0, transcendentals=0, bytes_accessed=2 * size),
        name="fetch",
    )(after, *arrays)


def project(layer, x, gains, w_qkv, copies, qkv):
    h = normed(x, gains[layer, 0:1, :])
    for part in range(3):
        c = slice(part * D, (part + 1) * D)
        if copies:
            copies[part].wait()
        qkv[:, c] = dot(h, w_qkv[:, c]).astype(BF)


def attend(queries, keys, values, bias, mixed):
    count = queries.shape[0]
    first = iota((count, LANES), 1) < 64
    ones = jnp.ones((WIN * WIN, LANES), BF)
    for pair in range(HEADS // 2):
        c = slice(pair * LANES, (pair + 1) * LANES)
        q = queries[:, c] * BF(0.125)
        k = keys[:, c]
        v = jnp.concatenate([values[:, c], ones], 1)
        out = []
        for head in range(2):
            mine = first if head == 0 else jnp.logical_not(first)
            scores = dot_nt(jnp.where(mine, q, BF(0)), k)
            if bias is not None:
                scores = scores + bias
            probs = jnp.exp(scores - jnp.max(scores, -1, keepdims=True)).astype(BF)
            both = dot(probs, v)
            out.append(both[:, :LANES] / both[:, LANES:])
        mixed[:, c] = jnp.where(first, out[0], out[1]).astype(BF)


def finish(layer, x, mixed, gains, w_proj, w_up, w_down, copies):
    if copies:
        copies[3].wait()
    attended = x + dot(mixed, w_proj[...])
    h = normed(attended, gains[layer, 1:2, :])
    total = attended
    for t in range(FF // TILE):
        if copies:
            copies[2 * t + 4].wait()
            copies[2 * t + 5].wait()
        f = slice(t * TILE, (t + 1) * TILE)
        total = total + dot(gelu(dot(h, w_up[:, f])).astype(BF), w_down[f, :])
    return total.astype(BF)


def bin_kernel(
    arrived, background, gains, wq, wp, wu, wd,
    keep, above, right, corner,
    lined, pick, vq, vp, vu, vd, qkv, mixed, state, sems,
):
    copies = weight_copies(0, (wq, wp, wu, wd), (vq, vp, vu, vd), sems)
    for copy in copies:
        copy.start()
    for k in range(4):
        lined[:, k * LANES : (k + 1) * LANES] = arrived[:, k * CAP : (k + 1) * CAP, :].reshape(
            OWNERS * CAP, LANES
        )
    sub = iota((OWNERS, 8, LANES), 1)
    weight = jnp.where(sub == 0, float(CLON), 1.0)
    marks = arrived[:, 4 * CAP : SLAB, :].astype(F32) * weight
    marks = jnp.sum(marks.reshape(OWNERS // 8, 64, LANES), 1).astype(jnp.int32)
    row = iota((CELLS, LANES), 0)
    inner = row % BLK
    cell = (inner // WIN) * CLON + (row // BLK) * WIN + inner % WIN + 1
    tally = jnp.zeros((CELLS, LANES), F32)
    for g in range(OWNERS // 8):
        hit = jnp.where(cell == marks[g : g + 1, :], 1.0, 0.0)
        tally = tally + hit
        pick[:, g * LANES : (g + 1) * LANES] = hit.astype(BF)
    tally = jnp.sum(tally, 1, keepdims=True)
    sums = dot(pick[...], lined[...]) / jnp.maximum(tally, 1.0)
    for w in range(2):
        r = slice(w * BLK, (w + 1) * BLK)
        back = background[:, w * WIN : (w + 1) * WIN, :].astype(F32).reshape(BLK, D)
        state[r, :] = (back + sums[r, :]).astype(BF).astype(F32)
    project(0, state[...], gains, vq, copies, qkv)
    for w in range(2):
        r = pl.ds(w * BLK, BLK)
        parts = [qkv.at[r, pl.ds(part * D, D)] for part in range(3)]
        attend(*parts, None, mixed.at[r])
    done = finish(0, state[...], mixed[...], gains, vp, vu, vd, copies)
    one = done[:BLK].reshape(WIN, WIN, D)
    two = done[BLK:].reshape(WIN, WIN, D)
    corner[...] = one[HALF:, :HALF]
    right[...] = one[:HALF, :HALF]
    above[:, :HALF, :] = one[HALF:, HALF:]
    above[:, HALF:, :] = two[HALF:]
    keep[:, :HALF, :] = one[:HALF, HALF:]
    keep[:, HALF:, :] = two[:HALF]


WEIGHT_SCRATCH = [
    pltpu.VMEM((D, 3 * D), BF),
    pltpu.VMEM((D, D), BF),
    pltpu.VMEM((D, FF), BF),
    pltpu.VMEM((FF, D), BF),
]
WEIGHT_SEMS = pltpu.SemaphoreType.DMA((4 + 2 * FF // TILE,))
BLOCK_SCRATCH = [
    pltpu.VMEM((CELLS, 3 * D), BF),
    pltpu.VMEM((CELLS, D), BF),
    pltpu.VMEM((CELLS, D), F32),
]
BLOCK_COST = pl.CostEstimate(flops=4 << 30, transcendentals=2 << 20, bytes_accessed=8 << 20)
WIDE = jax.ShapeDtypeStruct((HALF, CLON - HALF, D), BF)
NARROW = jax.ShapeDtypeStruct((HALF, HALF, D), BF)
PIECES = (WIDE, WIDE, NARROW, NARROW)


def bin_block(arrived, background, gains, *weights):
    return pl.pallas_call(
        bin_kernel,
        out_shape=PIECES,
        in_specs=[VMEM] * 3 + [HBM] * 4,
        out_specs=[VMEM] * 4,
        scratch_shapes=[
            pltpu.VMEM((OWNERS * CAP, D), BF),
            pltpu.VMEM((CELLS, OWNERS * CAP), BF),
        ]
        + WEIGHT_SCRATCH
        + BLOCK_SCRATCH
        + [WEIGHT_SEMS],
        compiler_params=pltpu.CompilerParams(vmem_limit_bytes=BIN_VMEM),
        cost_estimate=BLOCK_COST,
        name="bin_block",
    )(arrived, background, gains, *weights)


def region_bias(first):
    area = WIN * WIN
    split = (iota((area, area), 0) < BLK // 2) != (iota((area, area), 1) < BLK // 2)
    return jnp.where(split & (first == 1), -1e30, 0.0)


def shift_kernel(
    first, mine, above, right, corner, gains, wq, wp, wu, wd,
    edge, back, left, diagonal, late_q, late_kv, late_x, qkv, mixed, state, bias,
):
    h = BLK // 2
    bias[...] = region_bias(first[0])
    top = above[...].astype(F32)
    bottom = mine[...].astype(F32)
    state[0:h, :] = top[:, :WIN, :].reshape(h, D)
    state[h : 2 * h, :] = bottom[:, :WIN, :].reshape(h, D)
    top = jnp.concatenate([top[:, WIN:, :], corner[...].astype(F32)], 1)
    bottom = jnp.concatenate([bottom[:, WIN:, :], right[...].astype(F32)], 1)
    state[2 * h : 3 * h, :] = top.reshape(h, D)
    state[3 * h : 4 * h, :] = bottom.reshape(h, D)
    project(1, state[...], gains, wq, (), qkv)
    parts = [qkv.at[pl.ds(0, BLK), pl.ds(part * D, D)] for part in range(3)]
    attend(parts[0].at[pl.ds(0, h)], parts[1], parts[2], bias[0:h, :], mixed.at[pl.ds(0, h)])
    parts = [qkv.at[pl.ds(BLK, BLK), pl.ds(part * D, D)] for part in range(3)]
    attend(*parts, bias[...], mixed.at[pl.ds(h, BLK)])
    late_q[...] = qkv[h:BLK, :D]
    late_kv[...] = qkv[0:BLK, D:]
    late_x[...] = state[h:BLK, :].astype(BF)
    x = jnp.concatenate([state[0:h, :], state[BLK:, :]], 0)
    done = finish(1, x, mixed[...], gains, wp, wu, wd, ())
    one = done[:h].reshape(HALF, WIN, D)
    two = done[h:].reshape(WIN, WIN, D)
    diagonal[...] = two[:HALF, HALF:]
    left[...] = two[HALF:, HALF:]
    back[:, :WIN, :] = one
    back[:, WIN:, :] = two[:HALF, :HALF]
    edge[...] = two[HALF:, :HALF]


def shift_block(first, pieces, gains, *weights):
    h = BLK // 2
    return pl.pallas_call(
        shift_kernel,
        out_shape=(
            NARROW,
            WIDE,
            NARROW,
            NARROW,
            jax.ShapeDtypeStruct((h, D), BF),
            jax.ShapeDtypeStruct((BLK, 2 * D), BF),
            jax.ShapeDtypeStruct((h, D), BF),
        ),
        in_specs=[SMEM] + [VMEM] * 9,
        out_specs=[VMEM] * 7,
        scratch_shapes=[
            pltpu.VMEM((CELLS, 3 * D), BF),
            pltpu.VMEM((CELLS - h, D), BF),
            pltpu.VMEM((CELLS, D), F32),
            pltpu.VMEM((BLK, BLK), F32),
        ],
        compiler_params=pltpu.CompilerParams(vmem_limit_bytes=SHIFT_VMEM),
        cost_estimate=BLOCK_COST,
        name="shift_block",
    )(first, *pieces, gains, *weights)


def late_kernel(first, q, kv, x, gains, wp, wu, wd, out, mixed):
    h = BLK // 2
    bias = region_bias(first[0])[h:, :]
    attend(q, kv.at[:, pl.ds(0, D)], kv.at[:, pl.ds(D, D)], bias, mixed)
    done = finish(1, x[...].astype(F32), mixed[...], gains, wp, wu, wd, ())
    out[...] = done.reshape(HALF, WIN, D)


def late_block(first, q, kv, x, gains, *weights):
    return pl.pallas_call(
        late_kernel,
        out_shape=jax.ShapeDtypeStruct((HALF, WIN, D), BF),
        in_specs=[SMEM] + [VMEM] * 7,
        out_specs=VMEM,
        scratch_shapes=[pltpu.VMEM((BLK // 2, D), BF)],
        compiler_params=pltpu.CompilerParams(vmem_limit_bytes=LATE_VMEM),
        cost_estimate=pl.CostEstimate(
            flops=1 << 30, transcendentals=1 << 19, bytes_accessed=6 << 20
        ),
        name="late_block",
    )(first, q, kv, x, gains, *weights)


def moved(block, lat_step, lon_step):
    lat_count = lax.axis_size("lat")
    lon_count = lax.axis_size("lon")
    route = [
        (
            i * lon_count + j,
            (i + lat_step) % lat_count * lon_count + (j + lon_step) % lon_count,
        )
        for i in range(lat_count)
        for j in range(lon_count)
    ]
    return lax.ppermute(block, ("lat", "lon"), route)


def on_device(
    obs_rows,
    obs_dest,
    obs_token,
    obs_count,
    background,
    w_obs_in,
    w_obs_out,
    w_qkv,
    w_proj,
    w_up,
    w_down,
    norm_gain,
):
    lat = lax.axis_index("lat")
    place = (lax.axis_index("lon") * N_LAT + lat).astype(jnp.int32).reshape(1)
    slab = encode(
        place,
        obs_count,
        obs_dest.reshape(1, OBS_DEV),
        obs_token.reshape(1, OBS_DEV),
        obs_rows,
        w_obs_in,
        w_obs_out,
    )
    arrived = lax.all_to_all(slab, ("lon", "lat"), split_axis=0, concat_axis=0, tiled=True)
    weights = (w_qkv, w_proj, w_up, w_down)
    mine, above, right, corner = bin_block(arrived, background, norm_gain, *weights)
    late = fetch(mine, *weights)
    above = moved(above, 1, 0)
    right = moved(right, 0, -1)
    corner = moved(corner, 1, -1)
    first = (lat == 0).astype(jnp.int32).reshape(1)
    edge, back, left, corner, q, kv, x = shift_block(
        first, (mine, above, right, corner), norm_gain, *late
    )
    below = moved(back, -1, 0)
    mid = late_block(first, q, kv, x, norm_gain, *late[1:])
    left, corner, mid = lax.optimization_barrier((left, corner, mid))
    left = moved(left, 0, 1)
    corner = moved(corner, -1, 1)
    top = jnp.concatenate([left, mid, edge], 1)
    bottom = jnp.concatenate([corner, below], 1)
    return jnp.concatenate([top, bottom], 0)


def solution(mesh):
    both = P(("lat", "lon"))
    rows = P(("lat", "lon"), None)
    grid = P("lat", "lon", None)
    return jax.shard_map(
        on_device,
        mesh=mesh,
        in_specs=(rows, rows, both, both, grid) + (P(),) * 7,
        out_specs=grid,
        check_vma=False,
    )
```

```python
import jax
import jax.numpy as jnp
from jax import lax
from jax.experimental import pallas as pl
from jax.experimental.pallas import tpu as pltpu
from jax.sharding import PartitionSpec as P

D = 512
FF = 2048
HEADS = 8
WIN = 16
HALF = 8
CLAT = 16
CLON = 32
CELLS = CLAT * CLON
OBS_DEV = 1024
OWNERS = 128
N_LAT = 8
N_LON = 16
CAP = 16
LANES = 128
SLAB = 4 * CAP + 8
BLK = 256
TILE = 1024
ENC_TILES = (1024, 1024)
AHEAD = 3
ROUTE = 512
ENC = 1024
PUT = 1024
EPS = 1e-5
ENCODE_VMEM = 67043328 - (100 << 10)
BIN_VMEM = (64 << 20) - (16000 << 10)
SHIFT_VMEM = 16 << 20
LATE_VMEM = 8 << 20
FETCH_VMEM = (64 << 20) - (18500 << 10)
BF = jnp.bfloat16
F32 = jnp.float32
VMEM = pl.BlockSpec(memory_space=pltpu.VMEM)
HBM = pl.BlockSpec(memory_space=pltpu.HBM)
SMEM = pl.BlockSpec(memory_space=pltpu.SMEM)


def gelu(v):
    c = 0.7978845608028654
    inner = v * (c + (c * 0.044715) * (v * v))
    half = 0.5 * v
    return half + half * jnp.tanh(inner)


def dot(a, b):
    return jnp.dot(a, b, preferred_element_type=F32)


def dot_nt(a, b):
    return lax.dot_general(a, b, (((1,), (1,)), ((), ())), preferred_element_type=F32)


def normed(x, gain):
    mean = jnp.mean(x, -1, keepdims=True)
    centred = x - mean
    var = jnp.mean(centred * centred, -1, keepdims=True)
    return (centred * lax.rsqrt(var + EPS) * gain).astype(BF)


def iota(shape, axis):
    return lax.broadcasted_iota(jnp.int32, shape, axis)


def encode_kernel(
    place, count, dest_hbm, token_hbm, rows_hbm, w_in_hbm, w_out_hbm, slab_hbm,
    dest, token, rows, w_in, w_out, slab, encoded, total, slots, in_sems, out_sems, index_sems,
):
    copies = [pltpu.make_async_copy(rows_hbm, rows, in_sems.at[0])]
    spans = []
    for t, width in enumerate(ENC_TILES):
        f = slice(sum(ENC_TILES[:t]), sum(ENC_TILES[: t + 1]))
        spans.append(f)
        copies.append(pltpu.make_async_copy(w_in_hbm.at[:, f], w_in.at[:, f], in_sems.at[2 * t + 1]))
        copies.append(pltpu.make_async_copy(w_out_hbm.at[f, :], w_out.at[f, :], in_sems.at[2 * t + 2]))
    index_copies = [
        pltpu.make_async_copy(dest_hbm, dest, index_sems.at[0]),
        pltpu.make_async_copy(token_hbm, token, index_sems.at[1]),
    ]
    for copy in index_copies + copies[:AHEAD]:
        copy.start()

    def arrive(i):
        copies[i].wait()
        if i + AHEAD < len(copies):
            copies[i + AHEAD].start()

    live_count = count[0]
    lane_base = (place[0] % 8) * CAP
    before = iota((ROUTE, ROUTE), 0) < iota((ROUTE, ROUTE), 1)
    upper = jnp.where(before, 1.0, 0.0).astype(BF)
    owner_col = iota((OWNERS, ROUTE), 0)
    lane_col = iota((LANES, ROUTE), 0)
    for copy in index_copies:
        copy.wait()
    carry = jnp.zeros((OWNERS, 1), F32)
    high = jnp.zeros((OWNERS, LANES), F32)
    low = jnp.zeros((OWNERS, LANES), F32)
    for b in range(OBS_DEV // ROUTE):
        cols = slice(b * ROUTE, (b + 1) * ROUTE)
        owner = dest[:, cols]
        target = owner % N_LON * N_LAT + owner // N_LON
        live = (iota((1, ROUTE), 1) + b * ROUTE) < live_count
        hits = jnp.where((owner_col == target) & live, 1.0, 0.0)
        hits_bf = hits.astype(BF)
        earlier = dot(hits_bf, upper) + carry
        carry = carry + jnp.sum(hits, 1, keepdims=True)
        rank = jnp.sum(earlier * hits, 0, keepdims=True).astype(jnp.int32)
        slots[:, cols] = jnp.where(live, target * CAP + rank, -1)
        cell = token[:, cols]
        spread = lane_col == (rank + lane_base)
        row_part = jnp.where(spread, (cell // CLON).astype(F32), 0.0).astype(BF)
        col_part = jnp.where(spread, (cell % CLON + 1).astype(F32), 0.0).astype(BF)
        high = high + dot_nt(hits_bf, row_part)
        low = low + dot_nt(hits_bf, col_part)
    sub = iota((OWNERS, 8, LANES), 1)
    marks = jnp.where(sub == 0, high[:, None, :], jnp.where(sub == 1, low[:, None, :], 0.0))
    slab[:, 4 * CAP : SLAB, :] = marks.astype(BF)
    arrive(0)
    for t, f in enumerate(spans):
        arrive(2 * t + 1)
        arrive(2 * t + 2)

        def encode_block(b, _):
            r = pl.ds(pl.multiple_of(b * ENC, ENC), ENC)
            hidden = gelu(dot(rows[r, :], w_in[:, f])).astype(BF)
            part = dot(hidden, w_out[f, :])
            if t > 0:
                part = total[r, :] + part
            if t + 1 < len(spans):
                total[r, :] = part
            else:
                encoded[r, :] = part.astype(BF)
            return 0

        lax.fori_loop(0, OBS_DEV // ENC, encode_block, 0)
    step = PUT // CAP

    def slab_copy(b):
        d = pl.ds(b * step, step)
        return pltpu.make_async_copy(slab.at[d], slab_hbm.at[d], out_sems.at[b])

    def place_block(b, _):
        wanted = iota((PUT, OBS_DEV), 0) + b * PUT
        pick = jnp.where(slots[...] == wanted, 1.0, 0.0).astype(BF)
        moved = dot(pick, encoded[...]).astype(BF).reshape(step, CAP, D)
        d = pl.ds(b * step, step)
        for k in range(4):
            slab[d, k * CAP : (k + 1) * CAP, :] = moved[:, :, k * LANES : (k + 1) * LANES]
        slab_copy(b).start()
        return 0

    lax.fori_loop(0, OWNERS // step, place_block, 0)
    for b in range(OWNERS // step):
        slab_copy(b).wait()


def encode(place, count, dest, token, rows, w_in, w_out):
    return pl.pallas_call(
        encode_kernel,
        out_shape=jax.ShapeDtypeStruct((OWNERS, SLAB, LANES), BF),
        in_specs=[SMEM, SMEM, HBM, HBM, HBM, HBM, HBM],
        out_specs=HBM,
        scratch_shapes=[
            pltpu.VMEM((1, OBS_DEV), jnp.int32),
            pltpu.VMEM((1, OBS_DEV), jnp.int32),
            pltpu.VMEM((OBS_DEV, D), BF),
            pltpu.VMEM((D, FF), BF),
            pltpu.VMEM((FF, D), BF),
            pltpu.VMEM((OWNERS, SLAB, LANES), BF),
            pltpu.VMEM((OBS_DEV, D), BF),
            pltpu.VMEM((OBS_DEV, D), F32),
            pltpu.VMEM((1, OBS_DEV), jnp.int32),
            pltpu.SemaphoreType.DMA((2 * len(ENC_TILES) + 1,)),
            pltpu.SemaphoreType.DMA((OWNERS * CAP // PUT,)),
            pltpu.SemaphoreType.DMA((2,)),
        ],
        compiler_params=pltpu.CompilerParams(vmem_limit_bytes=ENCODE_VMEM),
        cost_estimate=pl.CostEstimate(
            flops=7 << 30, transcendentals=OBS_DEV * FF, bytes_accessed=8 << 20
        ),
        name="encode",
    )(place, count, dest, token, rows, w_in, w_out)


def weight_copies(layer, hbm, vmem, sems):
    w_qkv, w_proj, w_up, w_down = hbm
    v_qkv, v_proj, v_up, v_down = vmem
    pairs = []
    for part in range(3):
        c = slice(part * D, (part + 1) * D)
        pairs.append((w_qkv.at[layer, :, c], v_qkv.at[:, c]))
    pairs.append((w_proj.at[layer], v_proj))
    for t in range(FF // TILE):
        f = slice(t * TILE, (t + 1) * TILE)
        pairs.append((w_up.at[layer, :, f], v_up.at[:, f]))
        pairs.append((w_down.at[layer, f, :], v_down.at[f, :]))
    return [pltpu.make_async_copy(a, b, sems.at[i]) for i, (a, b) in enumerate(pairs)]


def fetch_kernel(after, wq, wp, wu, wd, vq, vp, vu, vd, sems):
    copies = []
    for i, (a, b) in enumerate(((wq, vq), (wp, vp), (wu, vu), (wd, vd))):
        copies.append(pltpu.make_async_copy(a.at[1], b, sems.at[i]))
        copies[-1].start()
    for copy in copies:
        copy.wait()


def fetch(after, *arrays):
    size = sum(a.size * a.dtype.itemsize for a in arrays)
    return pl.pallas_call(
        fetch_kernel,
        out_shape=[jax.ShapeDtypeStruct(a.shape[1:], a.dtype) for a in arrays],
        in_specs=[HBM] * 5,
        out_specs=[VMEM] * 4,
        scratch_shapes=[pltpu.SemaphoreType.DMA((4,))],
        compiler_params=pltpu.CompilerParams(vmem_limit_bytes=FETCH_VMEM),
        cost_estimate=pl.CostEstimate(flops=0, transcendentals=0, bytes_accessed=2 * size),
        name="fetch",
    )(after, *arrays)


def project(layer, x, gains, w_qkv, copies, qkv):
    h = normed(x, gains[layer, 0:1, :])
    for part in range(3):
        c = slice(part * D, (part + 1) * D)
        if copies:
            copies[part].wait()
        qkv[:, c] = dot(h, w_qkv[:, c]).astype(BF)


def attend(queries, keys, values, bias, mixed):
    count = queries.shape[0]
    first = iota((count, LANES), 1) < 64
    ones = jnp.ones((WIN * WIN, LANES), BF)
    for pair in range(HEADS // 2):
        c = slice(pair * LANES, (pair + 1) * LANES)
        q = queries[:, c] * BF(0.125)
        k = keys[:, c]
        v = jnp.concatenate([values[:, c], ones], 1)
        out = []
        for head in range(2):
            mine = first if head == 0 else jnp.logical_not(first)
            scores = dot_nt(jnp.where(mine, q, BF(0)), k)
            if bias is not None:
                scores = scores + bias
            probs = jnp.exp(scores - jnp.max(scores, -1, keepdims=True)).astype(BF)
            both = dot(probs, v)
            out.append(both[:, :LANES] / both[:, LANES:])
        mixed[:, c] = jnp.where(first, out[0], out[1]).astype(BF)


def finish(layer, x, mixed, gains, w_proj, w_up, w_down, copies):
    if copies:
        copies[3].wait()
    attended = x + dot(mixed, w_proj[...])
    h = normed(attended, gains[layer, 1:2, :])
    total = attended
    for t in range(FF // TILE):
        if copies:
            copies[2 * t + 4].wait()
            copies[2 * t + 5].wait()
        f = slice(t * TILE, (t + 1) * TILE)
        total = total + dot(gelu(dot(h, w_up[:, f])).astype(BF), w_down[f, :])
    return total.astype(BF)


def bin_kernel(
    arrived, background, gains, wq, wp, wu, wd,
    keep, above, right, corner,
    lined, pick, vq, vp, vu, vd, qkv, mixed, state, sems,
):
    copies = weight_copies(0, (wq, wp, wu, wd), (vq, vp, vu, vd), sems)
    for copy in copies:
        copy.start()
    for k in range(4):
        lined[:, k * LANES : (k + 1) * LANES] = arrived[:, k * CAP : (k + 1) * CAP, :].reshape(
            OWNERS * CAP, LANES
        )
    sub = iota((OWNERS, 8, LANES), 1)
    weight = jnp.where(sub == 0, float(CLON), 1.0)
    marks = arrived[:, 4 * CAP : SLAB, :].astype(F32) * weight
    marks = jnp.sum(marks.reshape(OWNERS // 8, 64, LANES), 1).astype(jnp.int32)
    row = iota((CELLS, LANES), 0)
    inner = row % BLK
    cell = (inner // WIN) * CLON + (row // BLK) * WIN + inner % WIN + 1
    tally = jnp.zeros((CELLS, LANES), F32)
    for g in range(OWNERS // 8):
        hit = jnp.where(cell == marks[g : g + 1, :], 1.0, 0.0)
        tally = tally + hit
        pick[:, g * LANES : (g + 1) * LANES] = hit.astype(BF)
    tally = jnp.sum(tally, 1, keepdims=True)
    sums = dot(pick[...], lined[...]) / jnp.maximum(tally, 1.0)
    for w in range(2):
        r = slice(w * BLK, (w + 1) * BLK)
        back = background[:, w * WIN : (w + 1) * WIN, :].astype(F32).reshape(BLK, D)
        state[r, :] = (back + sums[r, :]).astype(BF).astype(F32)
    project(0, state[...], gains, vq, copies, qkv)
    for w in range(2):
        r = pl.ds(w * BLK, BLK)
        parts = [qkv.at[r, pl.ds(part * D, D)] for part in range(3)]
        attend(*parts, None, mixed.at[r])
    done = finish(0, state[...], mixed[...], gains, vp, vu, vd, copies)
    one = done[:BLK].reshape(WIN, WIN, D)
    two = done[BLK:].reshape(WIN, WIN, D)
    corner[...] = one[HALF:, :HALF]
    right[...] = one[:HALF, :HALF]
    above[:, :HALF, :] = one[HALF:, HALF:]
    above[:, HALF:, :] = two[HALF:]
    keep[:, :HALF, :] = one[:HALF, HALF:]
    keep[:, HALF:, :] = two[:HALF]


WEIGHT_SCRATCH = [
    pltpu.VMEM((D, 3 * D), BF),
    pltpu.VMEM((D, D), BF),
    pltpu.VMEM((D, FF), BF),
    pltpu.VMEM((FF, D), BF),
]
WEIGHT_SEMS = pltpu.SemaphoreType.DMA((4 + 2 * FF // TILE,))
BLOCK_SCRATCH = [
    pltpu.VMEM((CELLS, 3 * D), BF),
    pltpu.VMEM((CELLS, D), BF),
    pltpu.VMEM((CELLS, D), F32),
]
BLOCK_COST = pl.CostEstimate(flops=4 << 30, transcendentals=2 << 20, bytes_accessed=8 << 20)
WIDE = jax.ShapeDtypeStruct((HALF, CLON - HALF, D), BF)
NARROW = jax.ShapeDtypeStruct((HALF, HALF, D), BF)
PIECES = (WIDE, WIDE, NARROW, NARROW)


def bin_block(arrived, background, gains, *weights):
    return pl.pallas_call(
        bin_kernel,
        out_shape=PIECES,
        in_specs=[VMEM] * 3 + [HBM] * 4,
        out_specs=[VMEM] * 4,
        scratch_shapes=[
            pltpu.VMEM((OWNERS * CAP, D), BF),
            pltpu.VMEM((CELLS, OWNERS * CAP), BF),
        ]
        + WEIGHT_SCRATCH
        + BLOCK_SCRATCH
        + [WEIGHT_SEMS],
        compiler_params=pltpu.CompilerParams(vmem_limit_bytes=BIN_VMEM),
        cost_estimate=BLOCK_COST,
        name="bin_block",
    )(arrived, background, gains, *weights)


def region_bias(first):
    area = WIN * WIN
    split = (iota((area, area), 0) < BLK // 2) != (iota((area, area), 1) < BLK // 2)
    return jnp.where(split & (first == 1), -1e30, 0.0)


def shift_kernel(
    first, mine, above, right, corner, gains, wq, wp, wu, wd,
    edge, back, left, diagonal, late_q, late_kv, late_x, qkv, mixed, state, bias,
):
    h = BLK // 2
    bias[...] = region_bias(first[0])
    top = above[...].astype(F32)
    bottom = mine[...].astype(F32)
    state[0:h, :] = top[:, :WIN, :].reshape(h, D)
    state[h : 2 * h, :] = bottom[:, :WIN, :].reshape(h, D)
    top = jnp.concatenate([top[:, WIN:, :], corner[...].astype(F32)], 1)
    bottom = jnp.concatenate([bottom[:, WIN:, :], right[...].astype(F32)], 1)
    state[2 * h : 3 * h, :] = top.reshape(h, D)
    state[3 * h : 4 * h, :] = bottom.reshape(h, D)
    project(1, state[...], gains, wq, (), qkv)
    parts = [qkv.at[pl.ds(0, BLK), pl.ds(part * D, D)] for part in range(3)]
    attend(parts[0].at[pl.ds(0, h)], parts[1], parts[2], bias[0:h, :], mixed.at[pl.ds(0, h)])
    parts = [qkv.at[pl.ds(BLK, BLK), pl.ds(part * D, D)] for part in range(3)]
    attend(*parts, bias[...], mixed.at[pl.ds(h, BLK)])
    late_q[...] = qkv[h:BLK, :D]
    late_kv[...] = qkv[0:BLK, D:]
    late_x[...] = state[h:BLK, :].astype(BF)
    x = jnp.concatenate([state[0:h, :], state[BLK:, :]], 0)
    done = finish(1, x, mixed[...], gains, wp, wu, wd, ())
    one = done[:h].reshape(HALF, WIN, D)
    two = done[h:].reshape(WIN, WIN, D)
    diagonal[...] = two[:HALF, HALF:]
    left[...] = two[HALF:, HALF:]
    back[:, :WIN, :] = one
    back[:, WIN:, :] = two[:HALF, :HALF]
    edge[...] = two[HALF:, :HALF]


def shift_block(first, pieces, gains, *weights):
    h = BLK // 2
    return pl.pallas_call(
        shift_kernel,
        out_shape=(
            NARROW,
            WIDE,
            NARROW,
            NARROW,
            jax.ShapeDtypeStruct((h, D), BF),
            jax.ShapeDtypeStruct((BLK, 2 * D), BF),
            jax.ShapeDtypeStruct((h, D), BF),
        ),
        in_specs=[SMEM] + [VMEM] * 9,
        out_specs=[VMEM] * 7,
        scratch_shapes=[
            pltpu.VMEM((CELLS, 3 * D), BF),
            pltpu.VMEM((CELLS - h, D), BF),
            pltpu.VMEM((CELLS, D), F32),
            pltpu.VMEM((BLK, BLK), F32),
        ],
        compiler_params=pltpu.CompilerParams(vmem_limit_bytes=SHIFT_VMEM),
        cost_estimate=BLOCK_COST,
        name="shift_block",
    )(first, *pieces, gains, *weights)


def late_kernel(first, q, kv, x, gains, wp, wu, wd, out, mixed):
    h = BLK // 2
    bias = region_bias(first[0])[h:, :]
    attend(q, kv.at[:, pl.ds(0, D)], kv.at[:, pl.ds(D, D)], bias, mixed)
    done = finish(1, x[...].astype(F32), mixed[...], gains, wp, wu, wd, ())
    out[...] = done.reshape(HALF, WIN, D)


def late_block(first, q, kv, x, gains, *weights):
    return pl.pallas_call(
        late_kernel,
        out_shape=jax.ShapeDtypeStruct((HALF, WIN, D), BF),
        in_specs=[SMEM] + [VMEM] * 7,
        out_specs=VMEM,
        scratch_shapes=[pltpu.VMEM((BLK // 2, D), BF)],
        compiler_params=pltpu.CompilerParams(vmem_limit_bytes=LATE_VMEM),
        cost_estimate=pl.CostEstimate(
            flops=1 << 30, transcendentals=1 << 19, bytes_accessed=6 << 20
        ),
        name="late_block",
    )(first, q, kv, x, gains, *weights)


def place_kernel(left, mid, edge, corner, below, out, sems):
    low = CLON - HALF
    spots = (
        (left, slice(0, HALF), slice(0, HALF)),
        (mid, slice(0, HALF), slice(HALF, low)),
        (edge, slice(0, HALF), slice(low, CLON)),
        (corner, slice(HALF, CLAT), slice(0, HALF)),
        (below, slice(HALF, CLAT), slice(HALF, CLON)),
    )
    copies = []
    for i, (piece, rows, cols) in enumerate(spots):
        copies.append(pltpu.make_async_copy(piece, out.at[rows, cols, :], sems.at[i]))
        copies[-1].start()
    for copy in copies:
        copy.wait()


def assemble(*pieces):
    return pl.pallas_call(
        place_kernel,
        out_shape=jax.ShapeDtypeStruct((CLAT, CLON, D), BF),
        in_specs=[VMEM] * 5,
        out_specs=HBM,
        scratch_shapes=[pltpu.SemaphoreType.DMA((5,))],
        compiler_params=pltpu.CompilerParams(vmem_limit_bytes=LATE_VMEM),
        cost_estimate=pl.CostEstimate(flops=0, transcendentals=0, bytes_accessed=1 << 20),
        name="assemble",
    )(*pieces)


def moved(block, lat_step, lon_step):
    lat_count = lax.axis_size("lat")
    lon_count = lax.axis_size("lon")
    route = [
        (
            i * lon_count + j,
            (i + lat_step) % lat_count * lon_count + (j + lon_step) % lon_count,
        )
        for i in range(lat_count)
        for j in range(lon_count)
    ]
    return lax.ppermute(block, ("lat", "lon"), route)


def on_device(
    obs_rows,
    obs_dest,
    obs_token,
    obs_count,
    background,
    w_obs_in,
    w_obs_out,
    w_qkv,
    w_proj,
    w_up,
    w_down,
    norm_gain,
):
    lat = lax.axis_index("lat")
    place = (lax.axis_index("lon") * N_LAT + lat).astype(jnp.int32).reshape(1)
    slab = encode(
        place,
        obs_count,
        obs_dest.reshape(1, OBS_DEV),
        obs_token.reshape(1, OBS_DEV),
        obs_rows,
        w_obs_in,
        w_obs_out,
    )
    arrived = lax.all_to_all(slab, ("lon", "lat"), split_axis=0, concat_axis=0, tiled=True)
    weights = (w_qkv, w_proj, w_up, w_down)
    mine, above, right, corner = bin_block(arrived, background, norm_gain, *weights)
    late = fetch(mine, *weights)
    above = moved(above, 1, 0)
    right = moved(right, 0, -1)
    corner = moved(corner, 1, -1)
    first = (lat == 0).astype(jnp.int32).reshape(1)
    edge, back, left, corner, q, kv, x = shift_block(
        first, (mine, above, right, corner), norm_gain, *late
    )
    below = moved(back, -1, 0)
    mid = late_block(first, q, kv, x, norm_gain, *late[1:])
    left, corner, mid = lax.optimization_barrier((left, corner, mid))
    left = moved(left, 0, 1)
    corner = moved(corner, -1, 1)
    return assemble(left, mid, edge, corner, below)


def solution(mesh):
    both = P(("lat", "lon"))
    rows = P(("lat", "lon"), None)
    grid = P("lat", "lon", None)
    return jax.shard_map(
        on_device,
        mesh=mesh,
        in_specs=(rows, rows, both, both, grid) + (P(),) * 7,
        out_specs=grid,
        check_vma=False,
    )
```

```python
import jax
import jax.numpy as jnp
from jax import lax
from jax.experimental import pallas as pl
from jax.experimental.pallas import tpu as pltpu
from jax.sharding import PartitionSpec as P

D = 512
FF = 2048
HEADS = 8
WIN = 16
HALF = 8
CLAT = 16
CLON = 32
CELLS = CLAT * CLON
OBS_DEV = 1024
OWNERS = 128
N_LAT = 8
N_LON = 16
CAP = 16
LANES = 128
SLAB = 4 * CAP + 8
BLK = 256
TILE = 2048
ENC_TILES = (1024, 1024)
AHEAD = 3
ROUTE = 512
ENC = 1024
PUT = 1024
EPS = 1e-5
ENCODE_VMEM = 67043328 - (100 << 10)
BIN_VMEM = (64 << 20) - (16000 << 10)
SHIFT_VMEM = 16 << 20
LATE_VMEM = 8 << 20
FETCH_VMEM = (64 << 20) - (18500 << 10)
BF = jnp.bfloat16
F32 = jnp.float32
VMEM = pl.BlockSpec(memory_space=pltpu.VMEM)
HBM = pl.BlockSpec(memory_space=pltpu.HBM)
SMEM = pl.BlockSpec(memory_space=pltpu.SMEM)


def gelu(v):
    c = 0.7978845608028654
    inner = v * (c + (c * 0.044715) * (v * v))
    half = 0.5 * v
    return half + half * jnp.tanh(inner)


def dot(a, b):
    return jnp.dot(a, b, preferred_element_type=F32)


def dot_nt(a, b):
    return lax.dot_general(a, b, (((1,), (1,)), ((), ())), preferred_element_type=F32)


def normed(x, gain):
    mean = jnp.mean(x, -1, keepdims=True)
    centred = x - mean
    var = jnp.mean(centred * centred, -1, keepdims=True)
    return (centred * lax.rsqrt(var + EPS) * gain).astype(BF)


def iota(shape, axis):
    return lax.broadcasted_iota(jnp.int32, shape, axis)


def encode_kernel(
    place, count, dest_hbm, token_hbm, rows_hbm, w_in_hbm, w_out_hbm, slab_hbm,
    dest, token, rows, w_in, w_out, slab, encoded, total, slots, in_sems, out_sems, index_sems,
):
    copies = [pltpu.make_async_copy(rows_hbm, rows, in_sems.at[0])]
    spans = []
    for t, width in enumerate(ENC_TILES):
        f = slice(sum(ENC_TILES[:t]), sum(ENC_TILES[: t + 1]))
        spans.append(f)
        copies.append(pltpu.make_async_copy(w_in_hbm.at[:, f], w_in.at[:, f], in_sems.at[2 * t + 1]))
        copies.append(pltpu.make_async_copy(w_out_hbm.at[f, :], w_out.at[f, :], in_sems.at[2 * t + 2]))
    index_copies = [
        pltpu.make_async_copy(dest_hbm, dest, index_sems.at[0]),
        pltpu.make_async_copy(token_hbm, token, index_sems.at[1]),
    ]
    for copy in index_copies + copies[:AHEAD]:
        copy.start()

    def arrive(i):
        copies[i].wait()
        if i + AHEAD < len(copies):
            copies[i + AHEAD].start()

    live_count = count[0]
    lane_base = (place[0] % 8) * CAP
    before = iota((ROUTE, ROUTE), 0) < iota((ROUTE, ROUTE), 1)
    upper = jnp.where(before, 1.0, 0.0).astype(BF)
    owner_col = iota((OWNERS, ROUTE), 0)
    lane_col = iota((LANES, ROUTE), 0)
    for copy in index_copies:
        copy.wait()
    carry = jnp.zeros((OWNERS, 1), F32)
    high = jnp.zeros((OWNERS, LANES), F32)
    low = jnp.zeros((OWNERS, LANES), F32)
    for b in range(OBS_DEV // ROUTE):
        cols = slice(b * ROUTE, (b + 1) * ROUTE)
        owner = dest[:, cols]
        target = owner % N_LON * N_LAT + owner // N_LON
        live = (iota((1, ROUTE), 1) + b * ROUTE) < live_count
        hits = jnp.where((owner_col == target) & live, 1.0, 0.0)
        hits_bf = hits.astype(BF)
        earlier = dot(hits_bf, upper) + carry
        carry = carry + jnp.sum(hits, 1, keepdims=True)
        rank = jnp.sum(earlier * hits, 0, keepdims=True).astype(jnp.int32)
        slots[:, cols] = jnp.where(live, target * CAP + rank, -1)
        cell = token[:, cols]
        spread = lane_col == (rank + lane_base)
        row_part = jnp.where(spread, (cell // CLON).astype(F32), 0.0).astype(BF)
        col_part = jnp.where(spread, (cell % CLON + 1).astype(F32), 0.0).astype(BF)
        high = high + dot_nt(hits_bf, row_part)
        low = low + dot_nt(hits_bf, col_part)
    sub = iota((OWNERS, 8, LANES), 1)
    marks = jnp.where(sub == 0, high[:, None, :], jnp.where(sub == 1, low[:, None, :], 0.0))
    slab[:, 4 * CAP : SLAB, :] = marks.astype(BF)
    arrive(0)
    for t, f in enumerate(spans):
        arrive(2 * t + 1)
        arrive(2 * t + 2)

        def encode_block(b, _):
            r = pl.ds(pl.multiple_of(b * ENC, ENC), ENC)
            hidden = gelu(dot(rows[r, :], w_in[:, f])).astype(BF)
            part = dot(hidden, w_out[f, :])
            if t > 0:
                part = total[r, :] + part
            if t + 1 < len(spans):
                total[r, :] = part
            else:
                encoded[r, :] = part.astype(BF)
            return 0

        lax.fori_loop(0, OBS_DEV // ENC, encode_block, 0)
    step = PUT // CAP

    def slab_copy(b):
        d = pl.ds(b * step, step)
        return pltpu.make_async_copy(slab.at[d], slab_hbm.at[d], out_sems.at[b])

    def place_block(b, _):
        wanted = iota((PUT, OBS_DEV), 0) + b * PUT
        pick = jnp.where(slots[...] == wanted, 1.0, 0.0).astype(BF)
        moved = dot(pick, encoded[...]).astype(BF).reshape(step, CAP, D)
        d = pl.ds(b * step, step)
        for k in range(4):
            slab[d, k * CAP : (k + 1) * CAP, :] = moved[:, :, k * LANES : (k + 1) * LANES]
        slab_copy(b).start()
        return 0

    lax.fori_loop(0, OWNERS // step, place_block, 0)
    for b in range(OWNERS // step):
        slab_copy(b).wait()


def encode(place, count, dest, token, rows, w_in, w_out):
    return pl.pallas_call(
        encode_kernel,
        out_shape=jax.ShapeDtypeStruct((OWNERS, SLAB, LANES), BF),
        in_specs=[SMEM, SMEM, HBM, HBM, HBM, HBM, HBM],
        out_specs=HBM,
        scratch_shapes=[
            pltpu.VMEM((1, OBS_DEV), jnp.int32),
            pltpu.VMEM((1, OBS_DEV), jnp.int32),
            pltpu.VMEM((OBS_DEV, D), BF),
            pltpu.VMEM((D, FF), BF),
            pltpu.VMEM((FF, D), BF),
            pltpu.VMEM((OWNERS, SLAB, LANES), BF),
            pltpu.VMEM((OBS_DEV, D), BF),
            pltpu.VMEM((OBS_DEV, D), F32),
            pltpu.VMEM((1, OBS_DEV), jnp.int32),
            pltpu.SemaphoreType.DMA((2 * len(ENC_TILES) + 1,)),
            pltpu.SemaphoreType.DMA((OWNERS * CAP // PUT,)),
            pltpu.SemaphoreType.DMA((2,)),
        ],
        compiler_params=pltpu.CompilerParams(vmem_limit_bytes=ENCODE_VMEM),
        cost_estimate=pl.CostEstimate(
            flops=7 << 30, transcendentals=OBS_DEV * FF, bytes_accessed=8 << 20
        ),
        name="encode",
    )(place, count, dest, token, rows, w_in, w_out)


def weight_copies(layer, hbm, vmem, sems):
    w_qkv, w_proj, w_up, w_down = hbm
    v_qkv, v_proj, v_up, v_down = vmem
    pairs = []
    for part in range(3):
        c = slice(part * D, (part + 1) * D)
        pairs.append((w_qkv.at[layer, :, c], v_qkv.at[:, c]))
    pairs.append((w_proj.at[layer], v_proj))
    for t in range(FF // TILE):
        f = slice(t * TILE, (t + 1) * TILE)
        pairs.append((w_up.at[layer, :, f], v_up.at[:, f]))
        pairs.append((w_down.at[layer, f, :], v_down.at[f, :]))
    return [pltpu.make_async_copy(a, b, sems.at[i]) for i, (a, b) in enumerate(pairs)]


def fetch_kernel(after, wq, wp, wu, wd, vq, vp, vu, vd, sems):
    copies = []
    for i, (a, b) in enumerate(((wq, vq), (wp, vp), (wu, vu), (wd, vd))):
        copies.append(pltpu.make_async_copy(a.at[1], b, sems.at[i]))
        copies[-1].start()
    for copy in copies:
        copy.wait()


def fetch(after, *arrays):
    size = sum(a.size * a.dtype.itemsize for a in arrays)
    return pl.pallas_call(
        fetch_kernel,
        out_shape=[jax.ShapeDtypeStruct(a.shape[1:], a.dtype) for a in arrays],
        in_specs=[HBM] * 5,
        out_specs=[VMEM] * 4,
        scratch_shapes=[pltpu.SemaphoreType.DMA((4,))],
        compiler_params=pltpu.CompilerParams(vmem_limit_bytes=FETCH_VMEM),
        cost_estimate=pl.CostEstimate(flops=0, transcendentals=0, bytes_accessed=2 * size),
        name="fetch",
    )(after, *arrays)


def project(layer, x, gains, w_qkv, copies, qkv):
    h = normed(x, gains[layer, 0:1, :])
    for part in range(3):
        c = slice(part * D, (part + 1) * D)
        if copies:
            copies[part].wait()
        qkv[:, c] = dot(h, w_qkv[:, c]).astype(BF)


def attend(queries, keys, values, bias, mixed):
    count = queries.shape[0]
    first = iota((count, LANES), 1) < 64
    ones = jnp.ones((WIN * WIN, LANES), BF)
    for pair in range(HEADS // 2):
        c = slice(pair * LANES, (pair + 1) * LANES)
        q = queries[:, c] * BF(0.125)
        k = keys[:, c]
        v = jnp.concatenate([values[:, c], ones], 1)
        out = []
        for head in range(2):
            mine = first if head == 0 else jnp.logical_not(first)
            scores = dot_nt(jnp.where(mine, q, BF(0)), k)
            if bias is not None:
                scores = scores + bias
            probs = jnp.exp(scores - jnp.max(scores, -1, keepdims=True)).astype(BF)
            both = dot(probs, v)
            out.append(both[:, :LANES] / both[:, LANES:])
        mixed[:, c] = jnp.where(first, out[0], out[1]).astype(BF)


def finish(layer, x, mixed, gains, w_proj, w_up, w_down, copies):
    if copies:
        copies[3].wait()
    attended = x + dot(mixed, w_proj[...])
    h = normed(attended, gains[layer, 1:2, :])
    total = attended
    for t in range(FF // TILE):
        if copies:
            copies[2 * t + 4].wait()
            copies[2 * t + 5].wait()
        f = slice(t * TILE, (t + 1) * TILE)
        total = total + dot(gelu(dot(h, w_up[:, f])).astype(BF), w_down[f, :])
    return total.astype(BF)


def bin_kernel(
    arrived, background, gains, wq, wp, wu, wd,
    keep, above, right, corner,
    lined, pick, vq, vp, vu, vd, qkv, mixed, state, sems,
):
    copies = weight_copies(0, (wq, wp, wu, wd), (vq, vp, vu, vd), sems)
    for copy in copies:
        copy.start()
    for k in range(4):
        lined[:, k * LANES : (k + 1) * LANES] = arrived[:, k * CAP : (k + 1) * CAP, :].reshape(
            OWNERS * CAP, LANES
        )
    sub = iota((OWNERS, 8, LANES), 1)
    weight = jnp.where(sub == 0, float(CLON), 1.0)
    marks = arrived[:, 4 * CAP : SLAB, :].astype(F32) * weight
    marks = jnp.sum(marks.reshape(OWNERS // 8, 64, LANES), 1).astype(jnp.int32)
    row = iota((CELLS, LANES), 0)
    inner = row % BLK
    cell = (inner // WIN) * CLON + (row // BLK) * WIN + inner % WIN + 1
    tally = jnp.zeros((CELLS, LANES), F32)
    for g in range(OWNERS // 8):
        hit = jnp.where(cell == marks[g : g + 1, :], 1.0, 0.0)
        tally = tally + hit
        pick[:, g * LANES : (g + 1) * LANES] = hit.astype(BF)
    tally = jnp.sum(tally, 1, keepdims=True)
    sums = dot(pick[...], lined[...]) / jnp.maximum(tally, 1.0)
    for w in range(2):
        r = slice(w * BLK, (w + 1) * BLK)
        back = background[:, w * WIN : (w + 1) * WIN, :].astype(F32).reshape(BLK, D)
        state[r, :] = (back + sums[r, :]).astype(BF).astype(F32)
    project(0, state[...], gains, vq, copies, qkv)
    for w in range(2):
        r = pl.ds(w * BLK, BLK)
        parts = [qkv.at[r, pl.ds(part * D, D)] for part in range(3)]
        attend(*parts, None, mixed.at[r])
    done = finish(0, state[...], mixed[...], gains, vp, vu, vd, copies)
    one = done[:BLK].reshape(WIN, WIN, D)
    two = done[BLK:].reshape(WIN, WIN, D)
    corner[...] = one[HALF:, :HALF]
    right[...] = one[:HALF, :HALF]
    above[:, :HALF, :] = one[HALF:, HALF:]
    above[:, HALF:, :] = two[HALF:]
    keep[:, :HALF, :] = one[:HALF, HALF:]
    keep[:, HALF:, :] = two[:HALF]


WEIGHT_SCRATCH = [
    pltpu.VMEM((D, 3 * D), BF),
    pltpu.VMEM((D, D), BF),
    pltpu.VMEM((D, FF), BF),
    pltpu.VMEM((FF, D), BF),
]
WEIGHT_SEMS = pltpu.SemaphoreType.DMA((4 + 2 * FF // TILE,))
BLOCK_SCRATCH = [
    pltpu.VMEM((CELLS, 3 * D), BF),
    pltpu.VMEM((CELLS, D), BF),
    pltpu.VMEM((CELLS, D), F32),
]
BLOCK_COST = pl.CostEstimate(flops=4 << 30, transcendentals=2 << 20, bytes_accessed=8 << 20)
WIDE = jax.ShapeDtypeStruct((HALF, CLON - HALF, D), BF)
NARROW = jax.ShapeDtypeStruct((HALF, HALF, D), BF)
PIECES = (WIDE, WIDE, NARROW, NARROW)


def bin_block(arrived, background, gains, *weights):
    return pl.pallas_call(
        bin_kernel,
        out_shape=PIECES,
        in_specs=[VMEM] * 3 + [HBM] * 4,
        out_specs=[VMEM] * 4,
        scratch_shapes=[
            pltpu.VMEM((OWNERS * CAP, D), BF),
            pltpu.VMEM((CELLS, OWNERS * CAP), BF),
        ]
        + WEIGHT_SCRATCH
        + BLOCK_SCRATCH
        + [WEIGHT_SEMS],
        compiler_params=pltpu.CompilerParams(vmem_limit_bytes=BIN_VMEM),
        cost_estimate=BLOCK_COST,
        name="bin_block",
    )(arrived, background, gains, *weights)


def region_bias(first):
    area = WIN * WIN
    split = (iota((area, area), 0) < BLK // 2) != (iota((area, area), 1) < BLK // 2)
    return jnp.where(split & (first == 1), -1e30, 0.0)


def shift_kernel(
    first, mine, above, right, corner, gains, wq, wp, wu, wd,
    edge, back, left, diagonal, late_q, late_kv, late_x, qkv, mixed, state, bias,
):
    h = BLK // 2
    bias[...] = region_bias(first[0])
    top = above[...].astype(F32)
    bottom = mine[...].astype(F32)
    state[0:h, :] = top[:, :WIN, :].reshape(h, D)
    state[h : 2 * h, :] = bottom[:, :WIN, :].reshape(h, D)
    top = jnp.concatenate([top[:, WIN:, :], corner[...].astype(F32)], 1)
    bottom = jnp.concatenate([bottom[:, WIN:, :], right[...].astype(F32)], 1)
    state[2 * h : 3 * h, :] = top.reshape(h, D)
    state[3 * h : 4 * h, :] = bottom.reshape(h, D)
    project(1, state[...], gains, wq, (), qkv)
    parts = [qkv.at[pl.ds(0, BLK), pl.ds(part * D, D)] for part in range(3)]
    attend(parts[0].at[pl.ds(0, h)], parts[1], parts[2], bias[0:h, :], mixed.at[pl.ds(0, h)])
    parts = [qkv.at[pl.ds(BLK, BLK), pl.ds(part * D, D)] for part in range(3)]
    attend(*parts, bias[...], mixed.at[pl.ds(h, BLK)])
    late_q[...] = qkv[h:BLK, :D]
    late_kv[...] = qkv[0:BLK, D:]
    late_x[...] = state[h:BLK, :].astype(BF)
    x = jnp.concatenate([state[0:h, :], state[BLK:, :]], 0)
    done = finish(1, x, mixed[...], gains, wp, wu, wd, ())
    one = done[:h].reshape(HALF, WIN, D)
    two = done[h:].reshape(WIN, WIN, D)
    diagonal[...] = two[:HALF, HALF:]
    left[...] = two[HALF:, HALF:]
    back[:, :WIN, :] = one
    back[:, WIN:, :] = two[:HALF, :HALF]
    edge[...] = two[HALF:, :HALF]


def shift_block(first, pieces, gains, *weights):
    h = BLK // 2
    return pl.pallas_call(
        shift_kernel,
        out_shape=(
            NARROW,
            WIDE,
            NARROW,
            NARROW,
            jax.ShapeDtypeStruct((h, D), BF),
            jax.ShapeDtypeStruct((BLK, 2 * D), BF),
            jax.ShapeDtypeStruct((h, D), BF),
        ),
        in_specs=[SMEM] + [VMEM] * 9,
        out_specs=[VMEM] * 7,
        scratch_shapes=[
            pltpu.VMEM((CELLS, 3 * D), BF),
            pltpu.VMEM((CELLS - h, D), BF),
            pltpu.VMEM((CELLS, D), F32),
            pltpu.VMEM((BLK, BLK), F32),
        ],
        compiler_params=pltpu.CompilerParams(vmem_limit_bytes=SHIFT_VMEM),
        cost_estimate=BLOCK_COST,
        name="shift_block",
    )(first, *pieces, gains, *weights)


def late_kernel(first, q, kv, x, gains, wp, wu, wd, out, mixed):
    h = BLK // 2
    bias = region_bias(first[0])[h:, :]
    attend(q, kv.at[:, pl.ds(0, D)], kv.at[:, pl.ds(D, D)], bias, mixed)
    done = finish(1, x[...].astype(F32), mixed[...], gains, wp, wu, wd, ())
    out[...] = done.reshape(HALF, WIN, D)


def late_block(first, q, kv, x, gains, *weights):
    return pl.pallas_call(
        late_kernel,
        out_shape=jax.ShapeDtypeStruct((HALF, WIN, D), BF),
        in_specs=[SMEM] + [VMEM] * 7,
        out_specs=VMEM,
        scratch_shapes=[pltpu.VMEM((BLK // 2, D), BF)],
        compiler_params=pltpu.CompilerParams(vmem_limit_bytes=LATE_VMEM),
        cost_estimate=pl.CostEstimate(
            flops=1 << 30, transcendentals=1 << 19, bytes_accessed=6 << 20
        ),
        name="late_block",
    )(first, q, kv, x, gains, *weights)


def place_kernel(left, mid, edge, corner, below, out, sems):
    low = CLON - HALF
    spots = (
        (left, slice(0, HALF), slice(0, HALF)),
        (mid, slice(0, HALF), slice(HALF, low)),
        (edge, slice(0, HALF), slice(low, CLON)),
        (corner, slice(HALF, CLAT), slice(0, HALF)),
        (below, slice(HALF, CLAT), slice(HALF, CLON)),
    )
    copies = []
    for i, (piece, rows, cols) in enumerate(spots):
        copies.append(pltpu.make_async_copy(piece, out.at[rows, cols, :], sems.at[i]))
        copies[-1].start()
    for copy in copies:
        copy.wait()


def assemble(*pieces):
    return pl.pallas_call(
        place_kernel,
        out_shape=jax.ShapeDtypeStruct((CLAT, CLON, D), BF),
        in_specs=[VMEM] * 5,
        out_specs=HBM,
        scratch_shapes=[pltpu.SemaphoreType.DMA((5,))],
        compiler_params=pltpu.CompilerParams(vmem_limit_bytes=LATE_VMEM),
        cost_estimate=pl.CostEstimate(flops=0, transcendentals=0, bytes_accessed=1 << 20),
        name="assemble",
    )(*pieces)


def moved(block, lat_step, lon_step):
    lat_count = lax.axis_size("lat")
    lon_count = lax.axis_size("lon")
    route = [
        (
            i * lon_count + j,
            (i + lat_step) % lat_count * lon_count + (j + lon_step) % lon_count,
        )
        for i in range(lat_count)
        for j in range(lon_count)
    ]
    return lax.ppermute(block, ("lat", "lon"), route)


def on_device(
    obs_rows,
    obs_dest,
    obs_token,
    obs_count,
    background,
    w_obs_in,
    w_obs_out,
    w_qkv,
    w_proj,
    w_up,
    w_down,
    norm_gain,
):
    lat = lax.axis_index("lat")
    place = (lax.axis_index("lon") * N_LAT + lat).astype(jnp.int32).reshape(1)
    slab = encode(
        place,
        obs_count,
        obs_dest.reshape(1, OBS_DEV),
        obs_token.reshape(1, OBS_DEV),
        obs_rows,
        w_obs_in,
        w_obs_out,
    )
    arrived = lax.all_to_all(slab, ("lon", "lat"), split_axis=0, concat_axis=0, tiled=True)
    weights = (w_qkv, w_proj, w_up, w_down)
    mine, above, right, corner = bin_block(arrived, background, norm_gain, *weights)
    late = fetch(mine, *weights)
    above = moved(above, 1, 0)
    right = moved(right, 0, -1)
    corner = moved(corner, 1, -1)
    first = (lat == 0).astype(jnp.int32).reshape(1)
    edge, back, left, corner, q, kv, x = shift_block(
        first, (mine, above, right, corner), norm_gain, *late
    )
    below = moved(back, -1, 0)
    mid = late_block(first, q, kv, x, norm_gain, *late[1:])
    left, corner, mid = lax.optimization_barrier((left, corner, mid))
    left = moved(left, 0, 1)
    corner = moved(corner, -1, 1)
    return assemble(left, mid, edge, corner, below)


def solution(mesh):
    both = P(("lat", "lon"))
    rows = P(("lat", "lon"), None)
    grid = P("lat", "lon", None)
    return jax.shard_map(
        on_device,
        mesh=mesh,
        in_specs=(rows, rows, both, both, grid) + (P(),) * 7,
        out_specs=grid,
        check_vma=False,
    )
```
